128 devices in a mesh: view: 8 (over x, core), vox: 16 (over z, y).
Axes of the slice: x: 4, y: 4, z: 4, core: 2. Of those that a mesh axis runs over, the one named last changes fastest.
Arguments:
- features: bfloat16 [131072, 1024], P(('view', 'vox')), may hold values from -6 to 6
- w_embed: bfloat16 [1024, 768], replicated, may hold values from -0.1875 to 0.1875
- owner_device: int32 [131072, 1], P(('view', 'vox')), may hold values from 0 to 127; in each aligned block of 1024 rows (0 to 1023, 1024 to 2047, ...) at most 16 rows name the same one
- voxel_slot: int32 [131072], P(('view', 'vox')), may hold values from 0 to 511
- window_ids: int32 [65536], P(('view', 'vox')), may hold values from 0 to 1023, never falling along the last dimension, each value on 1 to 512 neighbouring positions
- w_heads: bfloat16 [768, 2304], replicated
- w_out: bfloat16 [768, 768], replicated, may hold values from -0.21875 to 0.21875
- w_up: bfloat16 [768, 3072], replicated, may hold values from -0.21875 to 0.21875
- w_down: bfloat16 [3072, 768], replicated, may hold values from -0.109375 to 0.109375
Outputs:
- encoded: bfloat16 [65536, 768], P(('view', 'vox'))
The draws below stay inside these ranges and needn't reach their ends.
Inputs may be any that keep to these rules, and one draw needn't show every extreme that they name: `owner_device`: among the patches of one device, at most 16 name the same owner. `window_ids`: never falls along the voxels; a window is a run of 1 to 512 consecutive voxels.
All inputs are finite; a program needn't handle non-finite values.
Results may differ from the reference program's by a relative error of at most 0.013.
The reference program's roundings to bfloat16 on the way (of `projected`, `normed`, `triple`, `weights`, `attended` and `expanded`) count: a program that leaves them out, or rounds other values in their place, can miss the bound.
Values may be sent and summed in bfloat16 or wider, within the bound.
No kernel may reach another device: no remote copies, remote signals or barrier semaphores. Data moves between devices by JAX's collectives and lax.ppermute only.
A program may use at most 128 MiB of HBM per device.

```python
import math
import jax
import jax.numpy as jnp
import numpy as np
from jax import lax

D = 1024
C = 768
HEADS = 12
FFH = 3072
P_DEV = 1024
V_DEV = 512
WMOST = 512
CAP = 16
PATCHES = 131072
VOXELS = 65536
WINDOWS = 1024
DEVICES = 128


def draw_w_heads(key, part):
    base = jax.random.truncated_normal(key, -4.0, 4.0, (C, 3 * C), jnp.float32) * C ** (-0.5)
    return base.astype(jnp.bfloat16)


def plant(result, own_key, low, high):
    index_at = [jax.random.randint(jax.random.fold_in(own_key, axis), (), 0, length) for axis, length in enumerate(result.shape)]
    widest = result.shape.index(max(result.shape))
    beside = index_at[:widest] + [(index_at[widest] + 1) % result.shape[widest]] + index_at[widest + 1:]
    return result.at[tuple(index_at)].set(low).at[tuple(beside)].set(high)


def shard_levels(key, extent, pieces, smallest, largest):
    gain = 1.0
    for dim, blocks in pieces:
        draws = jax.random.uniform(jax.random.fold_in(jax.random.fold_in(key, 6), dim), (blocks,), jnp.float32, smallest / len(pieces), largest / len(pieces))
        gain = gain * jnp.repeat(jnp.exp(draws), extent[dim] // blocks).reshape((-1,) + (1,) * (len(extent) - 1 - dim))
    return gain


def profile(count, total, reach, skew):
    weights = [(1 << 20) // math.isqrt(standing ** skew) + 1 for standing in range(2, count + 1)]
    spare, given = total - reach - (count - 1), [1] * (count - 1)
    while spare > 0:
        free = [i for i in range(count - 1) if given[i] < reach]
        whole, remaining = sum([weights[i] for i in free]), spare
        for i in free:
            extra = min(reach - given[i], max(1, remaining * weights[i] // whole), spare)
            given[i] = given[i] + extra
            spare = spare - extra
    return np.array([reach] + given)


def ragged_sizes(key, amount, total, reach, lean):
    if amount == 2:
        one = jax.random.randint(key, (), max(1, total - reach), min(reach, total - 1) + 1)
        return jnp.stack([one, total - one])
    tallies = jnp.asarray(profile(amount, total, reach, lean), jnp.int32)
    twos = (amount - 1) // 2
    source_of, receiver = tallies[1:1 + 2 * twos:2], tallies[2:2 + 2 * twos:2]
    slack = jnp.minimum(source_of - 1, reach - receiver)
    moved = jax.random.randint(jax.random.fold_in(key, 1), (twos,), 0, 1 << 20) % (slack + 1)
    tallies = tallies.at[1:1 + 2 * twos:2].set(source_of - moved).at[2:2 + 2 * twos:2].set(receiver + moved)
    return tallies[jax.random.permutation(jax.random.fold_in(key, 2), amount)]


def deal_out(rng, own, number, rows, count, top, reach, slope):
    order = jax.random.permutation(rng, count)
    heavy_load, common = shares(count, rows * top, reach, slope, True), shares(count, rows * top, reach, slope, False)
    places = jnp.arange(count)

    def named(sizes, rotation):
        used = int((sizes > 0).sum())
        fixed = max(1, used // 4)
        shifted = fixed + (places - fixed + rotation * (used - fixed)) % max(1, count - fixed)
        return jnp.zeros((count,), jnp.int32).at[order[jnp.where(places < fixed, places, shifted)]].set(jnp.asarray(sizes, jnp.int32))

    sizes = jnp.where(number % 4 == 0, named(heavy_load, number // 4), named(common, number - number // 4 - 1))
    mixed = jax.random.permutation(jax.random.fold_in(own, 3), count)
    donor, receiver = mixed[0:count // 2 * 2:2], mixed[1:count // 2 * 2:2]
    room = jnp.minimum(sizes[donor] - 1, reach - sizes[receiver]) // 2
    room = jnp.where((donor == order[0]) | (receiver == order[0]) | (sizes[receiver] == 0), 0, jnp.maximum(room, 0))
    shifted = jax.random.randint(jax.random.fold_in(own, 4), (count // 2,), 0, 1 << 20) % (room + 1)
    sizes = sizes.at[donor].add(-shifted).at[receiver].add(shifted)
    members = jnp.searchsorted(jnp.cumsum(sizes), jnp.arange(rows * top), side="right").astype(jnp.int32)
    grid = members.reshape(top, rows).T
    grid = grid[jax.random.permutation(jax.random.fold_in(own, 1), rows)]
    rotation = jax.random.randint(jax.random.fold_in(own, 2), (rows, 1), 0, top)
    return jnp.take_along_axis(grid, (jnp.arange(top)[None, :] + rotation) % top, axis=1)


def shares(number_of, total, reach, lean, full):
    weights = [(1 << 20) // math.isqrt(rank ** lean) + 1 for rank in range(1, number_of + 1)]
    largest = reach if full else min(reach, max(-(-total // number_of), total * weights[0] // sum(weights)))
    least = 1 if total - largest >= number_of - 1 else 0
    given, spare = [largest] + [least] * (number_of - 1), total - largest - least * (number_of - 1)
    while spare > 0:
        movable = [i for i in range(1, number_of) if given[i] < largest] or [i for i in range(1, number_of) if given[i] < reach]
        whole, budget = sum([weights[i] for i in movable]), spare
        for i in movable:
            addition = min(reach - given[i], max(1, budget * weights[i] // whole), spare)
            given[i] = given[i] + addition
            spare = spare - addition
    return np.array(given)


def centred(key, shape, deviation, limit, pieces=(), held_as=jnp.bfloat16):
    drawn = deviation * jax.random.normal(key, shape, jnp.float32)
    if pieces:
        drawn = drawn * shard_levels(key, shape, pieces, -0.22, 0.18)
    return jnp.clip(drawn, -limit, limit).astype(held_as)


def setup_inputs(seed: int = 0) -> dict:
    key_of = jax.random.split(jax.random.key(seed), 10)
    features = centred(key_of[0], (PATCHES, D), 1.0, 6.0, ((0, 128),))
    w_embed = centred(key_of[1], (D, C), D ** -0.5, 0.1875)
    owner_device_keys = jax.random.split(jax.random.fold_in(key_of[2], 1), PATCHES // P_DEV)
    owner_device_turns = jax.random.permutation(jax.random.fold_in(key_of[2], 3), PATCHES // P_DEV)
    owner_device = jax.vmap(lambda own, number: deal_out(jax.random.fold_in(key_of[2], 2), own, number, P_DEV, DEVICES, 1, CAP, 2))(owner_device_keys, owner_device_turns).reshape((PATCHES, 1))
    voxel_slot = plant(jax.random.randint(key_of[3], (PATCHES,), 0, V_DEV), jax.random.fold_in(key_of[3], 1), 0, V_DEV - 1).astype(jnp.int32)
    window_ids = jnp.searchsorted(jnp.cumsum(ragged_sizes(key_of[4], WINDOWS, VOXELS, WMOST, 2)), jnp.arange(VOXELS), side="right").astype(jnp.int32)
    w_heads = draw_w_heads(jax.random.fold_in(key_of[9], 71), 0)
    w_out = centred(key_of[6], (C, C), C ** -0.5, 0.21875)
    w_up = centred(key_of[7], (C, FFH), C ** -0.5, 0.21875)
    w_down = centred(key_of[8], (FFH, C), FFH ** -0.5, 0.109375)
    return {"features": features, "w_embed": w_embed, "owner_device": owner_device, "voxel_slot": voxel_slot, "window_ids": window_ids, "w_heads": w_heads, "w_out": w_out, "w_up": w_up, "w_down": w_down}


epsilon = 1e-06

def layer_norm(values):
    average = lax.optimization_barrier(jnp.mean(values, axis=-1, keepdims=True))
    centered = values - average
    variance = lax.optimization_barrier(jnp.mean(centered * centered, axis=-1, keepdims=True))
    return centered * lax.rsqrt(variance + epsilon)

def window_attention(queries, key_value, query_tags, key_tags):
    head_size = C // HEADS
    head_queries = queries.astype(jnp.float32).reshape(queries.shape[0], HEADS, head_size)
    head_keys = key_value[:, :C].astype(jnp.float32).reshape(key_value.shape[0], HEADS, head_size)
    head_values = key_value[:, C:].astype(jnp.float32).reshape(key_value.shape[0], HEADS, head_size)
    scores = jnp.einsum('qhd,khd->hqk', head_queries, head_keys) * head_size ** (-0.5)
    same = query_tags[:, None] == key_tags[None, :]
    scores = jnp.where(same[None], scores, -1e+30)
    highest = lax.optimization_barrier(jnp.max(scores, axis=-1, keepdims=True))
    exponent = jnp.exp(scores - highest)
    weights = (exponent / lax.optimization_barrier(jnp.sum(exponent, axis=-1, keepdims=True))).astype(jnp.bfloat16)
    attended = jnp.einsum('hqk,khd->qhd', weights.astype(jnp.float32), head_values)
    return attended.reshape(queries.shape[0], C).astype(jnp.bfloat16)

def reference(features, w_embed, owner_device, voxel_slot, window_ids, w_heads, w_out, w_up, w_down):
    projected = jnp.dot(features, w_embed, preferred_element_type=jnp.float32).astype(jnp.bfloat16)
    target = (owner_device[:, 0] * V_DEV + voxel_slot).astype(jnp.int32)
    summed = jax.ops.segment_sum(projected.astype(jnp.float32), target, num_segments=VOXELS)
    counts = jax.ops.segment_sum(jnp.ones(target.shape, jnp.float32), target, num_segments=VOXELS)
    latent = summed / jnp.maximum(counts, 1.0)[:, None]
    normed = layer_norm(latent).astype(jnp.bfloat16)
    triple = jnp.dot(normed, w_heads, preferred_element_type=jnp.float32).astype(jnp.bfloat16)
    queries = triple[:, :C]
    key_value = triple[:, C:]
    tags = (window_ids + 1).astype(jnp.int32)
    padding = jnp.zeros((WMOST, 2 * C), jnp.bfloat16)
    key_pad = jnp.concatenate([padding, key_value, padding], axis=0)
    tag_zeros = jnp.zeros((WMOST,), jnp.int32)
    tag_pad = jnp.concatenate([tag_zeros, tags, tag_zeros], axis=0)

    def one_block(block_index):
        first_row = (block_index * V_DEV).astype(jnp.int32)
        block_queries = lax.dynamic_slice_in_dim(queries, first_row, V_DEV, 0)
        block_tags = lax.dynamic_slice_in_dim(tags, first_row, V_DEV, 0)
        block_keys = lax.dynamic_slice_in_dim(key_pad, first_row, V_DEV + 2 * WMOST, 0)
        block_key_tags = lax.dynamic_slice_in_dim(tag_pad, first_row, V_DEV + 2 * WMOST, 0)
        return window_attention(block_queries, block_keys, block_tags, block_key_tags)
    attended = lax.map(one_block, jnp.arange(VOXELS // V_DEV, dtype=jnp.int32)).reshape(VOXELS, C)
    middle = latent + jnp.dot(attended, w_out, preferred_element_type=jnp.float32)
    normed_two = layer_norm(middle).astype(jnp.bfloat16)
    expanded = jax.nn.gelu(jnp.dot(normed_two, w_up, preferred_element_type=jnp.float32), approximate=True).astype(jnp.bfloat16)
    return (middle + jnp.dot(expanded, w_down, preferred_element_type=jnp.float32)).astype(jnp.bfloat16)
```

```python
import jax
import jax.numpy as jnp
from jax import lax
from jax.experimental import pallas as pl
from jax.experimental.pallas import tpu as pltpu
from jax.sharding import PartitionSpec as P

C = 768
HEADS = 12
HEAD = C // HEADS
PAIRS = HEADS // 2
LANES = 128
CHUNKS = C // LANES
BLOCK = 128
epsilon = 1e-06
AXES = ("view", "vox")
f32 = jnp.float32
bf16 = jnp.bfloat16
i32 = jnp.int32
MASKED = -1e30


def passed_along(block, distance):
    devices = range(lax.axis_size(AXES))
    route = [(i - distance, i) for i in devices if i - distance in devices]
    return lax.ppermute(block, AXES, route)


def layer_norm(values):
    average = jnp.mean(values, axis=-1, keepdims=True)
    centered = values - average
    variance = jnp.mean(centered * centered, axis=-1, keepdims=True)
    return centered * lax.rsqrt(variance + epsilon)


def across(a, b):
    return lax.dot_general(a, b, (((1,), (1,)), ((), ())), preferred_element_type=f32)


def dot(a, b):
    return jnp.dot(a, b, preferred_element_type=f32)


def iota(shape, dim):
    return lax.broadcasted_iota(i32, shape, dim)


def params(mib):
    return pltpu.CompilerParams(vmem_limit_bytes=mib << 20)


def dispatch_kernel(
    features_ref, embed_ref, owner_ref, slot_ref, out_ref, payload_ref, position_ref, digits_ref
):
    step = pl.program_id(0)
    patches = features_ref.shape[0]
    devices = digits_ref.shape[1]
    group = out_ref.shape[0]
    capacity = (out_ref.shape[1] - 8) // CHUNKS
    part = 256
    mine = lax.rem(lax.axis_index("vox"), LANES // capacity)

    @pl.when(step == 0)
    def _():
        owner = owner_ref[...]
        hits = jnp.where(iota((devices, patches), 0) == owner, 1.0, 0.0)
        earlier = jnp.where(iota((part, part), 0) < iota((part, part), 1), 1.0, 0.0).astype(bf16)
        running = jnp.zeros((devices, 1), f32)
        ranks = []
        for start in range(0, patches, part):
            here = hits[:, start : start + part]
            before = dot(here.astype(bf16), earlier) + running
            running = running + jnp.sum(here, axis=1, keepdims=True)
            ranks.append(jnp.sum(here * before, axis=0, keepdims=True))
        rank = jnp.concatenate(ranks, axis=1).astype(i32)
        position_ref[...] = owner * capacity + rank
        place = jnp.where(iota((LANES, patches), 0) == rank + capacity * mine, 1.0, 0.0).astype(bf16)
        code = slot_ref[...] + 1
        high = (code >> 4).astype(f32)
        low = (code & 15).astype(f32)
        digits_ref[0] = across((hits * high).astype(bf16), place)
        digits_ref[1] = across((hits * low).astype(bf16), place)
        payload_ref[...] = dot(features_ref[...], embed_ref[...]).astype(bf16)

    rows = group * capacity
    chosen = jnp.where(iota((rows, patches), 0) + step * rows == position_ref[...], 1.0, 0.0)
    block = dot(chosen.astype(bf16), payload_ref[...]).astype(bf16)
    for c in range(CHUNKS):
        out_ref[:, c * capacity : (c + 1) * capacity, :] = block[
            :, c * LANES : (c + 1) * LANES
        ].reshape(group, capacity, LANES)
    here = pl.ds(pl.multiple_of(step * group, 8), group)
    high = jnp.broadcast_to(digits_ref[0, here, :][:, None, :], (group, 8, LANES))
    low = jnp.broadcast_to(digits_ref[1, here, :][:, None, :], (group, 8, LANES))
    out_ref[:, CHUNKS * capacity :, :] = jnp.where(
        iota((group, 8, LANES), 1) < 4, high, low
    ).astype(bf16)


def dispatch(features, w_embed, owner, slot, devices, capacity):
    patches, width = features.shape
    group = 32
    tall = CHUNKS * capacity + 8
    whole = lambda i: (0, 0)
    return pl.pallas_call(
        dispatch_kernel,
        out_shape=jax.ShapeDtypeStruct((devices, tall, LANES), bf16),
        grid=(devices // group,),
        in_specs=[
            pl.BlockSpec((patches, width), whole, pipeline_mode=pl.Buffered(1)),
            pl.BlockSpec((width, C), whole, pipeline_mode=pl.Buffered(1)),
            pl.BlockSpec((1, patches), whole),
            pl.BlockSpec((1, patches), whole),
        ],
        out_specs=pl.BlockSpec((group, tall, LANES), lambda i: (i, 0, 0)),
        scratch_shapes=[
            pltpu.VMEM((patches, C), bf16),
            pltpu.VMEM((1, patches), i32),
            pltpu.VMEM((2, devices, LANES), f32),
        ],
        compiler_params=params(24),
        name="dispatch",
    )(features, w_embed, owner, slot)


def gather_kernel(arrived_ref, latent_ref, normed_ref, total_ref, tally_ref):
    step = pl.program_id(0)
    sources = arrived_ref.shape[0]
    capacity = (arrived_ref.shape[1] - 8) // CHUNKS
    voxels = latent_ref.shape[0]
    each = LANES // capacity
    digits = arrived_ref[:, CHUNKS * capacity :, :].astype(f32)
    digits = jnp.sum(digits.reshape(sources // each, each, 8, LANES), axis=1)
    code = digits[:, 0, :] * 16.0 + digits[:, 4, :]
    slot = jnp.concatenate([code[g : g + 1] for g in range(sources // each)], axis=1).astype(i32) - 1
    rows = sources * capacity
    member = jnp.where(iota((voxels, rows), 0) == slot, 1.0, 0.0)
    data = jnp.concatenate(
        [
            arrived_ref[:, c * capacity : (c + 1) * capacity, :].reshape(rows, LANES)
            for c in range(CHUNKS)
        ],
        axis=1,
    )
    added = dot(member.astype(bf16), data)
    counted = member[:, :LANES]
    for k in range(1, rows // LANES):
        counted = counted + member[:, k * LANES : (k + 1) * LANES]

    @pl.when(step == 0)
    def _():
        total_ref[...] = added
        tally_ref[...] = counted

    @pl.when(step > 0)
    def _():
        total_ref[...] += added
        tally_ref[...] += counted

    @pl.when(step == pl.num_programs(0) - 1)
    def _():
        counts = jnp.sum(tally_ref[...], axis=1, keepdims=True)
        latent = total_ref[...] / jnp.maximum(counts, 1.0)
        latent_ref[...] = latent
        normed_ref[...] = layer_norm(latent).astype(bf16)


def gather(arrived, voxels):
    sources, tall, _ = arrived.shape
    group = 32
    whole = lambda i: (0, 0)
    return pl.pallas_call(
        gather_kernel,
        out_shape=(
            jax.ShapeDtypeStruct((voxels, C), f32),
            jax.ShapeDtypeStruct((voxels, C), bf16),
        ),
        grid=(sources // group,),
        in_specs=[pl.BlockSpec((group, tall, LANES), lambda i: (i, 0, 0))],
        out_specs=(pl.BlockSpec((voxels, C), whole), pl.BlockSpec((voxels, C), whole)),
        scratch_shapes=[pltpu.VMEM((voxels, C), f32), pltpu.VMEM((voxels, LANES), f32)],
        compiler_params=params(20),
        name="gather",
    )(arrived)


def column_of(row):
    return jnp.broadcast_to(row, (LANES, row.shape[1])).T


def by_half(first, second):
    return jnp.where(iota(first.shape, 1) < HEAD, first, second)


def scores_of(query_pair, key_pair, half, bias):
    lane = iota(query_pair.shape, 1)
    keep = (lane >= HEAD) if half else (lane < HEAD)
    return across(jnp.where(keep, query_pair, jnp.zeros_like(query_pair)), key_pair) + bias


def weighted(score, highest, value_pair):
    exponent = jnp.exp(score - highest).astype(bf16)
    wide = jnp.concatenate([value_pair, jnp.ones_like(value_pair)], axis=1)
    return dot(exponent, wide)


def bias_of(column, row):
    tiles = [
        jnp.where(column == row[:, k : k + LANES], 0.0, MASKED) for k in range(0, row.shape[1], LANES)
    ]
    return jnp.concatenate(tiles, axis=1)


def near_kernel(
    tag_ref, tag_row_ref, normed_ref, heads_ref, query_ref, value_ref, top_ref, sum_ref, kv_ref, column_ref
):
    voxels = normed_ref.shape[0]
    blocks = voxels // BLOCK
    normed = normed_ref[...]
    query_ref[...] = dot(normed, heads_ref[:, :C]).astype(bf16) * jnp.asarray(HEAD**-0.5, bf16)
    kv_ref[...] = dot(normed, heads_ref[:, C:]).astype(bf16)
    column_ref[...] = column_of(tag_row_ref[...])

    def one_block(b, carry):
        rows = pl.ds(pl.multiple_of(b * BLOCK, BLOCK), BLOCK)
        first, last = tag_ref[b * BLOCK], tag_ref[b * BLOCK + BLOCK - 1]
        low = i32(0)
        high = i32(0)
        for k in range(blocks):
            low = low + (tag_ref[k * BLOCK + BLOCK - 1] < first).astype(i32)
            high = high + (tag_ref[k * BLOCK] <= last).astype(i32)
        count = high - low

        def attend(n):
            keys = pl.ds(pl.multiple_of(low * BLOCK, BLOCK), n * BLOCK)
            bias = bias_of(column_ref[rows, :], tag_row_ref[:, keys])
            for p in range(PAIRS):
                lanes = slice(p * LANES, (p + 1) * LANES)
                query = query_ref[rows, lanes]
                key = kv_ref[keys, lanes]
                value = kv_ref[keys, C + p * LANES : C + (p + 1) * LANES]
                outs, tops = [], []
                for half in range(2):
                    score = scores_of(query, key, half, bias)
                    highest = jnp.max(score, axis=1, keepdims=True)
                    outs.append(weighted(score, highest, value))
                    tops.append(jnp.broadcast_to(highest, (BLOCK, LANES)))
                value_ref[rows, lanes] = by_half(outs[0][:, :LANES], outs[1][:, :LANES])
                sum_ref[rows, lanes] = by_half(outs[0][:, LANES:], outs[1][:, LANES:])
                top_ref[rows, lanes] = by_half(tops[0], tops[1])

        for n in range(1, blocks + 1):
            pl.when(count == n)(lambda n=n: attend(n))
        return carry

    lax.fori_loop(0, blocks, one_block, 0)


VMEM = pl.BlockSpec(memory_space=pltpu.VMEM)
SMEM = pl.BlockSpec(memory_space=pltpu.SMEM)


def near(tags, normed, w_heads):
    voxels = normed.shape[0]
    return pl.pallas_call(
        near_kernel,
        out_shape=(
            jax.ShapeDtypeStruct((voxels, C), bf16),
            jax.ShapeDtypeStruct((voxels, C), f32),
            jax.ShapeDtypeStruct((voxels, C), f32),
            jax.ShapeDtypeStruct((voxels, C), f32),
        ),
        in_specs=[SMEM, VMEM, VMEM, VMEM],
        out_specs=(VMEM, VMEM, VMEM, VMEM),
        scratch_shapes=[pltpu.VMEM((voxels, 2 * C), bf16), pltpu.VMEM((voxels, LANES), i32)],
        compiler_params=params(20),
        name="near",
    )(tags, tags.reshape(1, voxels), normed, w_heads)


def finish_kernel(
    tag_ref, before_tag_ref, after_tag_ref, tag_row_ref, before_row_ref, after_row_ref,
    before_ref, after_ref, heads_ref, query_ref, near_value_ref, near_top_ref, near_sum_ref, latent_ref,
    w_out_ref, w_up_ref, w_down_ref, out_ref, kv_ref, column_ref, row_ref, value_ref, top_ref, sum_ref
):
    voxels = query_ref.shape[0]
    blocks = voxels // BLOCK
    sizes = (2, blocks)
    value_ref[...] = near_value_ref[...]
    top_ref[...] = near_top_ref[...]
    sum_ref[...] = near_sum_ref[...]
    column_ref[...] = column_of(tag_row_ref[...])
    start_tag, end_tag = tag_ref[0], tag_ref[voxels - 1]
    before_count = i32(0)
    after_count = i32(0)
    for k in range(blocks):
        before_count += (before_tag_ref[k * BLOCK + BLOCK - 1] == start_tag).astype(i32)
        after_count += (after_tag_ref[k * BLOCK] == end_tag).astype(i32)

    def project(side, source_ref, source_row_ref, n):
        size = n * BLOCK
        start = 0 if side else voxels - size
        kv_ref[side, :size] = dot(source_ref[start : start + size, :], heads_ref[:, C:]).astype(bf16)
        row_ref[side, :, :size] = source_row_ref[:, start : start + size]

    def span(count, action):
        for lower, n in zip((0,) + sizes, sizes):
            pl.when(jnp.logical_and(count > lower, count <= n))(lambda n=n: action(n))

    span(before_count, lambda n: project(0, before_ref, before_row_ref, n))
    span(after_count, lambda n: project(1, after_ref, after_row_ref, n))

    def one_block(step, carry):
        side, b = step // blocks, step % blocks
        rows = pl.ds(pl.multiple_of(b * BLOCK, BLOCK), BLOCK)
        touched = jnp.where(
            side == 0, tag_ref[b * BLOCK] == start_tag, tag_ref[b * BLOCK + BLOCK - 1] == end_tag
        )
        count = jnp.where(touched, jnp.where(side == 0, before_count, after_count), 0)

        def attend(n):
            size = n * BLOCK
            bias = bias_of(column_ref[rows, :], row_ref[side, :, :size])
            for p in range(PAIRS):
                lanes = slice(p * LANES, (p + 1) * LANES)
                query = query_ref[rows, lanes]
                key = kv_ref[side, :size, lanes]
                value = kv_ref[side, :size, C + p * LANES : C + (p + 1) * LANES]
                old = top_ref[rows, lanes]
                outs, tops = [], []
                for half in range(2):
                    score = scores_of(query, key, half, bias)
                    highest = jnp.maximum(
                        jnp.max(score, axis=1, keepdims=True), old[:, half * HEAD : half * HEAD + 1]
                    )
                    outs.append(weighted(score, highest, value))
                    tops.append(jnp.broadcast_to(highest, (BLOCK, LANES)))
                top = by_half(tops[0], tops[1])
                fade = jnp.exp(old - top)
                value_ref[rows, lanes] = value_ref[rows, lanes] * fade + by_half(
                    outs[0][:, :LANES], outs[1][:, :LANES]
                )
                sum_ref[rows, lanes] = sum_ref[rows, lanes] * fade + by_half(
                    outs[0][:, LANES:], outs[1][:, LANES:]
                )
                top_ref[rows, lanes] = top

        span(count, attend)
        return carry

    lax.fori_loop(0, 2 * blocks, one_block, 0)
    attended = (value_ref[...] / sum_ref[...]).astype(bf16)
    middle = latent_ref[...] + dot(attended, w_out_ref[...])
    normed = layer_norm(middle).astype(bf16)
    hidden = w_up_ref.shape[1]
    part = 512
    total = middle
    for k in range(0, hidden, part):
        raised = jax.nn.gelu(dot(normed, w_up_ref[:, k : k + part]), approximate=True).astype(bf16)
        total = total + dot(raised, w_down_ref[k : k + part, :])
    out_ref[...] = total.astype(bf16)


def finish(tags, before_tag, after_tag, before, after, w_heads, query, value, top, total, latent, w_out, w_up, w_down):
    voxels = query.shape[0]
    row = lambda t: t.reshape(1, voxels)
    return pl.pallas_call(
        finish_kernel,
        out_shape=jax.ShapeDtypeStruct((voxels, C), bf16),
        in_specs=[SMEM] * 3 + [VMEM] * 14,
        out_specs=VMEM,
        scratch_shapes=[
            pltpu.VMEM((2, voxels, 2 * C), bf16),
            pltpu.VMEM((voxels, LANES), i32),
            pltpu.VMEM((2, 1, voxels), i32),
            pltpu.VMEM((voxels, C), f32),
            pltpu.VMEM((voxels, C), f32),
            pltpu.VMEM((voxels, C), f32),
        ],
        compiler_params=params(26),
        name="finish",
    )(
        tags, before_tag, after_tag, row(tags), row(before_tag), row(after_tag), before, after, w_heads,
        query, value, top, total, latent, w_out, w_up, w_down
    )


def local(features, w_embed, owner_device, voxel_slot, window_ids, w_heads, w_out, w_up, w_down):
    devices = lax.axis_size(AXES)
    patches = features.shape[0]
    voxels = window_ids.shape[0]
    capacity = max(2, 2 * patches // devices)
    buffer = dispatch(
        features, w_embed, owner_device.reshape(1, patches), voxel_slot.reshape(1, patches), devices, capacity
    )
    buffer, tags = lax.optimization_barrier((buffer, window_ids + 1))
    arrived = lax.all_to_all(buffer, AXES, split_axis=0, concat_axis=0, tiled=True)
    before_tag = passed_along(tags, 1)
    after_tag = passed_along(tags, -1)
    arrived, before_tag, after_tag = lax.optimization_barrier((arrived, before_tag, after_tag))
    latent, normed = gather(arrived, voxels)
    before = passed_along(normed, 1)
    after = passed_along(normed, -1)
    query, value, top, total = near(tags, normed, w_heads)
    return finish(
        tags, before_tag, after_tag, before, after, w_heads, query, value, top, total, latent, w_out, w_up, w_down
    )


def solution(mesh):
    rows = P(AXES, None)
    return jax.shard_map(
        local,
        mesh=mesh,
        in_specs=(rows, P(), rows, P(AXES), P(AXES), P(), P(), P(), P()),
        out_specs=rows,
        check_vma=False,
    )
```

```python
import jax
import jax.numpy as jnp
from jax import lax
from jax.experimental import pallas as pl
from jax.experimental.pallas import tpu as pltpu
from jax.sharding import PartitionSpec as P

C = 768
HEADS = 12
HEAD = C // HEADS
PAIRS = HEADS // 2
LANES = 128
CHUNKS = C // LANES
BLOCK = 128
epsilon = 1e-06
AXES = ("view", "vox")
f32 = jnp.float32
bf16 = jnp.bfloat16
i32 = jnp.int32
MASKED = -1e30


def passed_along(block, distance):
    devices = range(lax.axis_size(AXES))
    route = [(i - distance, i) for i in devices if i - distance in devices]
    return lax.ppermute(block, AXES, route)


def layer_norm(values):
    average = jnp.mean(values, axis=-1, keepdims=True)
    centered = values - average
    variance = jnp.mean(centered * centered, axis=-1, keepdims=True)
    return centered * lax.rsqrt(variance + epsilon)


def across(a, b):
    return lax.dot_general(a, b, (((1,), (1,)), ((), ())), preferred_element_type=f32)


def dot(a, b):
    return jnp.dot(a, b, preferred_element_type=f32)


def iota(shape, dim):
    return lax.broadcasted_iota(i32, shape, dim)


def params(mib):
    return pltpu.CompilerParams(vmem_limit_bytes=mib << 20)


GROUPS = 4


def dispatch_kernel(
    features_hbm, embed_hbm, owner_hbm, slot_hbm, out_hbm,
    features_ref, embed_ref, owner_ref, slot_ref, out_ref, payload_ref, position_ref, digits_ref, in_sem, out_sem
):
    copies = [
        pltpu.make_async_copy(source, target, in_sem.at[k])
        for k, (source, target) in enumerate(
            (
                (owner_hbm, owner_ref),
                (slot_hbm, slot_ref),
                (features_hbm, features_ref),
                (embed_hbm, embed_ref),
            )
        )
    ]
    for copy in copies:
        copy.start()
    patches = features_ref.shape[0]
    devices = digits_ref.shape[1]
    group = devices // GROUPS
    capacity = (out_ref.shape[1] - 8) // CHUNKS
    part = 256
    mine = lax.rem(lax.axis_index("vox"), LANES // capacity)
    earlier = jnp.where(iota((part, part), 0) < iota((part, part), 1), 1.0, 0.0).astype(bf16)
    copies[0].wait()
    copies[1].wait()
    owner = owner_ref[...]
    hits = jnp.where(iota((devices, patches), 0) == owner, 1.0, 0.0)
    running = jnp.zeros((devices, 1), f32)
    ranks = []
    for start in range(0, patches, part):
        here = hits[:, start : start + part]
        before = dot(here.astype(bf16), earlier) + running
        running = running + jnp.sum(here, axis=1, keepdims=True)
        ranks.append(jnp.sum(here * before, axis=0, keepdims=True))
    rank = jnp.concatenate(ranks, axis=1).astype(i32)
    position_ref[...] = owner * capacity + rank
    place = jnp.where(iota((LANES, patches), 0) == rank + capacity * mine, 1.0, 0.0).astype(bf16)
    code = slot_ref[...] + 1
    digits_ref[0] = across((hits * (code >> 4).astype(f32)).astype(bf16), place)
    digits_ref[1] = across((hits * (code & 15).astype(f32)).astype(bf16), place)
    copies[2].wait()
    copies[3].wait()
    payload_ref[...] = dot(features_ref[...], embed_ref[...]).astype(bf16)
    rows = group * capacity
    sends = []
    for g in range(GROUPS):
        here = slice(g * group, (g + 1) * group)
        chosen = jnp.where(iota((rows, patches), 0) + g * rows == position_ref[...], 1.0, 0.0)
        block = dot(chosen.astype(bf16), payload_ref[...]).astype(bf16)
        for c in range(CHUNKS):
            out_ref[here, c * capacity : (c + 1) * capacity, :] = block[
                :, c * LANES : (c + 1) * LANES
            ].reshape(group, capacity, LANES)
        high = jnp.broadcast_to(digits_ref[0, here, :][:, None, :], (group, 8, LANES))
        low = jnp.broadcast_to(digits_ref[1, here, :][:, None, :], (group, 8, LANES))
        out_ref[here, CHUNKS * capacity :, :] = jnp.where(
            iota((group, 8, LANES), 1) < 4, high, low
        ).astype(bf16)
        send = pltpu.make_async_copy(out_ref.at[here], out_hbm.at[here], out_sem.at[g])
        send.start()
        sends.append(send)
    for send in sends:
        send.wait()


def kept(*arrays):
    return [pltpu.with_memory_space_constraint(array, pltpu.HBM) for array in arrays]


HBM = pl.BlockSpec(memory_space=pltpu.HBM)
VMEM = pl.BlockSpec(memory_space=pltpu.VMEM)
SMEM = pl.BlockSpec(memory_space=pltpu.SMEM)


def dispatch(features, w_embed, owner, slot, devices, capacity):
    patches, width = features.shape
    tall = CHUNKS * capacity + 8
    return pl.pallas_call(
        dispatch_kernel,
        out_shape=pltpu.HBM((devices, tall, LANES), bf16),
        in_specs=[HBM] * 4,
        out_specs=HBM,
        scratch_shapes=[
            pltpu.VMEM((patches, width), bf16),
            pltpu.VMEM((width, C), bf16),
            pltpu.VMEM((1, patches), i32),
            pltpu.VMEM((1, patches), i32),
            pltpu.VMEM((devices, tall, LANES), bf16),
            pltpu.VMEM((patches, C), bf16),
            pltpu.VMEM((1, patches), i32),
            pltpu.VMEM((2, devices, LANES), f32),
            pltpu.SemaphoreType.DMA((4,)),
            pltpu.SemaphoreType.DMA((GROUPS,)),
        ],
        compiler_params=params(32),
        name="dispatch",
    )(*kept(features, w_embed, owner, slot))


def gather_kernel(arrived_hbm, latent_ref, normed_ref, arrived_ref, digit_ref, member_ref, sem):
    sources = arrived_ref.shape[0]
    capacity = arrived_ref.shape[1] // CHUNKS
    tall = CHUNKS * capacity
    voxels = latent_ref.shape[0]
    each = LANES // capacity
    digit_copy = pltpu.make_async_copy(arrived_hbm.at[:, tall:, :], digit_ref, sem.at[0])
    digit_copy.start()
    data_copy = pltpu.make_async_copy(arrived_hbm.at[:, :tall, :], arrived_ref, sem.at[1])
    data_copy.start()
    digit_copy.wait()
    digits = jnp.sum(digit_ref[...].astype(f32).reshape(sources // each, each, 8, LANES), axis=1)
    code = (digits[:, 0, :] * 16.0 + digits[:, 4, :]).astype(i32) - 1
    counted = jnp.zeros((voxels, LANES), f32)
    for g in range(sources // each):
        member = jnp.where(iota((voxels, LANES), 0) == code[g : g + 1], 1.0, 0.0)
        counted = counted + member
        member_ref[:, g * LANES : (g + 1) * LANES] = member.astype(bf16)
    counts = jnp.sum(counted, axis=1, keepdims=True)
    data_copy.wait()
    data = jnp.concatenate(
        [
            arrived_ref[:, c * capacity : (c + 1) * capacity, :].reshape(sources * capacity, LANES)
            for c in range(CHUNKS)
        ],
        axis=1,
    )
    latent = dot(member_ref[...], data) / jnp.maximum(counts, 1.0)
    latent_ref[...] = latent
    normed_ref[...] = layer_norm(latent).astype(bf16)


def gather(arrived, voxels):
    sources, tall, _ = arrived.shape
    return pl.pallas_call(
        gather_kernel,
        out_shape=(
            jax.ShapeDtypeStruct((voxels, C), f32),
            jax.ShapeDtypeStruct((voxels, C), bf16),
        ),
        in_specs=[HBM],
        out_specs=(VMEM, VMEM),
        scratch_shapes=[
            pltpu.VMEM((sources, tall - 8, LANES), bf16),
            pltpu.VMEM((sources, 8, LANES), bf16),
            pltpu.VMEM((voxels, sources * ((tall - 8) // CHUNKS)), bf16),
            pltpu.SemaphoreType.DMA((2,)),
        ],
        compiler_params=params(24),
        name="gather",
    )(arrived)


def column_of(row):
    return jnp.broadcast_to(row, (LANES, row.shape[1])).T


def by_half(both):
    first, second = both[:BLOCK], both[BLOCK:]
    return jnp.where(iota(first.shape, 1) < HEAD, first, second)


def scores_of(query_pair, key_pair, bias):
    left = iota(query_pair.shape, 1) < HEAD
    none = jnp.zeros_like(query_pair)
    both = jnp.concatenate([jnp.where(left, query_pair, none), jnp.where(left, none, query_pair)], axis=0)
    return across(both, key_pair) + bias


def weighted(score, highest, value_pair):
    exponent = jnp.exp(score - highest).astype(bf16)
    wide = jnp.concatenate([value_pair, jnp.ones_like(value_pair)], axis=1)
    return dot(exponent, wide)


def bias_of(column, row):
    tiles = [
        jnp.where(column == row[:, k : k + LANES], 0.0, MASKED) for k in range(0, row.shape[1], LANES)
    ]
    bias = jnp.concatenate(tiles, axis=1)
    return jnp.concatenate([bias, bias], axis=0)


def rims(tag_ref, before_tag_ref, after_tag_ref):
    voxels = tag_ref.shape[0]
    blocks = voxels // BLOCK
    start_tag, end_tag = tag_ref[0], tag_ref[voxels - 1]
    head = i32(0)
    tail = i32(0)
    for k in range(blocks):
        head += (tag_ref[k * BLOCK] == start_tag).astype(i32)
        tail += (tag_ref[k * BLOCK + BLOCK - 1] == end_tag).astype(i32)
    ring = [lax.axis_index(axis) for axis in AXES]
    ends = [lax.axis_size(axis) - 1 for axis in AXES]
    first = jnp.logical_and(ring[0] == 0, ring[1] == 0)
    final = jnp.logical_and(ring[0] == ends[0], ring[1] == ends[1])
    head = jnp.where(jnp.logical_or(first, before_tag_ref[voxels - 1] != start_tag), 0, head)
    tail = jnp.where(jnp.logical_or(final, after_tag_ref[0] != end_tag), 0, tail)
    return head, tail


SPAN = 2 * BLOCK


def feed_forward(attended, latent, w_out_ref, w_up_ref, w_down_ref):
    middle = latent + dot(attended, w_out_ref[...])
    normed = layer_norm(middle).astype(bf16)
    total = middle
    part = 512
    for k in range(0, w_up_ref.shape[1], part):
        raised = jax.nn.gelu(dot(normed, w_up_ref[:, k : k + part]), approximate=True).astype(bf16)
        total = total + dot(raised, w_down_ref[k : k + part, :])
    return total.astype(bf16)


def near_kernel(
    tag_ref, before_tag_ref, after_tag_ref, tag_row_ref, normed_ref, heads_ref, latent_ref, w_out_ref, up_hbm, down_hbm,
    query_ref, value_ref, top_ref, sum_ref, out_ref, kv_ref, column_ref, up_ref, down_ref, sem
):
    up_copy = pltpu.make_async_copy(up_hbm, up_ref, sem.at[0])
    down_copy = pltpu.make_async_copy(down_hbm, down_ref, sem.at[1])
    up_copy.start()
    down_copy.start()
    voxels = normed_ref.shape[0]
    blocks = voxels // BLOCK
    normed = normed_ref[...]
    query_ref[...] = dot(normed, heads_ref[:, :C]).astype(bf16) * jnp.asarray(HEAD**-0.5, bf16)
    kv_ref[...] = dot(normed, heads_ref[:, C:]).astype(bf16)
    column_ref[...] = column_of(tag_row_ref[...])

    def one_block(b, carry):
        rows = pl.ds(pl.multiple_of(b * BLOCK, BLOCK), BLOCK)
        first, last = tag_ref[b * BLOCK], tag_ref[b * BLOCK + BLOCK - 1]
        low = i32(0)
        high = i32(0)
        for k in range(blocks):
            low = low + (tag_ref[k * BLOCK + BLOCK - 1] < first).astype(i32)
            high = high + (tag_ref[k * BLOCK] <= last).astype(i32)
        count = high - low

        def attend(n):
            keys = pl.ds(pl.multiple_of(low * BLOCK, BLOCK), n * BLOCK)
            bias = bias_of(column_ref[rows, :], tag_row_ref[:, keys])
            for p in range(PAIRS):
                lanes = slice(p * LANES, (p + 1) * LANES)
                score = scores_of(query_ref[rows, lanes], kv_ref[keys, lanes], bias)
                highest = jnp.max(score, axis=1, keepdims=True)
                result = weighted(score, highest, kv_ref[keys, C + p * LANES : C + (p + 1) * LANES])
                value_ref[rows, lanes] = by_half(result[:, :LANES])
                sum_ref[rows, lanes] = by_half(result[:, LANES:])
                top_ref[rows, lanes] = by_half(jnp.broadcast_to(highest, (2 * BLOCK, LANES)))

        for n in range(1, blocks + 1):
            pl.when(count == n)(lambda n=n: attend(n))
        return carry

    lax.fori_loop(0, blocks, one_block, 0)
    head, tail = rims(tag_ref, before_tag_ref, after_tag_ref)
    up_copy.wait()
    down_copy.wait()

    def one_span(k, carry):
        start = jnp.minimum((head + 2 * k) * BLOCK, voxels - SPAN)
        rows = pl.ds(pl.multiple_of(start, BLOCK), SPAN)
        attended = (value_ref[rows, :] / sum_ref[rows, :]).astype(bf16)
        out_ref[rows, :] = feed_forward(attended, latent_ref[rows, :], w_out_ref, up_ref, down_ref)
        return carry

    lax.fori_loop(0, (jnp.maximum(blocks - head - tail, 0) + 1) // 2, one_span, 0)


def near(tags, before_tag, after_tag, normed, w_heads, latent, w_out, w_up, w_down):
    voxels = normed.shape[0]
    state = jax.ShapeDtypeStruct((voxels, C), f32)
    rows = jax.ShapeDtypeStruct((voxels, C), bf16)
    return pl.pallas_call(
        near_kernel,
        out_shape=(rows, state, state, state, rows),
        in_specs=[SMEM] * 3 + [VMEM] * 5 + [HBM] * 2,
        out_specs=(VMEM,) * 5,
        scratch_shapes=[
            pltpu.VMEM((voxels, 2 * C), bf16),
            pltpu.VMEM((voxels, LANES), i32),
            pltpu.VMEM(w_up.shape, bf16),
            pltpu.VMEM(w_down.shape, bf16),
            pltpu.SemaphoreType.DMA((2,)),
        ],
        compiler_params=params(32),
        name="near",
    )(tags, before_tag, after_tag, tags.reshape(1, voxels), normed, w_heads, latent, w_out, *kept(w_up, w_down))


def finish_kernel(
    tag_ref, before_tag_ref, after_tag_ref, tag_row_ref, before_row_ref, after_row_ref,
    before_ref, after_ref, heads_ref, query_ref, value_ref, top_ref, sum_ref, near_out_ref, latent_ref,
    w_out_ref, up_hbm, down_hbm, out_ref,
    kv_ref, column_ref, row_ref, late_value_ref, late_sum_ref, late_top_ref, late_latent_ref, late_out_ref,
    up_ref, down_ref, sem
):
    up_copy = pltpu.make_async_copy(up_hbm, up_ref, sem.at[0])
    down_copy = pltpu.make_async_copy(down_hbm, down_ref, sem.at[1])
    up_copy.start()
    down_copy.start()
    voxels = query_ref.shape[0]
    blocks = voxels // BLOCK
    sizes = (2, blocks)
    column_ref[...] = column_of(tag_row_ref[...])
    start_tag, end_tag = tag_ref[0], tag_ref[voxels - 1]
    head, tail = rims(tag_ref, before_tag_ref, after_tag_ref)
    late = jnp.minimum(head + tail, blocks)
    before_count = i32(0)
    after_count = i32(0)
    for k in range(blocks):
        before_count += (before_tag_ref[k * BLOCK + BLOCK - 1] == start_tag).astype(i32)
        after_count += (after_tag_ref[k * BLOCK] == end_tag).astype(i32)
    before_count = jnp.where(head > 0, before_count, 0)
    after_count = jnp.where(tail > 0, after_count, 0)

    def project(side, source_ref, source_row_ref, n):
        size = n * BLOCK
        start = 0 if side else voxels - size
        kv_ref[side, :size] = dot(source_ref[start : start + size, :], heads_ref[:, C:]).astype(bf16)
        row_ref[side, :, :size] = source_row_ref[:, start : start + size]

    def span(count, action):
        for lower, n in zip((0,) + sizes, sizes):
            pl.when(jnp.logical_and(count > lower, count <= n))(lambda n=n: action(n))

    span(before_count, lambda n: project(0, before_ref, before_row_ref, n))
    span(after_count, lambda n: project(1, after_ref, after_row_ref, n))
    out_ref[...] = near_out_ref[...]

    def rows_of(k):
        b = jnp.where(k < head, k, k + blocks - late)
        return b, pl.ds(pl.multiple_of(b * BLOCK, BLOCK), BLOCK)

    def one_late(k, carry):
        b, rows = rows_of(k)
        put = pl.ds(pl.multiple_of(k * BLOCK, BLOCK), BLOCK)
        late_value_ref[put, :] = value_ref[rows, :]
        late_sum_ref[put, :] = sum_ref[rows, :]
        late_top_ref[put, :] = top_ref[rows, :]
        late_latent_ref[put, :] = latent_ref[rows, :]

        def one_side(side, carry):
            touched = jnp.where(side == 0, b < head, b >= blocks - tail)
            count = jnp.where(touched, jnp.where(side == 0, before_count, after_count), 0)

            def attend(n):
                size = n * BLOCK
                bias = bias_of(column_ref[rows, :], row_ref[side, :, :size])
                for p in range(PAIRS):
                    lanes = slice(p * LANES, (p + 1) * LANES)
                    old = late_top_ref[put, lanes]
                    score = scores_of(query_ref[rows, lanes], kv_ref[side, :size, lanes], bias)
                    known = jnp.concatenate([old[:, :1], old[:, HEAD : HEAD + 1]], axis=0)
                    highest = jnp.maximum(jnp.max(score, axis=1, keepdims=True), known)
                    result = weighted(score, highest, kv_ref[side, :size, C + p * LANES : C + (p + 1) * LANES])
                    top = by_half(jnp.broadcast_to(highest, (2 * BLOCK, LANES)))
                    fade = jnp.exp(old - top)
                    late_value_ref[put, lanes] = late_value_ref[put, lanes] * fade + by_half(result[:, :LANES])
                    late_sum_ref[put, lanes] = late_sum_ref[put, lanes] * fade + by_half(result[:, LANES:])
                    late_top_ref[put, lanes] = top

            span(count, attend)
            return carry

        return lax.fori_loop(0, 2, one_side, carry)

    lax.fori_loop(0, late, one_late, 0)
    up_copy.wait()
    down_copy.wait()

    def one_span(k, carry):
        rows = pl.ds(pl.multiple_of(k * SPAN, SPAN), SPAN)
        attended = (late_value_ref[rows, :] / late_sum_ref[rows, :]).astype(bf16)
        late_out_ref[rows, :] = feed_forward(attended, late_latent_ref[rows, :], w_out_ref, up_ref, down_ref)
        return carry

    lax.fori_loop(0, (late + 1) // 2, one_span, 0)

    def put_back(k, carry):
        _, rows = rows_of(k)
        out_ref[rows, :] = late_out_ref[pl.ds(pl.multiple_of(k * BLOCK, BLOCK), BLOCK), :]
        return carry

    lax.fori_loop(0, late, put_back, 0)


def finish(
    tags, before_tag, after_tag, before, after, w_heads, query, value, top, total, near_out, latent, w_out, w_up, w_down
):
    voxels = query.shape[0]
    row = lambda t: t.reshape(1, voxels)
    state = pltpu.VMEM((voxels, C), f32)
    return pl.pallas_call(
        finish_kernel,
        out_shape=jax.ShapeDtypeStruct((voxels, C), bf16),
        in_specs=[SMEM] * 3 + [VMEM] * 13 + [HBM] * 2,
        out_specs=VMEM,
        scratch_shapes=[
            pltpu.VMEM((2, voxels, 2 * C), bf16),
            pltpu.VMEM((voxels, LANES), i32),
            pltpu.VMEM((2, 1, voxels), i32),
            state,
            state,
            state,
            state,
            pltpu.VMEM((voxels, C), bf16),
            pltpu.VMEM(w_up.shape, bf16),
            pltpu.VMEM(w_down.shape, bf16),
            pltpu.SemaphoreType.DMA((2,)),
        ],
        compiler_params=params(36),
        name="finish",
    )(
        tags, before_tag, after_tag, row(tags), row(before_tag), row(after_tag), before, after, w_heads,
        query, value, top, total, near_out, latent, w_out, *kept(w_up, w_down)
    )


def local(features, w_embed, owner_device, voxel_slot, window_ids, w_heads, w_out, w_up, w_down):
    devices = lax.axis_size(AXES)
    patches = features.shape[0]
    voxels = window_ids.shape[0]
    capacity = max(2, 2 * patches // devices)
    buffer = dispatch(
        features, w_embed, owner_device.reshape(1, patches), voxel_slot.reshape(1, patches), devices, capacity
    )
    buffer, tags = lax.optimization_barrier((buffer, window_ids))
    arrived = lax.all_to_all(buffer, AXES, split_axis=0, concat_axis=0, tiled=True)
    before_tag = passed_along(tags, 1)
    after_tag = passed_along(tags, -1)
    arrived, before_tag, after_tag = lax.optimization_barrier((arrived, before_tag, after_tag))
    latent, normed = gather(arrived, voxels)
    before = passed_along(normed, 1)
    after = passed_along(normed, -1)
    query, value, top, total, out = near(
        tags, before_tag, after_tag, normed, w_heads, latent, w_out, w_up, w_down
    )
    return finish(
        tags, before_tag, after_tag, before, after, w_heads, query, value, top, total, out, latent, w_out, w_up, w_down
    )


def solution(mesh):
    rows = P(AXES, None)
    return jax.shard_map(
        local,
        mesh=mesh,
        in_specs=(rows, P(), rows, P(AXES), P(AXES), P(), P(), P(), P()),
        out_specs=rows,
        check_vma=False,
    )
```

```python
import jax
import jax.numpy as jnp
from jax import lax
from jax.experimental import pallas as pl
from jax.experimental.pallas import tpu as pltpu
from jax.sharding import PartitionSpec as P

C = 768
HEADS = 12
HEAD = C // HEADS
PAIRS = HEADS // 2
LANES = 128
CHUNKS = C // LANES
BLOCK = 128
epsilon = 1e-06
AXES = ("view", "vox")
f32 = jnp.float32
bf16 = jnp.bfloat16
i32 = jnp.int32
MASKED = -1e30


def passed_along(block, distance):
    devices = range(lax.axis_size(AXES))
    route = [(i - distance, i) for i in devices if i - distance in devices]
    return lax.ppermute(block, AXES, route)


def layer_norm(values):
    average = jnp.mean(values, axis=-1, keepdims=True)
    centered = values - average
    variance = jnp.mean(centered * centered, axis=-1, keepdims=True)
    return centered * lax.rsqrt(variance + epsilon)


def across(a, b):
    return lax.dot_general(a, b, (((1,), (1,)), ((), ())), preferred_element_type=f32)


def dot(a, b):
    return jnp.dot(a, b, preferred_element_type=f32)


def iota(shape, dim):
    return lax.broadcasted_iota(i32, shape, dim)


def params(mib):
    return pltpu.CompilerParams(vmem_limit_bytes=mib << 20)


GROUPS = 4


def dispatch_kernel(
    features_hbm, embed_hbm, owner_hbm, slot_hbm, out_hbm,
    features_ref, embed_ref, owner_ref, slot_ref, out_ref, payload_ref, position_ref, digits_ref, in_sem, out_sem
):
    copies = [
        pltpu.make_async_copy(source, target, in_sem.at[k])
        for k, (source, target) in enumerate(
            (
                (owner_hbm, owner_ref),
                (slot_hbm, slot_ref),
                (features_hbm, features_ref),
                (embed_hbm, embed_ref),
            )
        )
    ]
    for copy in copies:
        copy.start()
    patches = features_ref.shape[0]
    devices = digits_ref.shape[1]
    group = devices // GROUPS
    capacity = (out_ref.shape[1] - 8) // CHUNKS
    part = 256
    mine = lax.rem(lax.axis_index("vox"), LANES // capacity)
    earlier = jnp.where(iota((part, part), 0) < iota((part, part), 1), 1.0, 0.0).astype(bf16)
    copies[0].wait()
    copies[1].wait()
    owner = owner_ref[...]
    hits = jnp.where(iota((devices, patches), 0) == owner, 1.0, 0.0)
    running = jnp.zeros((devices, 1), f32)
    ranks = []
    for start in range(0, patches, part):
        here = hits[:, start : start + part]
        before = dot(here.astype(bf16), earlier) + running
        running = running + jnp.sum(here, axis=1, keepdims=True)
        ranks.append(jnp.sum(here * before, axis=0, keepdims=True))
    rank = jnp.concatenate(ranks, axis=1).astype(i32)
    position_ref[...] = owner * capacity + rank
    place = jnp.where(iota((LANES, patches), 0) == rank + capacity * mine, 1.0, 0.0).astype(bf16)
    code = slot_ref[...] + 1
    digits_ref[0] = across((hits * (code >> 4).astype(f32)).astype(bf16), place)
    digits_ref[1] = across((hits * (code & 15).astype(f32)).astype(bf16), place)
    copies[2].wait()
    copies[3].wait()
    payload_ref[...] = dot(features_ref[...], embed_ref[...]).astype(bf16)
    rows = group * capacity
    sends = []
    for g in range(GROUPS):
        here = slice(g * group, (g + 1) * group)
        chosen = jnp.where(iota((rows, patches), 0) + g * rows == position_ref[...], 1.0, 0.0)
        block = dot(chosen.astype(bf16), payload_ref[...]).astype(bf16)
        for c in range(CHUNKS):
            out_ref[here, c * capacity : (c + 1) * capacity, :] = block[
                :, c * LANES : (c + 1) * LANES
            ].reshape(group, capacity, LANES)
        high = jnp.broadcast_to(digits_ref[0, here, :][:, None, :], (group, 8, LANES))
        low = jnp.broadcast_to(digits_ref[1, here, :][:, None, :], (group, 8, LANES))
        out_ref[here, CHUNKS * capacity :, :] = jnp.where(
            iota((group, 8, LANES), 1) < 4, high, low
        ).astype(bf16)
        send = pltpu.make_async_copy(out_ref.at[here], out_hbm.at[here], out_sem.at[g])
        send.start()
        sends.append(send)
    for send in sends:
        send.wait()


def kept(*arrays):
    return [pltpu.with_memory_space_constraint(array, pltpu.HBM) for array in arrays]


HBM = pl.BlockSpec(memory_space=pltpu.HBM)
VMEM = pl.BlockSpec(memory_space=pltpu.VMEM)
SMEM = pl.BlockSpec(memory_space=pltpu.SMEM)


def dispatch(features, w_embed, owner, slot, devices, capacity):
    patches, width = features.shape
    tall = CHUNKS * capacity + 8
    return pl.pallas_call(
        dispatch_kernel,
        out_shape=pltpu.HBM((devices, tall, LANES), bf16),
        in_specs=[HBM] * 4,
        out_specs=HBM,
        scratch_shapes=[
            pltpu.VMEM((patches, width), bf16),
            pltpu.VMEM((width, C), bf16),
            pltpu.VMEM((1, patches), i32),
            pltpu.VMEM((1, patches), i32),
            pltpu.VMEM((devices, tall, LANES), bf16),
            pltpu.VMEM((patches, C), bf16),
            pltpu.VMEM((1, patches), i32),
            pltpu.VMEM((2, devices, LANES), f32),
            pltpu.SemaphoreType.DMA((4,)),
            pltpu.SemaphoreType.DMA((GROUPS,)),
        ],
        compiler_params=params(32),
        name="dispatch",
    )(*kept(features, w_embed, owner, slot))


def gather_kernel(arrived_hbm, latent_ref, low_ref, high_ref, arrived_ref, digit_ref, member_ref, sem):
    sources = arrived_ref.shape[0]
    capacity = arrived_ref.shape[1] // CHUNKS
    tall = CHUNKS * capacity
    voxels = latent_ref.shape[0]
    each = LANES // capacity
    digit_copy = pltpu.make_async_copy(arrived_hbm.at[:, tall:, :], digit_ref, sem.at[0])
    digit_copy.start()
    data_copy = pltpu.make_async_copy(arrived_hbm.at[:, :tall, :], arrived_ref, sem.at[1])
    data_copy.start()
    digit_copy.wait()
    digits = jnp.sum(digit_ref[...].astype(f32).reshape(sources // each, each, 8, LANES), axis=1)
    code = (digits[:, 0, :] * 16.0 + digits[:, 4, :]).astype(i32) - 1
    counted = jnp.zeros((voxels, LANES), f32)
    for g in range(sources // each):
        member = jnp.where(iota((voxels, LANES), 0) == code[g : g + 1], 1.0, 0.0)
        counted = counted + member
        member_ref[:, g * LANES : (g + 1) * LANES] = member.astype(bf16)
    counts = jnp.sum(counted, axis=1, keepdims=True)
    data_copy.wait()
    data = jnp.concatenate(
        [
            arrived_ref[:, c * capacity : (c + 1) * capacity, :].reshape(sources * capacity, LANES)
            for c in range(CHUNKS)
        ],
        axis=1,
    )
    latent = dot(member_ref[...], data) / jnp.maximum(counts, 1.0)
    latent_ref[...] = latent
    normed = layer_norm(latent).astype(bf16)
    low_ref[...] = normed[: voxels // 2]
    high_ref[...] = normed[voxels // 2 :]


def gather(arrived, voxels):
    sources, tall, _ = arrived.shape
    return pl.pallas_call(
        gather_kernel,
        out_shape=(
            jax.ShapeDtypeStruct((voxels, C), f32),
            jax.ShapeDtypeStruct((voxels // 2, C), bf16),
            jax.ShapeDtypeStruct((voxels // 2, C), bf16),
        ),
        in_specs=[HBM],
        out_specs=(VMEM, VMEM, VMEM),
        scratch_shapes=[
            pltpu.VMEM((sources, tall - 8, LANES), bf16),
            pltpu.VMEM((sources, 8, LANES), bf16),
            pltpu.VMEM((voxels, sources * ((tall - 8) // CHUNKS)), bf16),
            pltpu.SemaphoreType.DMA((2,)),
        ],
        compiler_params=params(24),
        name="gather",
    )(arrived)


def column_of(row):
    return jnp.broadcast_to(row, (LANES, row.shape[1])).T


def by_half(both):
    first, second = both[:BLOCK], both[BLOCK:]
    return jnp.where(iota(first.shape, 1) < HEAD, first, second)


def scores_of(query_pair, key_pair, bias):
    left = iota(query_pair.shape, 1) < HEAD
    none = jnp.zeros_like(query_pair)
    both = jnp.concatenate([jnp.where(left, query_pair, none), jnp.where(left, none, query_pair)], axis=0)
    return across(both, key_pair) + bias


def weighted(score, highest, value_pair):
    exponent = jnp.exp(score - highest).astype(bf16)
    wide = jnp.concatenate([value_pair, jnp.ones_like(value_pair)], axis=1)
    return dot(exponent, wide)


def bias_of(column, row):
    tiles = [
        jnp.where(column == row[:, k : k + LANES], 0.0, MASKED) for k in range(0, row.shape[1], LANES)
    ]
    bias = jnp.concatenate(tiles, axis=1)
    return jnp.concatenate([bias, bias], axis=0)


def rims(tag_ref, before_tag_ref, after_tag_ref):
    voxels = tag_ref.shape[0]
    blocks = voxels // BLOCK
    start_tag, end_tag = tag_ref[0], tag_ref[voxels - 1]
    head = i32(0)
    tail = i32(0)
    for k in range(blocks):
        head += (tag_ref[k * BLOCK] == start_tag).astype(i32)
        tail += (tag_ref[k * BLOCK + BLOCK - 1] == end_tag).astype(i32)
    ring = [lax.axis_index(axis) for axis in AXES]
    ends = [lax.axis_size(axis) - 1 for axis in AXES]
    first = jnp.logical_and(ring[0] == 0, ring[1] == 0)
    final = jnp.logical_and(ring[0] == ends[0], ring[1] == ends[1])
    head = jnp.where(jnp.logical_or(first, before_tag_ref[voxels - 1] != start_tag), 0, head)
    tail = jnp.where(jnp.logical_or(final, after_tag_ref[0] != end_tag), 0, tail)
    return head, tail


def feed_forward(attended, latent, w_out_ref, w_up_ref, w_down_ref):
    middle = latent + dot(attended, w_out_ref[...])
    normed = layer_norm(middle).astype(bf16)
    total = middle
    part = 512
    parts = range(0, w_up_ref.shape[1], part)
    raised = dot(normed, w_up_ref[:, :part])
    for k in parts:
        coming = dot(normed, w_up_ref[:, k + part : k + 2 * part]) if k + part in parts else None
        bent = jax.nn.gelu(raised, approximate=True).astype(bf16)
        total = total + dot(bent, w_down_ref[k : k + part, :])
        raised = coming
    return total.astype(bf16)


def settle(value, total, latent, out_ref, rows, w_out_ref, up_ref, down_ref):
    out_ref[rows, :] = feed_forward((value / total).astype(bf16), latent, w_out_ref, up_ref, down_ref)


def near_kernel(
    tag_ref, tag_row_ref, low_ref, high_ref, heads_ref, up_hbm, down_hbm,
    query_ref, value_ref, top_ref, sum_ref, up_ref, down_ref, kv_ref, column_ref, sem
):
    up_copy = pltpu.make_async_copy(up_hbm, up_ref, sem.at[0])
    down_copy = pltpu.make_async_copy(down_hbm, down_ref, sem.at[1])
    up_copy.start()
    down_copy.start()
    voxels = query_ref.shape[0]
    blocks = voxels // BLOCK
    normed = jnp.concatenate([low_ref[...], high_ref[...]], axis=0)
    query_ref[...] = dot(normed, heads_ref[:, :C]).astype(bf16) * jnp.asarray(HEAD**-0.5, bf16)
    kv_ref[...] = dot(normed, heads_ref[:, C:]).astype(bf16)
    column_ref[...] = column_of(tag_row_ref[...])

    def one_block(b, carry):
        rows = pl.ds(pl.multiple_of(b * BLOCK, BLOCK), BLOCK)
        first, last = tag_ref[b * BLOCK], tag_ref[b * BLOCK + BLOCK - 1]
        low = i32(0)
        high = i32(0)
        for k in range(blocks):
            low = low + (tag_ref[k * BLOCK + BLOCK - 1] < first).astype(i32)
            high = high + (tag_ref[k * BLOCK] <= last).astype(i32)
        short = high - low <= 2
        low = jnp.where(short, jnp.minimum(low, blocks - 2), 0)

        def attend(n):
            keys = pl.ds(pl.multiple_of(low * BLOCK, BLOCK), n * BLOCK)
            bias = bias_of(column_ref[rows, :], tag_row_ref[:, keys])
            for p in range(PAIRS):
                lanes = slice(p * LANES, (p + 1) * LANES)
                score = scores_of(query_ref[rows, lanes], kv_ref[keys, lanes], bias)
                highest = jnp.max(score, axis=1, keepdims=True)
                result = weighted(score, highest, kv_ref[keys, C + p * LANES : C + (p + 1) * LANES])
                value_ref[rows, lanes] = by_half(result[:, :LANES])
                sum_ref[rows, lanes] = by_half(result[:, LANES:])
                top_ref[rows, lanes] = by_half(jnp.broadcast_to(highest, (2 * BLOCK, LANES)))

        pl.when(short)(lambda: attend(2))
        pl.when(jnp.logical_not(short))(lambda: attend(blocks))
        return carry

    lax.fori_loop(0, blocks, one_block, 0)
    up_copy.wait()
    down_copy.wait()


def near(tags, low, high, w_heads, w_up, w_down):
    voxels = tags.shape[0]
    state = jax.ShapeDtypeStruct((voxels, C), f32)
    return pl.pallas_call(
        near_kernel,
        out_shape=(
            jax.ShapeDtypeStruct((voxels, C), bf16),
            state,
            state,
            state,
            pltpu.VMEM(w_up.shape, bf16),
            pltpu.VMEM(w_down.shape, bf16),
        ),
        in_specs=[SMEM] + [VMEM] * 4 + [HBM] * 2,
        out_specs=(VMEM,) * 6,
        scratch_shapes=[
            pltpu.VMEM((voxels, 2 * C), bf16),
            pltpu.VMEM((voxels, LANES), i32),
            pltpu.SemaphoreType.DMA((2,)),
        ],
        compiler_params=params(20),
        name="near",
    )(tags, tags.reshape(1, voxels), low, high, w_heads, *kept(w_up, w_down))


def extend(query_ref, rows, kv_ref, side, bias, new, put):
    for p in range(PAIRS):
        lanes = slice(p * LANES, (p + 1) * LANES)
        values = slice(C + p * LANES, C + (p + 1) * LANES)
        known = new[2][put, lanes]
        score = scores_of(query_ref[rows, lanes], kv_ref[side, :, lanes], bias)
        each = jnp.concatenate([known[:, :1], known[:, HEAD : HEAD + 1]], axis=0)
        highest = jnp.maximum(jnp.max(score, axis=1, keepdims=True), each)
        result = weighted(score, highest, kv_ref[side, :, values])
        top = by_half(jnp.broadcast_to(highest, (2 * BLOCK, LANES)))
        fade = jnp.exp(known - top)
        new[0][put, lanes] = new[0][put, lanes] * fade + by_half(result[:, :LANES])
        new[1][put, lanes] = new[1][put, lanes] * fade + by_half(result[:, LANES:])
        new[2][put, lanes] = top


def late_rows(k, head, late, blocks):
    b = jnp.where(k < head, k, k + blocks - late)
    put = pl.ds(pl.multiple_of(k * BLOCK, BLOCK), BLOCK)
    return b, pl.ds(pl.multiple_of(b * BLOCK, BLOCK), BLOCK), put


def middle_kernel(
    tag_ref, before_tag_ref, after_tag_ref, tag_row_ref, before_row_ref, after_row_ref,
    before_ref, after_ref, heads_ref, query_ref, value_ref, sum_ref, top_ref, latent_ref, w_out_ref, up_ref, down_ref,
    late_value_ref, late_sum_ref, late_top_ref, late_latent_ref, out_ref, kv_ref, column_ref
):
    voxels = query_ref.shape[0]
    blocks = voxels // BLOCK
    half = voxels // 2
    head, tail = rims(tag_ref, before_tag_ref, after_tag_ref)
    late = jnp.minimum(head + tail, blocks)

    @pl.when(late > 0)
    def _():
        column_ref[...] = column_of(tag_row_ref[...])
        both = jnp.concatenate([before_ref[...], after_ref[...]], axis=0)
        kv_ref[...] = dot(both, heads_ref[:, C:]).astype(bf16).reshape(2, half, 2 * C)

    def one_late(k, carry):
        b, rows, put = late_rows(k, head, late, blocks)
        new = (late_value_ref, late_sum_ref, late_top_ref)
        for source, target in zip((value_ref, sum_ref, top_ref, latent_ref), new + (late_latent_ref,)):
            target[put, :] = source[rows, :]

        def one_side(side, carry):
            @pl.when(jnp.where(side == 0, b < head, b >= blocks - tail))
            def _():
                keys = jnp.where(side == 0, before_row_ref[:, half:], after_row_ref[:, :half])
                extend(query_ref, rows, kv_ref, side, bias_of(column_ref[rows, :], keys), new, put)

            return carry

        return lax.fori_loop(0, 2, one_side, carry)

    lax.fori_loop(0, late, one_late, 0)
    early = blocks - late
    weights = (w_out_ref, up_ref, down_ref)

    @pl.when(jnp.logical_and(early > 0, early <= 2))
    def _():
        start = jnp.minimum(head, blocks - 2) * BLOCK
        rows = pl.ds(pl.multiple_of(start, BLOCK), half)
        settle(value_ref[rows, :], sum_ref[rows, :], latent_ref[rows, :], out_ref, rows, *weights)

    @pl.when(early > 2)
    def _():
        settle(value_ref[...], sum_ref[...], latent_ref[...], out_ref, slice(0, voxels), *weights)


def middle(tags, before_tag, after_tag, before, after, w_heads, query, value, total, top, latent, w_out, w_up, w_down):
    voxels = query.shape[0]
    row = lambda t: t.reshape(1, voxels)
    state = jax.ShapeDtypeStruct((voxels, C), f32)
    return pl.pallas_call(
        middle_kernel,
        out_shape=(state, state, state, state, jax.ShapeDtypeStruct((voxels, C), bf16)),
        in_specs=[SMEM] * 3 + [VMEM] * 14,
        out_specs=(VMEM,) * 5,
        scratch_shapes=[
            pltpu.VMEM((2, voxels // 2, 2 * C), bf16),
            pltpu.VMEM((voxels, LANES), i32),
        ],
        compiler_params=params(20),
        name="middle",
    )(
        tags, before_tag, after_tag, row(tags), row(before_tag), row(after_tag), before, after, w_heads,
        query, value, total, top, latent, w_out, w_up, w_down
    )


def finish_kernel(
    tag_ref, before_tag_ref, after_tag_ref, tag_row_ref, before_row_ref, after_row_ref,
    before_ref, after_ref, heads_ref, query_ref, late_value_ref, late_sum_ref, late_top_ref, late_latent_ref,
    early_ref, w_out_ref, up_ref, down_ref, out_ref,
    kv_ref, column_ref, value_ref, sum_ref, top_ref, late_out_ref
):
    voxels = query_ref.shape[0]
    blocks = voxels // BLOCK
    half = voxels // 2
    head, tail = rims(tag_ref, before_tag_ref, after_tag_ref)
    late = jnp.minimum(head + tail, blocks)
    far_before = jnp.logical_and(head > 0, before_tag_ref[half - 1] == tag_ref[0])
    far_after = jnp.logical_and(tail > 0, after_tag_ref[half] == tag_ref[voxels - 1])
    far = jnp.logical_or(far_before, far_after)
    out_ref[...] = early_ref[...]
    weights = (w_out_ref, up_ref, down_ref)
    new = (value_ref, sum_ref, top_ref)

    @pl.when(far)
    def _():
        column_ref[...] = column_of(tag_row_ref[...])

    @pl.when(far_before)
    def _():
        kv_ref[0] = dot(before_ref[...], heads_ref[:, C:]).astype(bf16)

    @pl.when(far_after)
    def _():
        kv_ref[1] = dot(after_ref[...], heads_ref[:, C:]).astype(bf16)

    def one_late(k, carry):
        b, rows, put = late_rows(k, head, late, blocks)
        for source, target in zip((late_value_ref, late_sum_ref, late_top_ref), new):
            target[put, :] = source[put, :]

        def one_side(side, carry):
            touched = jnp.where(
                side == 0,
                jnp.logical_and(far_before, b < head),
                jnp.logical_and(far_after, b >= blocks - tail),
            )

            @pl.when(touched)
            def _():
                keys = jnp.where(side == 0, before_row_ref[:, :half], after_row_ref[:, half:])
                extend(query_ref, rows, kv_ref, side, bias_of(column_ref[rows, :], keys), new, put)

            return carry

        return lax.fori_loop(0, 2, one_side, carry)

    lax.fori_loop(0, late, one_late, 0)

    def put_back(k, carry):
        _, rows, put = late_rows(k, head, late, blocks)
        out_ref[rows, :] = late_out_ref[put, :]
        return carry

    @pl.when(jnp.logical_and(late > 0, late <= 2))
    def _():
        rows = slice(0, half)
        settle(value_ref[rows, :], sum_ref[rows, :], late_latent_ref[rows, :], late_out_ref, rows, *weights)

    @pl.when(late > 2)
    def _():
        settle(value_ref[...], sum_ref[...], late_latent_ref[...], late_out_ref, slice(0, voxels), *weights)

    lax.fori_loop(0, late, put_back, 0)


def finish(
    tags, before_tag, after_tag, before, after, w_heads, query, late_value, late_sum, late_top, late_latent, early,
    w_out, w_up, w_down
):
    voxels = query.shape[0]
    row = lambda t: t.reshape(1, voxels)
    state = pltpu.VMEM((voxels, C), f32)
    return pl.pallas_call(
        finish_kernel,
        out_shape=jax.ShapeDtypeStruct((voxels, C), bf16),
        in_specs=[SMEM] * 3 + [VMEM] * 15,
        out_specs=VMEM,
        scratch_shapes=[
            pltpu.VMEM((2, voxels // 2, 2 * C), bf16),
            pltpu.VMEM((voxels, LANES), i32),
            state,
            state,
            state,
            pltpu.VMEM((voxels, C), bf16),
        ],
        compiler_params=params(26),
        name="finish",
    )(
        tags, before_tag, after_tag, row(tags), row(before_tag), row(after_tag), before, after, w_heads,
        query, late_value, late_sum, late_top, late_latent, early, w_out, w_up, w_down
    )


def local(features, w_embed, owner_device, voxel_slot, window_ids, w_heads, w_out, w_up, w_down):
    devices = lax.axis_size(AXES)
    patches = features.shape[0]
    voxels = window_ids.shape[0]
    capacity = max(2, 2 * patches // devices)
    buffer = dispatch(
        features, w_embed, owner_device.reshape(1, patches), voxel_slot.reshape(1, patches), devices, capacity
    )
    buffer, tags = lax.optimization_barrier((buffer, window_ids))
    arrived = lax.all_to_all(buffer, AXES, split_axis=0, concat_axis=0, tiled=True)
    before_tag = passed_along(tags, 1)
    after_tag = passed_along(tags, -1)
    arrived, before_tag, after_tag = lax.optimization_barrier((arrived, before_tag, after_tag))
    latent, low, high = gather(arrived, voxels)
    before_near = passed_along(high, 1)
    after_near = passed_along(low, -1)
    before_far = passed_along(low, 1)
    after_far = passed_along(high, -1)
    query, value, top, total, up, down = near(tags, low, high, w_heads, w_up, w_down)
    places = (tags, before_tag, after_tag)
    *late, early = middle(
        *places, before_near, after_near, w_heads, query, value, total, top, latent, w_out, up, down
    )
    return finish(*places, before_far, after_far, w_heads, query, *late, early, w_out, up, down)


def solution(mesh):
    rows = P(AXES, None)
    return jax.shard_map(
        local,
        mesh=mesh,
        in_specs=(rows, P(), rows, P(AXES), P(AXES), P(), P(), P(), P()),
        out_specs=rows,
        check_vma=False,
    )
```

```python
import jax
import jax.numpy as jnp
from jax import lax
from jax.experimental import pallas as pl
from jax.experimental.pallas import tpu as pltpu
from jax.sharding import PartitionSpec as P

C = 768
HEADS = 12
HEAD = C // HEADS
PAIRS = HEADS // 2
LANES = 128
CHUNKS = C // LANES
BLOCK = 128
epsilon = 1e-06
AXES = ("view", "vox")
f32 = jnp.float32
bf16 = jnp.bfloat16
i32 = jnp.int32
MASKED = -1e30


def passed_along(block, distance):
    devices = range(lax.axis_size(AXES))
    route = [(i - distance, i) for i in devices if i - distance in devices]
    return lax.ppermute(block, AXES, route)


def layer_norm(values):
    average = jnp.mean(values, axis=-1, keepdims=True)
    centered = values - average
    variance = jnp.mean(centered * centered, axis=-1, keepdims=True)
    return centered * lax.rsqrt(variance + epsilon)


def across(a, b):
    return lax.dot_general(a, b, (((1,), (1,)), ((), ())), preferred_element_type=f32)


def dot(a, b):
    return jnp.dot(a, b, preferred_element_type=f32)


def iota(shape, dim):
    return lax.broadcasted_iota(i32, shape, dim)


def params(mib):
    return pltpu.CompilerParams(vmem_limit_bytes=mib << 20)


GROUPS = 4


def dispatch_kernel(
    features_hbm, embed_hbm, owner_hbm, slot_hbm, out_hbm,
    features_ref, embed_ref, owner_ref, slot_ref, out_ref, payload_ref, position_ref, digits_ref, in_sem, out_sem
):
    copies = [
        pltpu.make_async_copy(source, target, in_sem.at[k])
        for k, (source, target) in enumerate(
            (
                (owner_hbm, owner_ref),
                (slot_hbm, slot_ref),
                (features_hbm, features_ref),
                (embed_hbm, embed_ref),
            )
        )
    ]
    for copy in copies:
        copy.start()
    patches = features_ref.shape[0]
    devices = digits_ref.shape[1]
    group = devices // GROUPS
    capacity = (out_ref.shape[1] - 8) // CHUNKS
    part = 256
    mine = lax.rem(lax.axis_index("vox"), LANES // capacity)
    earlier = jnp.where(iota((part, part), 0) < iota((part, part), 1), 1.0, 0.0).astype(bf16)
    copies[0].wait()
    copies[1].wait()
    owner = owner_ref[...]
    hits = jnp.where(iota((devices, patches), 0) == owner, 1.0, 0.0)
    running = jnp.zeros((devices, 1), f32)
    ranks = []
    for start in range(0, patches, part):
        here = hits[:, start : start + part]
        before = dot(here.astype(bf16), earlier) + running
        running = running + jnp.sum(here, axis=1, keepdims=True)
        ranks.append(jnp.sum(here * before, axis=0, keepdims=True))
    rank = jnp.concatenate(ranks, axis=1).astype(i32)
    position_ref[...] = owner * capacity + rank
    place = jnp.where(iota((LANES, patches), 0) == rank + capacity * mine, 1.0, 0.0).astype(bf16)
    code = slot_ref[...] + 1
    digits_ref[0] = across((hits * (code >> 4).astype(f32)).astype(bf16), place)
    digits_ref[1] = across((hits * (code & 15).astype(f32)).astype(bf16), place)
    copies[2].wait()
    copies[3].wait()
    payload_ref[...] = dot(features_ref[...], embed_ref[...]).astype(bf16)
    rows = group * capacity
    sends = []
    for g in range(GROUPS):
        here = slice(g * group, (g + 1) * group)
        chosen = jnp.where(iota((rows, patches), 0) + g * rows == position_ref[...], 1.0, 0.0)
        block = dot(chosen.astype(bf16), payload_ref[...]).astype(bf16)
        for c in range(CHUNKS):
            out_ref[here, c * capacity : (c + 1) * capacity, :] = block[
                :, c * LANES : (c + 1) * LANES
            ].reshape(group, capacity, LANES)
        high = jnp.broadcast_to(digits_ref[0, here, :][:, None, :], (group, 8, LANES))
        low = jnp.broadcast_to(digits_ref[1, here, :][:, None, :], (group, 8, LANES))
        out_ref[here, CHUNKS * capacity :, :] = jnp.where(
            iota((group, 8, LANES), 1) < 4, high, low
        ).astype(bf16)
        send = pltpu.make_async_copy(out_ref.at[here], out_hbm.at[here], out_sem.at[g])
        send.start()
        sends.append(send)
    for send in sends:
        send.wait()


def kept(*arrays):
    return [pltpu.with_memory_space_constraint(array, pltpu.HBM) for array in arrays]


HBM = pl.BlockSpec(memory_space=pltpu.HBM)
VMEM = pl.BlockSpec(memory_space=pltpu.VMEM)
SMEM = pl.BlockSpec(memory_space=pltpu.SMEM)


def dispatch(features, w_embed, owner, slot, devices, capacity):
    patches, width = features.shape
    tall = CHUNKS * capacity + 8
    return pl.pallas_call(
        dispatch_kernel,
        out_shape=pltpu.HBM((devices, tall, LANES), bf16),
        in_specs=[HBM] * 4,
        out_specs=HBM,
        scratch_shapes=[
            pltpu.VMEM((patches, width), bf16),
            pltpu.VMEM((width, C), bf16),
            pltpu.VMEM((1, patches), i32),
            pltpu.VMEM((1, patches), i32),
            pltpu.VMEM((devices, tall, LANES), bf16),
            pltpu.VMEM((patches, C), bf16),
            pltpu.VMEM((1, patches), i32),
            pltpu.VMEM((2, devices, LANES), f32),
            pltpu.SemaphoreType.DMA((4,)),
            pltpu.SemaphoreType.DMA((GROUPS,)),
        ],
        compiler_params=params(32),
        name="dispatch",
    )(*kept(features, w_embed, owner, slot))


def gather_kernel(arrived_hbm, latent_ref, low_ref, high_ref, arrived_ref, digit_ref, member_ref, sem):
    sources = arrived_ref.shape[0]
    capacity = arrived_ref.shape[1] // CHUNKS
    tall = CHUNKS * capacity
    voxels = latent_ref.shape[0]
    each = LANES // capacity
    digit_copy = pltpu.make_async_copy(arrived_hbm.at[:, tall:, :], digit_ref, sem.at[0])
    digit_copy.start()
    data_copy = pltpu.make_async_copy(arrived_hbm.at[:, :tall, :], arrived_ref, sem.at[1])
    data_copy.start()
    digit_copy.wait()
    digits = jnp.sum(digit_ref[...].astype(f32).reshape(sources // each, each, 8, LANES), axis=1)
    code = (digits[:, 0, :] * 16.0 + digits[:, 4, :]).astype(i32) - 1
    counted = jnp.zeros((voxels, LANES), f32)
    for g in range(sources // each):
        member = jnp.where(iota((voxels, LANES), 0) == code[g : g + 1], 1.0, 0.0)
        counted = counted + member
        member_ref[:, g * LANES : (g + 1) * LANES] = member.astype(bf16)
    counts = jnp.sum(counted, axis=1, keepdims=True)
    data_copy.wait()
    data = jnp.concatenate(
        [
            arrived_ref[:, c * capacity : (c + 1) * capacity, :].reshape(sources * capacity, LANES)
            for c in range(CHUNKS)
        ],
        axis=1,
    )
    latent = dot(member_ref[...], data) / jnp.maximum(counts, 1.0)
    latent_ref[...] = latent
    normed = layer_norm(latent).astype(bf16)
    low_ref[...] = normed[: voxels // 2]
    high_ref[...] = normed[voxels // 2 :]


def gather(arrived, voxels):
    sources, tall, _ = arrived.shape
    return pl.pallas_call(
        gather_kernel,
        out_shape=(
            jax.ShapeDtypeStruct((voxels, C), f32),
            jax.ShapeDtypeStruct((voxels // 2, C), bf16),
            jax.ShapeDtypeStruct((voxels // 2, C), bf16),
        ),
        in_specs=[HBM],
        out_specs=(VMEM, VMEM, VMEM),
        scratch_shapes=[
            pltpu.VMEM((sources, tall - 8, LANES), bf16),
            pltpu.VMEM((sources, 8, LANES), bf16),
            pltpu.VMEM((voxels, sources * ((tall - 8) // CHUNKS)), bf16),
            pltpu.SemaphoreType.DMA((2,)),
        ],
        compiler_params=params(24),
        name="gather",
    )(arrived)


def column_of(row):
    return jnp.broadcast_to(row, (LANES, row.shape[1])).T


def by_half(both):
    first, second = both[:BLOCK], both[BLOCK:]
    return jnp.where(iota(first.shape, 1) < HEAD, first, second)


def scores_of(query_pair, key_pair, bias):
    left = iota(query_pair.shape, 1) < HEAD
    none = jnp.zeros_like(query_pair)
    both = jnp.concatenate([jnp.where(left, query_pair, none), jnp.where(left, none, query_pair)], axis=0)
    return across(both, key_pair) + bias


def weighted(score, highest, value_pair):
    exponent = jnp.exp(score - highest).astype(bf16)
    wide = jnp.concatenate([value_pair, jnp.ones_like(value_pair)], axis=1)
    return dot(exponent, wide)


def bias_of(column, row):
    tiles = [
        jnp.where(column == row[:, k : k + LANES], 0.0, MASKED) for k in range(0, row.shape[1], LANES)
    ]
    bias = jnp.concatenate(tiles, axis=1)
    return jnp.concatenate([bias, bias], axis=0)


def rims(tag_ref, before_tag_ref, after_tag_ref):
    voxels = tag_ref.shape[0]
    blocks = voxels // BLOCK
    start_tag, end_tag = tag_ref[0], tag_ref[voxels - 1]
    head = i32(0)
    tail = i32(0)
    for k in range(blocks):
        head += (tag_ref[k * BLOCK] == start_tag).astype(i32)
        tail += (tag_ref[k * BLOCK + BLOCK - 1] == end_tag).astype(i32)
    ring = [lax.axis_index(axis) for axis in AXES]
    ends = [lax.axis_size(axis) - 1 for axis in AXES]
    first = jnp.logical_and(ring[0] == 0, ring[1] == 0)
    final = jnp.logical_and(ring[0] == ends[0], ring[1] == ends[1])
    head = jnp.where(jnp.logical_or(first, before_tag_ref[voxels - 1] != start_tag), 0, head)
    tail = jnp.where(jnp.logical_or(final, after_tag_ref[0] != end_tag), 0, tail)
    return head, tail


def feed_forward(attended, latent, w_out_ref, w_up_ref, w_down_ref):
    middle = latent + dot(attended, w_out_ref[...])
    normed = layer_norm(middle).astype(bf16)
    total = middle
    part = 512
    parts = range(0, w_up_ref.shape[1], part)
    raised = dot(normed, w_up_ref[:, :part])
    for k in parts:
        coming = dot(normed, w_up_ref[:, k + part : k + 2 * part]) if k + part in parts else None
        bent = jax.nn.gelu(raised, approximate=True).astype(bf16)
        total = total + dot(bent, w_down_ref[k : k + part, :])
        raised = coming
    return total.astype(bf16)


PIECES = 4


def near_kernel(
    tag_ref, tag_row_ref, low_ref, high_ref, heads_ref, up_hbm, down_hbm,
    query_ref, value_ref, top_ref, sum_ref, up_ref, down_ref, kv_ref, column_ref, sem
):
    fetches = []
    for k, (source, target) in enumerate(((up_hbm, up_ref), (down_hbm, down_ref))):
        each = source.shape[0] // PIECES
        for j in range(PIECES):
            piece = slice(j * each, (j + 1) * each)
            fetches.append(pltpu.make_async_copy(source.at[piece], target.at[piece], sem.at[k, j]))
    for copy in fetches:
        copy.start()
    voxels = query_ref.shape[0]
    blocks = voxels // BLOCK
    normed = jnp.concatenate([low_ref[...], high_ref[...]], axis=0)
    query_ref[...] = dot(normed, heads_ref[:, :C]).astype(bf16) * jnp.asarray(HEAD**-0.5, bf16)
    kv_ref[...] = dot(normed, heads_ref[:, C:]).astype(bf16)
    column_ref[...] = column_of(tag_row_ref[...])

    def one_block(b, carry):
        rows = pl.ds(pl.multiple_of(b * BLOCK, BLOCK), BLOCK)
        first, last = tag_ref[b * BLOCK], tag_ref[b * BLOCK + BLOCK - 1]
        low = i32(0)
        high = i32(0)
        for k in range(blocks):
            low = low + (tag_ref[k * BLOCK + BLOCK - 1] < first).astype(i32)
            high = high + (tag_ref[k * BLOCK] <= last).astype(i32)
        short = high - low <= 2
        low = jnp.where(short, jnp.minimum(low, blocks - 2), 0)

        def attend(n):
            keys = pl.ds(pl.multiple_of(low * BLOCK, BLOCK), n * BLOCK)
            bias = bias_of(column_ref[rows, :], tag_row_ref[:, keys])
            for p in range(PAIRS):
                lanes = slice(p * LANES, (p + 1) * LANES)
                score = scores_of(query_ref[rows, lanes], kv_ref[keys, lanes], bias)
                highest = jnp.max(score, axis=1, keepdims=True)
                result = weighted(score, highest, kv_ref[keys, C + p * LANES : C + (p + 1) * LANES])
                value_ref[rows, lanes] = by_half(result[:, :LANES])
                sum_ref[rows, lanes] = by_half(result[:, LANES:])
                top_ref[rows, lanes] = by_half(jnp.broadcast_to(highest, (2 * BLOCK, LANES)))

        pl.when(short)(lambda: attend(2))
        pl.when(jnp.logical_not(short))(lambda: attend(blocks))
        return carry

    lax.fori_loop(0, blocks, one_block, 0)
    for copy in fetches:
        copy.wait()


def near(tags, low, high, w_heads, w_up, w_down):
    voxels = tags.shape[0]
    state = jax.ShapeDtypeStruct((voxels, C), f32)
    return pl.pallas_call(
        near_kernel,
        out_shape=(
            jax.ShapeDtypeStruct((voxels, C), bf16),
            state,
            state,
            state,
            pltpu.VMEM(w_up.shape, bf16),
            pltpu.VMEM(w_down.shape, bf16),
        ),
        in_specs=[SMEM] + [VMEM] * 4 + [HBM] * 2,
        out_specs=(VMEM,) * 6,
        scratch_shapes=[
            pltpu.VMEM((voxels, 2 * C), bf16),
            pltpu.VMEM((voxels, LANES), i32),
            pltpu.SemaphoreType.DMA((2, PIECES)),
        ],
        compiler_params=params(20),
        name="near",
    )(tags, tags.reshape(1, voxels), low, high, w_heads, *kept(w_up, w_down))


def extend(query_ref, rows, kv_ref, side, bias, old, at, new, put):
    for p in range(PAIRS):
        lanes = slice(p * LANES, (p + 1) * LANES)
        values = slice(C + p * LANES, C + (p + 1) * LANES)
        score = scores_of(query_ref[rows, lanes], kv_ref[side, :, lanes], bias)
        highest = jnp.max(score, axis=1, keepdims=True)
        result = weighted(score, highest, kv_ref[side, :, values])
        here = by_half(jnp.broadcast_to(highest, (2 * BLOCK, LANES)))
        known = old[2][at, lanes]
        top = jnp.maximum(known, here)
        fade, grow = jnp.exp(known - top), jnp.exp(here - top)
        new[0][put, lanes] = old[0][at, lanes] * fade + by_half(result[:, :LANES]) * grow
        new[1][put, lanes] = old[1][at, lanes] * fade + by_half(result[:, LANES:]) * grow
        new[2][put, lanes] = top


def late_rows(k, head, late, blocks):
    b = jnp.where(k < head, k, k + blocks - late)
    put = pl.ds(pl.multiple_of(k * BLOCK, BLOCK), BLOCK)
    return b, pl.ds(pl.multiple_of(b * BLOCK, BLOCK), BLOCK), put


def project(need_before, need_after, before_ref, after_ref, heads_ref, kv_ref):
    half = before_ref.shape[0]

    @pl.when(jnp.logical_and(need_before, need_after))
    def _():
        both = jnp.concatenate([before_ref[...], after_ref[...]], axis=0)
        kv_ref[...] = dot(both, heads_ref[:, C:]).astype(bf16).reshape(2, half, 2 * C)

    @pl.when(need_before != need_after)
    def _():
        one = jnp.where(need_before, before_ref[...], after_ref[...])
        kv_ref[jnp.where(need_before, 0, 1)] = dot(one, heads_ref[:, C:]).astype(bf16)


def both_sides(touched, rows, keys, query_ref, kv_ref, column_ref, old, at, new, put):
    def one_side(side, carry):
        now = jnp.where(side == 0, touched[0], touched[1])
        again = jnp.logical_and(side == 1, touched[0])
        bias = lambda: bias_of(column_ref[rows, :], jnp.where(side == 0, keys[0], keys[1]))

        @pl.when(jnp.logical_and(now, jnp.logical_not(again)))
        def _():
            extend(query_ref, rows, kv_ref, side, bias(), old, at, new, put)

        @pl.when(jnp.logical_and(now, again))
        def _():
            extend(query_ref, rows, kv_ref, side, bias(), new, put, new, put)

        return carry

    lax.fori_loop(0, 2, one_side, 0)


def middle_kernel(
    tag_ref, before_tag_ref, after_tag_ref, tag_row_ref, before_row_ref, after_row_ref,
    before_ref, after_ref, heads_ref, query_ref, value_ref, sum_ref, top_ref, latent_ref, w_out_ref, up_ref, down_ref,
    late_value_ref, late_sum_ref, late_top_ref, out_ref, kv_ref, column_ref
):
    voxels = query_ref.shape[0]
    blocks = voxels // BLOCK
    half = voxels // 2
    head, tail = rims(tag_ref, before_tag_ref, after_tag_ref)
    late = jnp.minimum(head + tail, blocks)

    @pl.when(late > 0)
    def _():
        column_ref[...] = column_of(tag_row_ref[...])

    project(head > 0, tail > 0, before_ref, after_ref, heads_ref, kv_ref)

    def one_late(k, carry):
        b, rows, put = late_rows(k, head, late, blocks)
        touched = (b < head, b >= blocks - tail)
        keys = (before_row_ref[:, half:], after_row_ref[:, :half])
        old, new = (value_ref, sum_ref, top_ref), (late_value_ref, late_sum_ref, late_top_ref)
        both_sides(touched, rows, keys, query_ref, kv_ref, column_ref, old, rows, new, put)
        return carry

    lax.fori_loop(0, late, one_late, 0)
    early = blocks - late

    def settle(rows):
        attended = (value_ref[rows, :] / sum_ref[rows, :]).astype(bf16)
        out_ref[rows, :] = feed_forward(attended, latent_ref[rows, :], w_out_ref, up_ref, down_ref)

    @pl.when(jnp.logical_and(early > 0, early <= 2))
    def _():
        start = jnp.minimum(head, blocks - 2) * BLOCK
        settle(pl.ds(pl.multiple_of(start, BLOCK), half))

    @pl.when(early > 2)
    def _():
        settle(slice(0, voxels))


def middle(tags, before_tag, after_tag, before, after, w_heads, query, value, total, top, latent, w_out, w_up, w_down):
    voxels = query.shape[0]
    row = lambda t: t.reshape(1, voxels)
    state = jax.ShapeDtypeStruct((voxels, C), f32)
    return pl.pallas_call(
        middle_kernel,
        out_shape=(state, state, state, jax.ShapeDtypeStruct((voxels, C), bf16)),
        in_specs=[SMEM] * 3 + [VMEM] * 14,
        out_specs=(VMEM,) * 4,
        scratch_shapes=[
            pltpu.VMEM((2, voxels // 2, 2 * C), bf16),
            pltpu.VMEM((voxels, LANES), i32),
        ],
        compiler_params=params(20),
        name="middle",
    )(
        tags, before_tag, after_tag, row(tags), row(before_tag), row(after_tag), before, after, w_heads,
        query, value, total, top, latent, w_out, w_up, w_down
    )


def finish_kernel(
    tag_ref, before_tag_ref, after_tag_ref, tag_row_ref, before_row_ref, after_row_ref,
    before_ref, after_ref, heads_ref, query_ref, late_value_ref, late_sum_ref, late_top_ref,
    early_ref, latent_ref, w_out_ref, up_ref, down_ref, out_ref,
    kv_ref, column_ref, value_ref, sum_ref, top_ref, attended_ref, late_latent_ref, late_out_ref
):
    voxels = query_ref.shape[0]
    blocks = voxels // BLOCK
    half = voxels // 2
    head, tail = rims(tag_ref, before_tag_ref, after_tag_ref)
    late = jnp.minimum(head + tail, blocks)
    far_before = jnp.logical_and(head > 0, before_tag_ref[half - 1] == tag_ref[0])
    far_after = jnp.logical_and(tail > 0, after_tag_ref[half] == tag_ref[voxels - 1])

    @pl.when(jnp.logical_or(far_before, far_after))
    def _():
        column_ref[...] = column_of(tag_row_ref[...])

    project(far_before, far_after, before_ref, after_ref, heads_ref, kv_ref)

    def one_late(k, carry):
        b, rows, put = late_rows(k, head, late, blocks)
        touched = (jnp.logical_and(far_before, b < head), jnp.logical_and(far_after, b >= blocks - tail))
        keys = (before_row_ref[:, :half], after_row_ref[:, half:])
        old, new = (late_value_ref, late_sum_ref, late_top_ref), (value_ref, sum_ref, top_ref)
        both_sides(touched, rows, keys, query_ref, kv_ref, column_ref, old, put, new, put)
        changed = jnp.logical_or(*touched)

        @pl.when(changed)
        def _():
            attended_ref[put, :] = (value_ref[put, :] / sum_ref[put, :]).astype(bf16)

        @pl.when(jnp.logical_not(changed))
        def _():
            attended_ref[put, :] = (late_value_ref[put, :] / late_sum_ref[put, :]).astype(bf16)

        late_latent_ref[put, :] = latent_ref[rows, :]
        return carry

    lax.fori_loop(0, late, one_late, 0)
    out_ref[...] = early_ref[...]

    def settle(rows):
        late_out_ref[rows, :] = feed_forward(
            attended_ref[rows, :], late_latent_ref[rows, :], w_out_ref, up_ref, down_ref
        )

    @pl.when(jnp.logical_and(late > 0, late <= 2))
    def _():
        settle(slice(0, half))

    @pl.when(late > 2)
    def _():
        settle(slice(0, voxels))

    def put_back(k, carry):
        _, rows, put = late_rows(k, head, late, blocks)
        out_ref[rows, :] = late_out_ref[put, :]
        return carry

    lax.fori_loop(0, late, put_back, 0)


def finish(
    tags, before_tag, after_tag, before, after, w_heads, query, late_value, late_sum, late_top, early, latent,
    w_out, w_up, w_down
):
    voxels = query.shape[0]
    row = lambda t: t.reshape(1, voxels)
    state = pltpu.VMEM((voxels, C), f32)
    return pl.pallas_call(
        finish_kernel,
        out_shape=jax.ShapeDtypeStruct((voxels, C), bf16),
        in_specs=[SMEM] * 3 + [VMEM] * 15,
        out_specs=VMEM,
        scratch_shapes=[
            pltpu.VMEM((2, voxels // 2, 2 * C), bf16),
            pltpu.VMEM((voxels, LANES), i32),
            state,
            state,
            state,
            pltpu.VMEM((voxels, C), bf16),
            state,
            pltpu.VMEM((voxels, C), bf16),
        ],
        compiler_params=params(28),
        name="finish",
    )(
        tags, before_tag, after_tag, row(tags), row(before_tag), row(after_tag), before, after, w_heads,
        query, late_value, late_sum, late_top, early, latent, w_out, w_up, w_down
    )


def local(features, w_embed, owner_device, voxel_slot, window_ids, w_heads, w_out, w_up, w_down):
    devices = lax.axis_size(AXES)
    patches = features.shape[0]
    voxels = window_ids.shape[0]
    capacity = max(2, 2 * patches // devices)
    buffer = dispatch(
        features, w_embed, owner_device.reshape(1, patches), voxel_slot.reshape(1, patches), devices, capacity
    )
    buffer, tags = lax.optimization_barrier((buffer, window_ids))
    arrived = lax.all_to_all(buffer, AXES, split_axis=0, concat_axis=0, tiled=True)
    before_tag = passed_along(tags, 1)
    after_tag = passed_along(tags, -1)
    arrived, before_tag, after_tag = lax.optimization_barrier((arrived, before_tag, after_tag))
    latent, low, high = gather(arrived, voxels)
    before_near = passed_along(high, 1)
    after_near = passed_along(low, -1)
    before_far = passed_along(low, 1)
    after_far = passed_along(high, -1)
    query, value, top, total, up, down = near(tags, low, high, w_heads, w_up, w_down)
    places = (tags, before_tag, after_tag)
    *late, early = middle(
        *places, before_near, after_near, w_heads, query, value, total, top, latent, w_out, up, down
    )
    return finish(*places, before_far, after_far, w_heads, query, *late, early, latent, w_out, up, down)


def solution(mesh):
    rows = P(AXES, None)
    return jax.shard_map(
        local,
        mesh=mesh,
        in_specs=(rows, P(), rows, P(AXES), P(AXES), P(), P(), P(), P()),
        out_specs=rows,
        check_vma=False,
    )
```

```python
import jax
import jax.numpy as jnp
from jax import lax
from jax.experimental import pallas as pl
from jax.experimental.pallas import tpu as pltpu
from jax.sharding import PartitionSpec as P

C = 768
HEADS = 12
HEAD = C // HEADS
PAIRS = HEADS // 2
LANES = 128
CHUNKS = C // LANES
BLOCK = 128
epsilon = 1e-06
AXES = ("view", "vox")
f32 = jnp.float32
bf16 = jnp.bfloat16
i32 = jnp.int32
MASKED = -1e30


def passed_along(block, distance):
    devices = range(lax.axis_size(AXES))
    route = [(i - distance, i) for i in devices if i - distance in devices]
    return lax.ppermute(block, AXES, route)


def layer_norm(values):
    average = jnp.mean(values, axis=-1, keepdims=True)
    centered = values - average
    variance = jnp.mean(centered * centered, axis=-1, keepdims=True)
    return centered * lax.rsqrt(variance + epsilon)


def across(a, b):
    return lax.dot_general(a, b, (((1,), (1,)), ((), ())), preferred_element_type=f32)


def dot(a, b):
    return jnp.dot(a, b, preferred_element_type=f32)


def iota(shape, dim):
    return lax.broadcasted_iota(i32, shape, dim)


def params(mib):
    return pltpu.CompilerParams(vmem_limit_bytes=mib << 20)


GROUPS = 4


def dispatch_kernel(
    features_hbm, embed_hbm, owner_hbm, slot_hbm, out_hbm,
    features_ref, embed_ref, owner_ref, slot_ref, out_ref, payload_ref, position_ref, digits_ref, in_sem, out_sem
):
    copies = [
        pltpu.make_async_copy(source, target, in_sem.at[k])
        for k, (source, target) in enumerate(
            (
                (owner_hbm, owner_ref),
                (slot_hbm, slot_ref),
                (features_hbm, features_ref),
                (embed_hbm, embed_ref),
            )
        )
    ]
    for copy in copies:
        copy.start()
    patches = features_ref.shape[0]
    devices = digits_ref.shape[1]
    group = devices // GROUPS
    capacity = (out_ref.shape[1] - 8) // CHUNKS
    part = 256
    mine = lax.rem(lax.axis_index("vox"), LANES // capacity)
    earlier = jnp.where(iota((part, part), 0) < iota((part, part), 1), 1.0, 0.0).astype(bf16)
    copies[0].wait()
    copies[1].wait()
    owner = owner_ref[...]
    hits = jnp.where(iota((devices, patches), 0) == owner, 1.0, 0.0)
    running = jnp.zeros((devices, 1), f32)
    ranks = []
    for start in range(0, patches, part):
        here = hits[:, start : start + part]
        before = dot(here.astype(bf16), earlier) + running
        running = running + jnp.sum(here, axis=1, keepdims=True)
        ranks.append(jnp.sum(here * before, axis=0, keepdims=True))
    rank = jnp.concatenate(ranks, axis=1).astype(i32)
    position_ref[...] = owner * capacity + rank
    place = jnp.where(iota((LANES, patches), 0) == rank + capacity * mine, 1.0, 0.0).astype(bf16)
    code = slot_ref[...] + 1
    digits_ref[0] = across((hits * (code >> 4).astype(f32)).astype(bf16), place)
    digits_ref[1] = across((hits * (code & 15).astype(f32)).astype(bf16), place)
    copies[2].wait()
    copies[3].wait()
    payload_ref[...] = dot(features_ref[...], embed_ref[...]).astype(bf16)
    rows = group * capacity
    sends = []
    for g in range(GROUPS):
        here = slice(g * group, (g + 1) * group)
        chosen = jnp.where(iota((rows, patches), 0) + g * rows == position_ref[...], 1.0, 0.0)
        block = dot(chosen.astype(bf16), payload_ref[...]).astype(bf16)
        for c in range(CHUNKS):
            out_ref[here, c * capacity : (c + 1) * capacity, :] = block[
                :, c * LANES : (c + 1) * LANES
            ].reshape(group, capacity, LANES)
        high = jnp.broadcast_to(digits_ref[0, here, :][:, None, :], (group, 8, LANES))
        low = jnp.broadcast_to(digits_ref[1, here, :][:, None, :], (group, 8, LANES))
        out_ref[here, CHUNKS * capacity :, :] = jnp.where(
            iota((group, 8, LANES), 1) < 4, high, low
        ).astype(bf16)
        send = pltpu.make_async_copy(out_ref.at[here], out_hbm.at[here], out_sem.at[g])
        send.start()
        sends.append(send)
    for send in sends:
        send.wait()


def kept(*arrays):
    return [pltpu.with_memory_space_constraint(array, pltpu.HBM) for array in arrays]


HBM = pl.BlockSpec(memory_space=pltpu.HBM)
VMEM = pl.BlockSpec(memory_space=pltpu.VMEM)
SMEM = pl.BlockSpec(memory_space=pltpu.SMEM)


def dispatch(features, w_embed, owner, slot, devices, capacity):
    patches, width = features.shape
    tall = CHUNKS * capacity + 8
    return pl.pallas_call(
        dispatch_kernel,
        out_shape=pltpu.HBM((devices, tall, LANES), bf16),
        in_specs=[HBM] * 4,
        out_specs=HBM,
        scratch_shapes=[
            pltpu.VMEM((patches, width), bf16),
            pltpu.VMEM((width, C), bf16),
            pltpu.VMEM((1, patches), i32),
            pltpu.VMEM((1, patches), i32),
            pltpu.VMEM((devices, tall, LANES), bf16),
            pltpu.VMEM((patches, C), bf16),
            pltpu.VMEM((1, patches), i32),
            pltpu.VMEM((2, devices, LANES), f32),
            pltpu.SemaphoreType.DMA((4,)),
            pltpu.SemaphoreType.DMA((GROUPS,)),
        ],
        compiler_params=params(32),
        name="dispatch",
    )(*kept(features, w_embed, owner, slot))


def gather_kernel(arrived_hbm, latent_ref, low_ref, high_ref, arrived_ref, digit_ref, member_ref, sem):
    sources = arrived_ref.shape[0]
    capacity = arrived_ref.shape[1] // CHUNKS
    tall = CHUNKS * capacity
    voxels = latent_ref.shape[0]
    each = LANES // capacity
    digit_copy = pltpu.make_async_copy(arrived_hbm.at[:, tall:, :], digit_ref, sem.at[0])
    digit_copy.start()
    data_copy = pltpu.make_async_copy(arrived_hbm.at[:, :tall, :], arrived_ref, sem.at[1])
    data_copy.start()
    digit_copy.wait()
    digits = jnp.sum(digit_ref[...].astype(f32).reshape(sources // each, each, 8, LANES), axis=1)
    code = (digits[:, 0, :] * 16.0 + digits[:, 4, :]).astype(i32) - 1
    counted = jnp.zeros((voxels, LANES), f32)
    for g in range(sources // each):
        member = jnp.where(iota((voxels, LANES), 0) == code[g : g + 1], 1.0, 0.0)
        counted = counted + member
        member_ref[:, g * LANES : (g + 1) * LANES] = member.astype(bf16)
    counts = jnp.sum(counted, axis=1, keepdims=True)
    data_copy.wait()
    data = jnp.concatenate(
        [
            arrived_ref[:, c * capacity : (c + 1) * capacity, :].reshape(sources * capacity, LANES)
            for c in range(CHUNKS)
        ],
        axis=1,
    )
    latent = dot(member_ref[...], data) / jnp.maximum(counts, 1.0)
    latent_ref[...] = latent
    normed = layer_norm(latent).astype(bf16)
    low_ref[...] = normed[: voxels // 2]
    high_ref[...] = normed[voxels // 2 :]


def gather(arrived, voxels):
    sources, tall, _ = arrived.shape
    return pl.pallas_call(
        gather_kernel,
        out_shape=(
            jax.ShapeDtypeStruct((voxels, C), f32),
            jax.ShapeDtypeStruct((voxels // 2, C), bf16),
            jax.ShapeDtypeStruct((voxels // 2, C), bf16),
        ),
        in_specs=[HBM],
        out_specs=(VMEM, VMEM, VMEM),
        scratch_shapes=[
            pltpu.VMEM((sources, tall - 8, LANES), bf16),
            pltpu.VMEM((sources, 8, LANES), bf16),
            pltpu.VMEM((voxels, sources * ((tall - 8) // CHUNKS)), bf16),
            pltpu.SemaphoreType.DMA((2,)),
        ],
        compiler_params=params(24),
        name="gather",
    )(arrived)


def column_of(row):
    return jnp.broadcast_to(row, (LANES, row.shape[1])).T


def by_half(both):
    first, second = jnp.split(both, 2, axis=0)
    return jnp.where(iota(first.shape, 1) < HEAD, first, second)


def scores_of(query_pair, key_pair, bias):
    left = iota(query_pair.shape, 1) < HEAD
    none = jnp.zeros_like(query_pair)
    both = jnp.concatenate([jnp.where(left, query_pair, none), jnp.where(left, none, query_pair)], axis=0)
    return across(both, key_pair) + bias


def weighted(score, highest, value_pair):
    exponent = jnp.exp(score - highest).astype(bf16)
    wide = jnp.concatenate([value_pair, jnp.ones_like(value_pair)], axis=1)
    return dot(exponent, wide)


def bias_of(column, row):
    tiles = [
        jnp.where(column == row[:, k : k + LANES], 0.0, MASKED) for k in range(0, row.shape[1], LANES)
    ]
    bias = jnp.concatenate(tiles, axis=1)
    return jnp.concatenate([bias, bias], axis=0)


def rims(tag_ref, before_tag_ref, after_tag_ref):
    voxels = tag_ref.shape[0]
    blocks = voxels // BLOCK
    start_tag, end_tag = tag_ref[0], tag_ref[voxels - 1]
    head = i32(0)
    tail = i32(0)
    for k in range(blocks):
        head += (tag_ref[k * BLOCK] == start_tag).astype(i32)
        tail += (tag_ref[k * BLOCK + BLOCK - 1] == end_tag).astype(i32)
    ring = [lax.axis_index(axis) for axis in AXES]
    ends = [lax.axis_size(axis) - 1 for axis in AXES]
    first = jnp.logical_and(ring[0] == 0, ring[1] == 0)
    final = jnp.logical_and(ring[0] == ends[0], ring[1] == ends[1])
    head = jnp.where(jnp.logical_or(first, before_tag_ref[voxels - 1] != start_tag), 0, head)
    tail = jnp.where(jnp.logical_or(final, after_tag_ref[0] != end_tag), 0, tail)
    return head, tail


def feed_forward(attended, latent, w_out_ref, w_up_ref, w_down_ref):
    middle = latent + dot(attended, w_out_ref[...])
    normed = layer_norm(middle).astype(bf16)
    total = middle
    part = 512
    parts = range(0, w_up_ref.shape[1], part)
    raised = dot(normed, w_up_ref[:, :part])
    for k in parts:
        coming = dot(normed, w_up_ref[:, k + part : k + 2 * part]) if k + part in parts else None
        bent = jax.nn.gelu(raised, approximate=True).astype(bf16)
        total = total + dot(bent, w_down_ref[k : k + part, :])
        raised = coming
    return total.astype(bf16)


PIECES = 4


def fetched(source, target, sem):
    each = source.shape[0] // PIECES
    pieces = [slice(j * each, (j + 1) * each) for j in range(PIECES)]
    copies = [pltpu.make_async_copy(source.at[p], target.at[p], sem.at[j]) for j, p in enumerate(pieces)]
    for copy in copies:
        copy.start()
    return copies


def near_kernel(
    tag_ref, tag_row_ref, low_ref, high_ref, heads_ref, up_hbm,
    query_ref, value_ref, top_ref, sum_ref, up_ref, kv_ref, column_ref, sem
):
    fetches = fetched(up_hbm, up_ref, sem)
    voxels = query_ref.shape[0]
    blocks = voxels // BLOCK
    normed = jnp.concatenate([low_ref[...], high_ref[...]], axis=0)
    query_ref[...] = dot(normed, heads_ref[:, :C]).astype(bf16) * jnp.asarray(HEAD**-0.5, bf16)
    kv_ref[...] = dot(normed, heads_ref[:, C:]).astype(bf16)
    column_ref[...] = column_of(tag_row_ref[...])

    def one_block(b, carry):
        rows = pl.ds(pl.multiple_of(b * BLOCK, BLOCK), BLOCK)
        first, last = tag_ref[b * BLOCK], tag_ref[b * BLOCK + BLOCK - 1]
        low = i32(0)
        high = i32(0)
        for k in range(blocks):
            low = low + (tag_ref[k * BLOCK + BLOCK - 1] < first).astype(i32)
            high = high + (tag_ref[k * BLOCK] <= last).astype(i32)
        short = high - low <= 2
        low = jnp.where(short, jnp.minimum(low, blocks - 2), 0)

        def attend(n):
            keys = pl.ds(pl.multiple_of(low * BLOCK, BLOCK), n * BLOCK)
            bias = bias_of(column_ref[rows, :], tag_row_ref[:, keys])
            for p in range(PAIRS):
                lanes = slice(p * LANES, (p + 1) * LANES)
                score = scores_of(query_ref[rows, lanes], kv_ref[keys, lanes], bias)
                highest = jnp.max(score, axis=1, keepdims=True)
                result = weighted(score, highest, kv_ref[keys, C + p * LANES : C + (p + 1) * LANES])
                value_ref[rows, lanes] = by_half(result[:, :LANES])
                sum_ref[rows, lanes] = by_half(result[:, LANES:])
                top_ref[rows, lanes] = by_half(jnp.broadcast_to(highest, (2 * BLOCK, LANES)))

        pl.when(short)(lambda: attend(2))
        pl.when(jnp.logical_not(short))(lambda: attend(blocks))
        return carry

    lax.fori_loop(0, blocks, one_block, 0)
    for copy in fetches:
        copy.wait()


def near(tags, low, high, w_heads, w_up):
    voxels = tags.shape[0]
    state = jax.ShapeDtypeStruct((voxels, C), f32)
    return pl.pallas_call(
        near_kernel,
        out_shape=(
            jax.ShapeDtypeStruct((voxels, C), bf16),
            state,
            state,
            state,
            pltpu.VMEM(w_up.shape, bf16),
        ),
        in_specs=[SMEM] + [VMEM] * 4 + [HBM],
        out_specs=(VMEM,) * 5,
        scratch_shapes=[
            pltpu.VMEM((voxels, 2 * C), bf16),
            pltpu.VMEM((voxels, LANES), i32),
            pltpu.SemaphoreType.DMA((PIECES,)),
        ],
        compiler_params=params(20),
        name="near",
    )(tags, tags.reshape(1, voxels), low, high, w_heads, *kept(w_up))


def extend(query_ref, rows, kv_ref, side, bias, old, new):
    for p in range(PAIRS):
        lanes = slice(p * LANES, (p + 1) * LANES)
        values = slice(C + p * LANES, C + (p + 1) * LANES)
        score = scores_of(query_ref[rows, lanes], kv_ref[side, :, lanes], bias)
        highest = jnp.max(score, axis=1, keepdims=True)
        result = weighted(score, highest, kv_ref[side, :, values])
        here = by_half(jnp.broadcast_to(highest, result[:, :LANES].shape))
        known = old[2][rows, lanes]
        top = jnp.maximum(known, here)
        fade, grow = jnp.exp(known - top), jnp.exp(here - top)
        new[0][rows, lanes] = old[0][rows, lanes] * fade + by_half(result[:, :LANES]) * grow
        new[1][rows, lanes] = old[1][rows, lanes] * fade + by_half(result[:, LANES:]) * grow
        new[2][rows, lanes] = top


def late_rows(k, head, late, blocks):
    b = jnp.where(k < head, k, k + blocks - late)
    put = pl.ds(pl.multiple_of(k * BLOCK, BLOCK), BLOCK)
    return b, pl.ds(pl.multiple_of(b * BLOCK, BLOCK), BLOCK), put


def project(need_before, need_after, before_ref, after_ref, heads_ref, kv_ref):
    half = before_ref.shape[0]

    @pl.when(jnp.logical_and(need_before, need_after))
    def _():
        both = jnp.concatenate([before_ref[...], after_ref[...]], axis=0)
        kv_ref[...] = dot(both, heads_ref[:, C:]).astype(bf16).reshape(2, half, 2 * C)

    @pl.when(need_before != need_after)
    def _():
        one = jnp.where(need_before, before_ref[...], after_ref[...])
        kv_ref[jnp.where(need_before, 0, 1)] = dot(one, heads_ref[:, C:]).astype(bf16)


def middle_kernel(
    tag_ref, before_tag_ref, after_tag_ref, tag_row_ref, before_row_ref, after_row_ref,
    before_ref, after_ref, heads_ref, query_ref, value_ref, sum_ref, top_ref, latent_ref, w_out_ref, up_ref, down_hbm,
    late_value_ref, late_sum_ref, late_top_ref, out_ref, down_ref, kv_ref, column_ref, sem
):
    fetches = fetched(down_hbm, down_ref, sem)
    voxels = query_ref.shape[0]
    blocks = voxels // BLOCK
    half = voxels // 2
    head, tail = rims(tag_ref, before_tag_ref, after_tag_ref)
    late = jnp.minimum(head + tail, blocks)

    @pl.when(late > 0)
    def _():
        column_ref[...] = column_of(tag_row_ref[...])

    project(head > 0, tail > 0, before_ref, after_ref, heads_ref, kv_ref)

    old, new = (value_ref, sum_ref, top_ref), (late_value_ref, late_sum_ref, late_top_ref)

    def one_step(step, carry):
        part, side = step // 2, step % 2
        rows = pl.ds(pl.multiple_of(part * half, half), half)
        from_before = head > 2 * part
        needed = jnp.where(side == 0, from_before, tail > 2 * (1 - part))
        again = jnp.logical_and(side == 1, from_before)
        row = jnp.where(side == 0, before_row_ref[:, half:], after_row_ref[:, :half])
        bias = lambda: bias_of(column_ref[rows, :], row)

        @pl.when(jnp.logical_and(needed, jnp.logical_not(again)))
        def _():
            extend(query_ref, rows, kv_ref, side, bias(), old, new)

        @pl.when(jnp.logical_and(needed, again))
        def _():
            extend(query_ref, rows, kv_ref, side, bias(), new, new)

        return carry

    lax.fori_loop(0, 4, one_step, 0)
    for copy in fetches:
        copy.wait()
    early = blocks - late

    def settle(rows):
        attended = (value_ref[rows, :] / sum_ref[rows, :]).astype(bf16)
        out_ref[rows, :] = feed_forward(attended, latent_ref[rows, :], w_out_ref, up_ref, down_ref)

    @pl.when(jnp.logical_and(early > 0, early <= 2))
    def _():
        start = jnp.minimum(head, blocks - 2) * BLOCK
        settle(pl.ds(pl.multiple_of(start, BLOCK), half))

    @pl.when(early > 2)
    def _():
        settle(slice(0, voxels))


def middle(tags, before_tag, after_tag, before, after, w_heads, query, value, total, top, latent, w_out, w_up, w_down):
    voxels = query.shape[0]
    row = lambda t: t.reshape(1, voxels)
    state = jax.ShapeDtypeStruct((voxels, C), f32)
    return pl.pallas_call(
        middle_kernel,
        out_shape=(
            state,
            state,
            state,
            jax.ShapeDtypeStruct((voxels, C), bf16),
            pltpu.VMEM(w_down.shape, bf16),
        ),
        in_specs=[SMEM] * 3 + [VMEM] * 13 + [HBM],
        out_specs=(VMEM,) * 5,
        scratch_shapes=[
            pltpu.VMEM((2, voxels // 2, 2 * C), bf16),
            pltpu.VMEM((voxels, LANES), i32),
            pltpu.SemaphoreType.DMA((PIECES,)),
        ],
        compiler_params=params(20),
        name="middle",
    )(
        tags, before_tag, after_tag, row(tags), row(before_tag), row(after_tag), before, after, w_heads,
        query, value, total, top, latent, w_out, w_up, *kept(w_down)
    )


def finish_kernel(
    tag_ref, before_tag_ref, after_tag_ref, tag_row_ref, before_row_ref, after_row_ref,
    before_ref, after_ref, heads_ref, query_ref, late_value_ref, late_sum_ref, late_top_ref,
    early_ref, latent_ref, w_out_ref, up_ref, down_ref, out_ref,
    kv_ref, column_ref, value_ref, sum_ref, top_ref, attended_ref, late_latent_ref, late_out_ref
):
    voxels = query_ref.shape[0]
    blocks = voxels // BLOCK
    half = voxels // 2
    head, tail = rims(tag_ref, before_tag_ref, after_tag_ref)
    late = jnp.minimum(head + tail, blocks)
    far_before = jnp.logical_and(head > 0, before_tag_ref[half - 1] == tag_ref[0])
    far_after = jnp.logical_and(tail > 0, after_tag_ref[half] == tag_ref[voxels - 1])

    @pl.when(jnp.logical_or(far_before, far_after))
    def _():
        column_ref[...] = column_of(tag_row_ref[...])

    project(far_before, far_after, before_ref, after_ref, heads_ref, kv_ref)

    old, new = (late_value_ref, late_sum_ref, late_top_ref), (value_ref, sum_ref, top_ref)

    def one_part(part, carry):
        @pl.when(jnp.where(part == 0, far_before, far_after))
        def _():
            rows = pl.ds(pl.multiple_of(part * half, half), half)
            row = jnp.where(part == 0, before_row_ref[:, :half], after_row_ref[:, half:])
            extend(query_ref, rows, kv_ref, part, bias_of(column_ref[rows, :], row), old, new)

        return carry

    lax.fori_loop(0, 2, one_part, 0)

    def one_late(k, carry):
        b, rows, put = late_rows(k, head, late, blocks)
        changed = jnp.where(b < blocks // 2, far_before, far_after)

        @pl.when(changed)
        def _():
            attended_ref[put, :] = (value_ref[rows, :] / sum_ref[rows, :]).astype(bf16)

        @pl.when(jnp.logical_not(changed))
        def _():
            attended_ref[put, :] = (late_value_ref[rows, :] / late_sum_ref[rows, :]).astype(bf16)

        late_latent_ref[put, :] = latent_ref[rows, :]
        return carry

    lax.fori_loop(0, late, one_late, 0)
    out_ref[...] = early_ref[...]

    def settle(rows):
        late_out_ref[rows, :] = feed_forward(
            attended_ref[rows, :], late_latent_ref[rows, :], w_out_ref, up_ref, down_ref
        )

    @pl.when(jnp.logical_and(late > 0, late <= 2))
    def _():
        settle(slice(0, half))

    @pl.when(late > 2)
    def _():
        settle(slice(0, voxels))

    def put_back(k, carry):
        _, rows, put = late_rows(k, head, late, blocks)
        out_ref[rows, :] = late_out_ref[put, :]
        return carry

    lax.fori_loop(0, late, put_back, 0)


def finish(
    tags, before_tag, after_tag, before, after, w_heads, query, late_value, late_sum, late_top, early, latent,
    w_out, w_up, w_down
):
    voxels = query.shape[0]
    row = lambda t: t.reshape(1, voxels)
    state = pltpu.VMEM((voxels, C), f32)
    return pl.pallas_call(
        finish_kernel,
        out_shape=jax.ShapeDtypeStruct((voxels, C), bf16),
        in_specs=[SMEM] * 3 + [VMEM] * 15,
        out_specs=VMEM,
        scratch_shapes=[
            pltpu.VMEM((2, voxels // 2, 2 * C), bf16),
            pltpu.VMEM((voxels, LANES), i32),
            state,
            state,
            state,
            pltpu.VMEM((voxels, C), bf16),
            state,
            pltpu.VMEM((voxels, C), bf16),
        ],
        compiler_params=params(28),
        name="finish",
    )(
        tags, before_tag, after_tag, row(tags), row(before_tag), row(after_tag), before, after, w_heads,
        query, late_value, late_sum, late_top, early, latent, w_out, w_up, w_down
    )


def local(features, w_embed, owner_device, voxel_slot, window_ids, w_heads, w_out, w_up, w_down):
    devices = lax.axis_size(AXES)
    patches = features.shape[0]
    voxels = window_ids.shape[0]
    capacity = max(2, 2 * patches // devices)
    buffer = dispatch(
        features, w_embed, owner_device.reshape(1, patches), voxel_slot.reshape(1, patches), devices, capacity
    )
    buffer, tags = lax.optimization_barrier((buffer, window_ids))
    arrived = lax.all_to_all(buffer, AXES, split_axis=0, concat_axis=0, tiled=True)
    before_tag = passed_along(tags, 1)
    after_tag = passed_along(tags, -1)
    arrived, before_tag, after_tag = lax.optimization_barrier((arrived, before_tag, after_tag))
    latent, low, high = gather(arrived, voxels)
    before_near = passed_along(high, 1)
    after_near = passed_along(low, -1)
    before_far = passed_along(low, 1)
    after_far = passed_along(high, -1)
    query, value, top, total, up = near(tags, low, high, w_heads, w_up)
    places = (tags, before_tag, after_tag)
    *late, early, down = middle(
        *places, before_near, after_near, w_heads, query, value, total, top, latent, w_out, up, w_down
    )
    return finish(*places, before_far, after_far, w_heads, query, *late, early, latent, w_out, up, down)


def solution(mesh):
    rows = P(AXES, None)
    return jax.shard_map(
        local,
        mesh=mesh,
        in_specs=(rows, P(), rows, P(AXES), P(AXES), P(), P(), P(), P()),
        out_specs=rows,
        check_vma=False,
    )
```

```python
import jax
import jax.numpy as jnp
from jax import lax
from jax.experimental import pallas as pl
from jax.experimental.pallas import tpu as pltpu
from jax.sharding import PartitionSpec as P

C = 768
HEADS = 12
HEAD = C // HEADS
PAIRS = HEADS // 2
LANES = 128
CHUNKS = C // LANES
BLOCK = 128
epsilon = 1e-06
AXES = ("view", "vox")
f32 = jnp.float32
bf16 = jnp.bfloat16
i32 = jnp.int32
MASKED = -1e30


def passed_along(block, distance):
    devices = range(lax.axis_size(AXES))
    route = [(i - distance, i) for i in devices if i - distance in devices]
    return lax.ppermute(block, AXES, route)


def layer_norm(values):
    average = jnp.mean(values, axis=-1, keepdims=True)
    centered = values - average
    variance = jnp.mean(centered * centered, axis=-1, keepdims=True)
    return centered * lax.rsqrt(variance + epsilon)


def across(a, b):
    return lax.dot_general(a, b, (((1,), (1,)), ((), ())), preferred_element_type=f32)


def dot(a, b):
    return jnp.dot(a, b, preferred_element_type=f32)


def iota(shape, dim):
    return lax.broadcasted_iota(i32, shape, dim)


def params(mib):
    return pltpu.CompilerParams(vmem_limit_bytes=mib << 20)


GROUPS = 4


def dispatch_kernel(
    features_hbm, embed_hbm, owner_hbm, slot_hbm, out_hbm,
    features_ref, embed_ref, owner_ref, slot_ref, out_ref, payload_ref, position_ref, digits_ref, in_sem, out_sem
):
    copies = [
        pltpu.make_async_copy(source, target, in_sem.at[k])
        for k, (source, target) in enumerate(
            (
                (owner_hbm, owner_ref),
                (slot_hbm, slot_ref),
                (features_hbm, features_ref),
                (embed_hbm, embed_ref),
            )
        )
    ]
    for copy in copies:
        copy.start()
    patches = features_ref.shape[0]
    devices = digits_ref.shape[1]
    group = devices // GROUPS
    capacity = (out_ref.shape[1] - 8) // CHUNKS
    part = 256
    mine = lax.rem(lax.axis_index("vox"), LANES // capacity)
    earlier = jnp.where(iota((part, part), 0) < iota((part, part), 1), 1.0, 0.0).astype(bf16)
    copies[0].wait()
    copies[1].wait()
    owner = owner_ref[...]
    hits = jnp.where(iota((devices, patches), 0) == owner, 1.0, 0.0)
    running = jnp.zeros((devices, 1), f32)
    ranks = []
    for start in range(0, patches, part):
        here = hits[:, start : start + part]
        before = dot(here.astype(bf16), earlier) + running
        running = running + jnp.sum(here, axis=1, keepdims=True)
        ranks.append(jnp.sum(here * before, axis=0, keepdims=True))
    rank = jnp.concatenate(ranks, axis=1).astype(i32)
    position_ref[...] = owner * capacity + rank
    place = jnp.where(iota((LANES, patches), 0) == rank + capacity * mine, 1.0, 0.0).astype(bf16)
    code = slot_ref[...] + 1
    digits_ref[0] = across((hits * (code >> 4).astype(f32)).astype(bf16), place)
    digits_ref[1] = across((hits * (code & 15).astype(f32)).astype(bf16), place)
    copies[2].wait()
    copies[3].wait()
    payload_ref[...] = dot(features_ref[...], embed_ref[...]).astype(bf16)
    rows = group * capacity
    sends = []
    for g in range(GROUPS):
        here = slice(g * group, (g + 1) * group)
        chosen = jnp.where(iota((rows, patches), 0) + g * rows == position_ref[...], 1.0, 0.0)
        block = dot(chosen.astype(bf16), payload_ref[...]).astype(bf16)
        for c in range(CHUNKS):
            out_ref[here, c * capacity : (c + 1) * capacity, :] = block[
                :, c * LANES : (c + 1) * LANES
            ].reshape(group, capacity, LANES)
        high = jnp.broadcast_to(digits_ref[0, here, :][:, None, :], (group, 8, LANES))
        low = jnp.broadcast_to(digits_ref[1, here, :][:, None, :], (group, 8, LANES))
        out_ref[here, CHUNKS * capacity :, :] = jnp.where(
            iota((group, 8, LANES), 1) < 4, high, low
        ).astype(bf16)
        send = pltpu.make_async_copy(out_ref.at[here], out_hbm.at[here], out_sem.at[g])
        send.start()
        sends.append(send)
    for send in sends:
        send.wait()


def kept(*arrays):
    return [pltpu.with_memory_space_constraint(array, pltpu.HBM) for array in arrays]


HBM = pl.BlockSpec(memory_space=pltpu.HBM)
VMEM = pl.BlockSpec(memory_space=pltpu.VMEM)
SMEM = pl.BlockSpec(memory_space=pltpu.SMEM)


def dispatch(features, w_embed, owner, slot, devices, capacity):
    patches, width = features.shape
    tall = CHUNKS * capacity + 8
    return pl.pallas_call(
        dispatch_kernel,
        out_shape=pltpu.HBM((devices, tall, LANES), bf16),
        in_specs=[HBM] * 4,
        out_specs=HBM,
        scratch_shapes=[
            pltpu.VMEM((patches, width), bf16),
            pltpu.VMEM((width, C), bf16),
            pltpu.VMEM((1, patches), i32),
            pltpu.VMEM((1, patches), i32),
            pltpu.VMEM((devices, tall, LANES), bf16),
            pltpu.VMEM((patches, C), bf16),
            pltpu.VMEM((1, patches), i32),
            pltpu.VMEM((2, devices, LANES), f32),
            pltpu.SemaphoreType.DMA((4,)),
            pltpu.SemaphoreType.DMA((GROUPS,)),
        ],
        compiler_params=params(32),
        name="dispatch",
    )(*kept(features, w_embed, owner, slot))


def gather_kernel(arrived_hbm, latent_ref, low_ref, high_ref, arrived_ref, digit_ref, member_ref, sem):
    sources = arrived_ref.shape[0]
    capacity = arrived_ref.shape[1] // CHUNKS
    tall = CHUNKS * capacity
    voxels = latent_ref.shape[0]
    each = LANES // capacity
    digit_copy = pltpu.make_async_copy(arrived_hbm.at[:, tall:, :], digit_ref, sem.at[0])
    digit_copy.start()
    data_copy = pltpu.make_async_copy(arrived_hbm.at[:, :tall, :], arrived_ref, sem.at[1])
    data_copy.start()
    digit_copy.wait()
    digits = jnp.sum(digit_ref[...].astype(f32).reshape(sources // each, each, 8, LANES), axis=1)
    code = (digits[:, 0, :] * 16.0 + digits[:, 4, :]).astype(i32) - 1
    counted = jnp.zeros((voxels, LANES), f32)
    for g in range(sources // each):
        member = jnp.where(iota((voxels, LANES), 0) == code[g : g + 1], 1.0, 0.0)
        counted = counted + member
        member_ref[:, g * LANES : (g + 1) * LANES] = member.astype(bf16)
    counts = jnp.sum(counted, axis=1, keepdims=True)
    data_copy.wait()
    data = jnp.concatenate(
        [
            arrived_ref[:, c * capacity : (c + 1) * capacity, :].reshape(sources * capacity, LANES)
            for c in range(CHUNKS)
        ],
        axis=1,
    )
    latent = dot(member_ref[...], data) / jnp.maximum(counts, 1.0)
    latent_ref[...] = latent
    normed = layer_norm(latent).astype(bf16)
    low_ref[...] = normed[: voxels // 2]
    high_ref[...] = normed[voxels // 2 :]


def gather(arrived, voxels):
    sources, tall, _ = arrived.shape
    return pl.pallas_call(
        gather_kernel,
        out_shape=(
            jax.ShapeDtypeStruct((voxels, C), f32),
            jax.ShapeDtypeStruct((voxels // 2, C), bf16),
            jax.ShapeDtypeStruct((voxels // 2, C), bf16),
        ),
        in_specs=[HBM],
        out_specs=(VMEM, VMEM, VMEM),
        scratch_shapes=[
            pltpu.VMEM((sources, tall - 8, LANES), bf16),
            pltpu.VMEM((sources, 8, LANES), bf16),
            pltpu.VMEM((voxels, sources * ((tall - 8) // CHUNKS)), bf16),
            pltpu.SemaphoreType.DMA((2,)),
        ],
        compiler_params=params(24),
        name="gather",
    )(arrived)


def column_of(row):
    return jnp.broadcast_to(row, (LANES, row.shape[1])).T


def by_half(both):
    first, second = jnp.split(both, 2, axis=0)
    return jnp.where(iota(first.shape, 1) < HEAD, first, second)


def scores_of(query_pair, key_pair, bias):
    left = iota(query_pair.shape, 1) < HEAD
    none = jnp.zeros_like(query_pair)
    both = jnp.concatenate([jnp.where(left, query_pair, none), jnp.where(left, none, query_pair)], axis=0)
    return across(both, key_pair) + bias


def weighted(score, highest, value_pair):
    exponent = jnp.exp(score - highest).astype(bf16)
    wide = jnp.concatenate([value_pair, jnp.ones_like(value_pair)], axis=1)
    return dot(exponent, wide)


def bias_of(column, row):
    tiles = [
        jnp.where(column == row[:, k : k + LANES], 0.0, MASKED) for k in range(0, row.shape[1], LANES)
    ]
    bias = jnp.concatenate(tiles, axis=1)
    return jnp.concatenate([bias, bias], axis=0)


def rims(tag_ref, before_tag_ref, after_tag_ref):
    voxels = tag_ref.shape[0]
    blocks = voxels // BLOCK
    start_tag, end_tag = tag_ref[0], tag_ref[voxels - 1]
    head = i32(0)
    tail = i32(0)
    for k in range(blocks):
        head += (tag_ref[k * BLOCK] == start_tag).astype(i32)
        tail += (tag_ref[k * BLOCK + BLOCK - 1] == end_tag).astype(i32)
    ring = [lax.axis_index(axis) for axis in AXES]
    ends = [lax.axis_size(axis) - 1 for axis in AXES]
    first = jnp.logical_and(ring[0] == 0, ring[1] == 0)
    final = jnp.logical_and(ring[0] == ends[0], ring[1] == ends[1])
    head = jnp.where(jnp.logical_or(first, before_tag_ref[voxels - 1] != start_tag), 0, head)
    tail = jnp.where(jnp.logical_or(final, after_tag_ref[0] != end_tag), 0, tail)
    return head, tail


def feed_forward(attended, latent, w_out_ref, w_up_ref, w_down_ref):
    middle = latent + dot(attended, w_out_ref[...])
    normed = layer_norm(middle).astype(bf16)
    total = middle
    part = 512
    parts = range(0, w_up_ref.shape[1], part)
    raised = dot(normed, w_up_ref[:, :part])
    for k in parts:
        coming = dot(normed, w_up_ref[:, k + part : k + 2 * part]) if k + part in parts else None
        bent = jax.nn.gelu(raised, approximate=True).astype(bf16)
        total = total + dot(bent, w_down_ref[k : k + part, :])
        raised = coming
    return total.astype(bf16)


PIECES = 4


def fetched(source, target, sem):
    each = source.shape[0] // PIECES
    pieces = [slice(j * each, (j + 1) * each) for j in range(PIECES)]
    copies = [pltpu.make_async_copy(source.at[p], target.at[p], sem.at[j]) for j, p in enumerate(pieces)]
    for copy in copies:
        copy.start()
    return copies


def near_kernel(
    tag_ref, tag_row_ref, low_ref, high_ref, heads_ref, up_hbm,
    query_ref, value_ref, top_ref, sum_ref, up_ref, kv_ref, column_ref, sem
):
    fetches = fetched(up_hbm, up_ref, sem)
    voxels = query_ref.shape[0]
    blocks = voxels // BLOCK
    normed = jnp.concatenate([low_ref[...], high_ref[...]], axis=0)
    query_ref[...] = dot(normed, heads_ref[:, :C]).astype(bf16) * jnp.asarray(HEAD**-0.5, bf16)
    kv_ref[...] = dot(normed, heads_ref[:, C:]).astype(bf16)
    column_ref[...] = column_of(tag_row_ref[...])

    def one_block(b, carry):
        rows = pl.ds(pl.multiple_of(b * BLOCK, BLOCK), BLOCK)
        first, last = tag_ref[b * BLOCK], tag_ref[b * BLOCK + BLOCK - 1]
        low = i32(0)
        high = i32(0)
        for k in range(blocks):
            low = low + (tag_ref[k * BLOCK + BLOCK - 1] < first).astype(i32)
            high = high + (tag_ref[k * BLOCK] <= last).astype(i32)
        short = high - low <= 2
        low = jnp.where(short, jnp.minimum(low, blocks - 2), 0)

        def attend(n):
            keys = pl.ds(pl.multiple_of(low * BLOCK, BLOCK), n * BLOCK)
            bias = bias_of(column_ref[rows, :], tag_row_ref[:, keys])
            for p in range(PAIRS):
                lanes = slice(p * LANES, (p + 1) * LANES)
                score = scores_of(query_ref[rows, lanes], kv_ref[keys, lanes], bias)
                highest = jnp.max(score, axis=1, keepdims=True)
                result = weighted(score, highest, kv_ref[keys, C + p * LANES : C + (p + 1) * LANES])
                value_ref[rows, lanes] = by_half(result[:, :LANES])
                sum_ref[rows, lanes] = by_half(result[:, LANES:])
                top_ref[rows, lanes] = by_half(jnp.broadcast_to(highest, (2 * BLOCK, LANES)))

        pl.when(short)(lambda: attend(2))
        pl.when(jnp.logical_not(short))(lambda: attend(blocks))
        return carry

    lax.fori_loop(0, blocks, one_block, 0)
    for copy in fetches:
        copy.wait()


def near(tags, low, high, w_heads, w_up):
    voxels = tags.shape[0]
    state = jax.ShapeDtypeStruct((voxels, C), f32)
    return pl.pallas_call(
        near_kernel,
        out_shape=(
            jax.ShapeDtypeStruct((voxels, C), bf16),
            state,
            state,
            state,
            pltpu.VMEM(w_up.shape, bf16),
        ),
        in_specs=[SMEM] + [VMEM] * 4 + [HBM],
        out_specs=(VMEM,) * 5,
        scratch_shapes=[
            pltpu.VMEM((voxels, 2 * C), bf16),
            pltpu.VMEM((voxels, LANES), i32),
            pltpu.SemaphoreType.DMA((PIECES,)),
        ],
        compiler_params=params(20),
        name="near",
    )(tags, tags.reshape(1, voxels), low, high, w_heads, *kept(w_up))


def extend(query_ref, rows, kv_ref, side, bias, old, new):
    for p in range(PAIRS):
        lanes = slice(p * LANES, (p + 1) * LANES)
        values = slice(C + p * LANES, C + (p + 1) * LANES)
        score = scores_of(query_ref[rows, lanes], kv_ref[side, :, lanes], bias)
        highest = jnp.max(score, axis=1, keepdims=True)
        result = weighted(score, highest, kv_ref[side, :, values])
        here = by_half(jnp.broadcast_to(highest, result[:, :LANES].shape))
        known = old[2][rows, lanes]
        top = jnp.maximum(known, here)
        fade, grow = jnp.exp(known - top), jnp.exp(here - top)
        new[0][rows, lanes] = old[0][rows, lanes] * fade + by_half(result[:, :LANES]) * grow
        new[1][rows, lanes] = old[1][rows, lanes] * fade + by_half(result[:, LANES:]) * grow
        new[2][rows, lanes] = top


def late_rows(k, head, late, blocks):
    b = jnp.where(k < head, k, k + blocks - late)
    put = pl.ds(pl.multiple_of(k * BLOCK, BLOCK), BLOCK)
    return b, pl.ds(pl.multiple_of(b * BLOCK, BLOCK), BLOCK), put


def project(need_before, need_after, before_ref, after_ref, heads_ref, kv_ref):
    half = before_ref.shape[0]

    @pl.when(jnp.logical_and(need_before, need_after))
    def _():
        both = jnp.concatenate([before_ref[...], after_ref[...]], axis=0)
        kv_ref[...] = dot(both, heads_ref[:, C:]).astype(bf16).reshape(2, half, 2 * C)

    @pl.when(need_before != need_after)
    def _():
        one = jnp.where(need_before, before_ref[...], after_ref[...])
        kv_ref[jnp.where(need_before, 0, 1)] = dot(one, heads_ref[:, C:]).astype(bf16)


def middle_kernel(
    tag_ref, before_tag_ref, after_tag_ref, tag_row_ref, before_row_ref, after_row_ref,
    before_ref, after_ref, heads_ref, query_ref, value_ref, sum_ref, top_ref, latent_ref, w_out_ref, up_ref, down_hbm,
    late_value_ref, late_sum_ref, late_top_ref, out_ref, down_ref, kv_ref, column_ref, sem
):
    fetches = fetched(down_hbm, down_ref, sem)
    voxels = query_ref.shape[0]
    blocks = voxels // BLOCK
    half = voxels // 2
    head, tail = rims(tag_ref, before_tag_ref, after_tag_ref)
    late = jnp.minimum(head + tail, blocks)

    @pl.when(late > 0)
    def _():
        column_ref[...] = column_of(tag_row_ref[...])

    project(head > 0, tail > 0, before_ref, after_ref, heads_ref, kv_ref)

    old, new = (value_ref, sum_ref, top_ref), (late_value_ref, late_sum_ref, late_top_ref)

    def one_step(step, carry):
        part, side = step // 2, step % 2
        rows = pl.ds(pl.multiple_of(part * half, half), half)
        from_before = head > 2 * part
        needed = jnp.where(side == 0, from_before, tail > 2 * (1 - part))
        again = jnp.logical_and(side == 1, from_before)
        row = jnp.where(side == 0, before_row_ref[:, half:], after_row_ref[:, :half])
        bias = lambda: bias_of(column_ref[rows, :], row)

        @pl.when(jnp.logical_and(needed, jnp.logical_not(again)))
        def _():
            extend(query_ref, rows, kv_ref, side, bias(), old, new)

        @pl.when(jnp.logical_and(needed, again))
        def _():
            extend(query_ref, rows, kv_ref, side, bias(), new, new)

        return carry

    lax.fori_loop(0, 4, one_step, 0)
    for copy in fetches:
        copy.wait()
    early = blocks - late

    def settle(rows):
        attended = (value_ref[rows, :] / sum_ref[rows, :]).astype(bf16)
        out_ref[rows, :] = feed_forward(attended, latent_ref[rows, :], w_out_ref, up_ref, down_ref)

    def one_span(k, carry):
        start = jnp.minimum(head + 2 * k, blocks - 2) * BLOCK
        settle(pl.ds(pl.multiple_of(start, BLOCK), half))
        return carry

    lax.fori_loop(0, (early + 1) // 2, one_span, 0)


def middle(tags, before_tag, after_tag, before, after, w_heads, query, value, total, top, latent, w_out, w_up, w_down):
    voxels = query.shape[0]
    row = lambda t: t.reshape(1, voxels)
    state = jax.ShapeDtypeStruct((voxels, C), f32)
    return pl.pallas_call(
        middle_kernel,
        out_shape=(
            state,
            state,
            state,
            jax.ShapeDtypeStruct((voxels, C), bf16),
            pltpu.VMEM(w_down.shape, bf16),
        ),
        in_specs=[SMEM] * 3 + [VMEM] * 13 + [HBM],
        out_specs=(VMEM,) * 5,
        scratch_shapes=[
            pltpu.VMEM((2, voxels // 2, 2 * C), bf16),
            pltpu.VMEM((voxels, LANES), i32),
            pltpu.SemaphoreType.DMA((PIECES,)),
        ],
        compiler_params=params(20),
        name="middle",
    )(
        tags, before_tag, after_tag, row(tags), row(before_tag), row(after_tag), before, after, w_heads,
        query, value, total, top, latent, w_out, w_up, *kept(w_down)
    )


def finish_kernel(
    tag_ref, before_tag_ref, after_tag_ref, tag_row_ref, before_row_ref, after_row_ref,
    before_ref, after_ref, heads_ref, query_ref, late_value_ref, late_sum_ref, late_top_ref,
    early_ref, latent_ref, w_out_ref, up_ref, down_ref, out_ref,
    kv_ref, column_ref, value_ref, sum_ref, top_ref, attended_ref, late_latent_ref, late_out_ref
):
    voxels = query_ref.shape[0]
    blocks = voxels // BLOCK
    half = voxels // 2
    head, tail = rims(tag_ref, before_tag_ref, after_tag_ref)
    late = jnp.minimum(head + tail, blocks)
    far_before = jnp.logical_and(head > 0, before_tag_ref[half - 1] == tag_ref[0])
    far_after = jnp.logical_and(tail > 0, after_tag_ref[half] == tag_ref[voxels - 1])

    @pl.when(jnp.logical_or(far_before, far_after))
    def _():
        column_ref[...] = column_of(tag_row_ref[...])

    project(far_before, far_after, before_ref, after_ref, heads_ref, kv_ref)

    old, new = (late_value_ref, late_sum_ref, late_top_ref), (value_ref, sum_ref, top_ref)

    def one_part(part, carry):
        @pl.when(jnp.where(part == 0, far_before, far_after))
        def _():
            rows = pl.ds(pl.multiple_of(part * half, half), half)
            row = jnp.where(part == 0, before_row_ref[:, :half], after_row_ref[:, half:])
            extend(query_ref, rows, kv_ref, part, bias_of(column_ref[rows, :], row), old, new)

        return carry

    lax.fori_loop(0, 2, one_part, 0)

    def one_late(k, carry):
        b, rows, put = late_rows(k, head, late, blocks)
        changed = jnp.where(b < blocks // 2, far_before, far_after)

        @pl.when(changed)
        def _():
            attended_ref[put, :] = (value_ref[rows, :] / sum_ref[rows, :]).astype(bf16)

        @pl.when(jnp.logical_not(changed))
        def _():
            attended_ref[put, :] = (late_value_ref[rows, :] / late_sum_ref[rows, :]).astype(bf16)

        late_latent_ref[put, :] = latent_ref[rows, :]
        return carry

    lax.fori_loop(0, late, one_late, 0)
    out_ref[...] = early_ref[...]

    def settle(rows):
        late_out_ref[rows, :] = feed_forward(
            attended_ref[rows, :], late_latent_ref[rows, :], w_out_ref, up_ref, down_ref
        )

    def one_span(k, carry):
        settle(pl.ds(pl.multiple_of(k * half, half), half))
        return carry

    lax.fori_loop(0, (late + 1) // 2, one_span, 0)

    def put_back(k, carry):
        _, rows, put = late_rows(k, head, late, blocks)
        out_ref[rows, :] = late_out_ref[put, :]
        return carry

    lax.fori_loop(0, late, put_back, 0)


def finish(
    tags, before_tag, after_tag, before, after, w_heads, query, late_value, late_sum, late_top, early, latent,
    w_out, w_up, w_down
):
    voxels = query.shape[0]
    row = lambda t: t.reshape(1, voxels)
    state = pltpu.VMEM((voxels, C), f32)
    return pl.pallas_call(
        finish_kernel,
        out_shape=jax.ShapeDtypeStruct((voxels, C), bf16),
        in_specs=[SMEM] * 3 + [VMEM] * 15,
        out_specs=VMEM,
        scratch_shapes=[
            pltpu.VMEM((2, voxels // 2, 2 * C), bf16),
            pltpu.VMEM((voxels, LANES), i32),
            state,
            state,
            state,
            pltpu.VMEM((voxels, C), bf16),
            state,
            pltpu.VMEM((voxels, C), bf16),
        ],
        compiler_params=params(28),
        name="finish",
    )(
        tags, before_tag, after_tag, row(tags), row(before_tag), row(after_tag), before, after, w_heads,
        query, late_value, late_sum, late_top, early, latent, w_out, w_up, w_down
    )


def local(features, w_embed, owner_device, voxel_slot, window_ids, w_heads, w_out, w_up, w_down):
    devices = lax.axis_size(AXES)
    patches = features.shape[0]
    voxels = window_ids.shape[0]
    capacity = max(2, 2 * patches // devices)
    buffer = dispatch(
        features, w_embed, owner_device.reshape(1, patches), voxel_slot.reshape(1, patches), devices, capacity
    )
    buffer, tags = lax.optimization_barrier((buffer, window_ids))
    arrived = lax.all_to_all(buffer, AXES, split_axis=0, concat_axis=0, tiled=True)
    before_tag = passed_along(tags, 1)
    after_tag = passed_along(tags, -1)
    arrived, before_tag, after_tag = lax.optimization_barrier((arrived, before_tag, after_tag))
    latent, low, high = gather(arrived, voxels)
    before_near = passed_along(high, 1)
    after_near = passed_along(low, -1)
    before_far = passed_along(low, 1)
    after_far = passed_along(high, -1)
    query, value, top, total, up = near(tags, low, high, w_heads, w_up)
    places = (tags, before_tag, after_tag)
    *late, early, down = middle(
        *places, before_near, after_near, w_heads, query, value, total, top, latent, w_out, up, w_down
    )
    return finish(*places, before_far, after_far, w_heads, query, *late, early, latent, w_out, up, down)


def solution(mesh):
    rows = P(AXES, None)
    return jax.shard_map(
        local,
        mesh=mesh,
        in_specs=(rows, P(), rows, P(AXES), P(AXES), P(), P(), P(), P()),
        out_specs=rows,
        check_vma=False,
    )
```

```python
import jax
import jax.numpy as jnp
from jax import lax
from jax.experimental import pallas as pl
from jax.experimental.pallas import tpu as pltpu
from jax.sharding import PartitionSpec as P

C = 768
HEADS = 12
HEAD = C // HEADS
PAIRS = HEADS // 2
LANES = 128
CHUNKS = C // LANES
BLOCK = 128
epsilon = 1e-06
AXES = ("view", "vox")
f32 = jnp.float32
bf16 = jnp.bfloat16
i32 = jnp.int32
MASKED = -1e30


def passed_along(block, distance):
    devices = range(lax.axis_size(AXES))
    route = [(i - distance, i) for i in devices if i - distance in devices]
    return lax.ppermute(block, AXES, route)


def layer_norm(values):
    average = jnp.mean(values, axis=-1, keepdims=True)
    centered = values - average
    variance = jnp.mean(centered * centered, axis=-1, keepdims=True)
    return centered * lax.rsqrt(variance + epsilon)


def across(a, b):
    return lax.dot_general(a, b, (((1,), (1,)), ((), ())), preferred_element_type=f32)


def dot(a, b):
    return jnp.dot(a, b, preferred_element_type=f32)


def iota(shape, dim):
    return lax.broadcasted_iota(i32, shape, dim)


def params(mib):
    return pltpu.CompilerParams(vmem_limit_bytes=mib << 20)


GROUPS = 4


def dispatch_kernel(
    features_hbm, embed_hbm, owner_hbm, slot_hbm, out_hbm,
    features_ref, embed_ref, owner_ref, slot_ref, out_ref, payload_ref, position_ref, digits_ref, in_sem, out_sem
):
    copies = [
        pltpu.make_async_copy(source, target, in_sem.at[k])
        for k, (source, target) in enumerate(
            (
                (owner_hbm, owner_ref),
                (slot_hbm, slot_ref),
                (features_hbm, features_ref),
                (embed_hbm, embed_ref),
            )
        )
    ]
    for copy in copies:
        copy.start()
    patches = features_ref.shape[0]
    devices = digits_ref.shape[1]
    group = devices // GROUPS
    capacity = (out_ref.shape[1] - 8) // CHUNKS
    part = 256
    mine = lax.rem(lax.axis_index("vox"), LANES // capacity)
    earlier = jnp.where(iota((part, part), 0) < iota((part, part), 1), 1.0, 0.0).astype(bf16)
    copies[0].wait()
    copies[1].wait()
    owner = owner_ref[...]
    hits = jnp.where(iota((devices, patches), 0) == owner, 1.0, 0.0)
    running = jnp.zeros((devices, 1), f32)
    ranks = []
    for start in range(0, patches, part):
        here = hits[:, start : start + part]
        before = dot(here.astype(bf16), earlier) + running
        running = running + jnp.sum(here, axis=1, keepdims=True)
        ranks.append(jnp.sum(here * before, axis=0, keepdims=True))
    rank = jnp.concatenate(ranks, axis=1).astype(i32)
    position_ref[...] = owner * capacity + rank
    place = jnp.where(iota((LANES, patches), 0) == rank + capacity * mine, 1.0, 0.0).astype(bf16)
    code = slot_ref[...] + 1
    digits_ref[0] = across((hits * (code >> 4).astype(f32)).astype(bf16), place)
    digits_ref[1] = across((hits * (code & 15).astype(f32)).astype(bf16), place)
    copies[2].wait()
    copies[3].wait()
    payload_ref[...] = dot(features_ref[...], embed_ref[...]).astype(bf16)
    rows = group * capacity
    sends = []
    for g in range(GROUPS):
        here = slice(g * group, (g + 1) * group)
        chosen = jnp.where(iota((rows, patches), 0) + g * rows == position_ref[...], 1.0, 0.0)
        block = dot(chosen.astype(bf16), payload_ref[...]).astype(bf16)
        for c in range(CHUNKS):
            out_ref[here, c * capacity : (c + 1) * capacity, :] = block[
                :, c * LANES : (c + 1) * LANES
            ].reshape(group, capacity, LANES)
        high = jnp.broadcast_to(digits_ref[0, here, :][:, None, :], (group, 8, LANES))
        low = jnp.broadcast_to(digits_ref[1, here, :][:, None, :], (group, 8, LANES))
        out_ref[here, CHUNKS * capacity :, :] = jnp.where(
            iota((group, 8, LANES), 1) < 4, high, low
        ).astype(bf16)
        send = pltpu.make_async_copy(out_ref.at[here], out_hbm.at[here], out_sem.at[g])
        send.start()
        sends.append(send)
    for send in sends:
        send.wait()


def kept(*arrays):
    return [pltpu.with_memory_space_constraint(array, pltpu.HBM) for array in arrays]


HBM = pl.BlockSpec(memory_space=pltpu.HBM)
VMEM = pl.BlockSpec(memory_space=pltpu.VMEM)
SMEM = pl.BlockSpec(memory_space=pltpu.SMEM)


def dispatch(features, w_embed, owner, slot, devices, capacity):
    patches, width = features.shape
    tall = CHUNKS * capacity + 8
    return pl.pallas_call(
        dispatch_kernel,
        out_shape=pltpu.HBM((devices, tall, LANES), bf16),
        in_specs=[HBM] * 4,
        out_specs=HBM,
        scratch_shapes=[
            pltpu.VMEM((patches, width), bf16),
            pltpu.VMEM((width, C), bf16),
            pltpu.VMEM((1, patches), i32),
            pltpu.VMEM((1, patches), i32),
            pltpu.VMEM((devices, tall, LANES), bf16),
            pltpu.VMEM((patches, C), bf16),
            pltpu.VMEM((1, patches), i32),
            pltpu.VMEM((2, devices, LANES), f32),
            pltpu.SemaphoreType.DMA((4,)),
            pltpu.SemaphoreType.DMA((GROUPS,)),
        ],
        compiler_params=params(32),
        name="dispatch",
    )(*kept(features, w_embed, owner, slot))


def gather_kernel(arrived_hbm, latent_ref, low_ref, high_ref, arrived_ref, digit_ref, member_ref, sem):
    sources = arrived_ref.shape[0]
    capacity = arrived_ref.shape[1] // CHUNKS
    tall = CHUNKS * capacity
    voxels = latent_ref.shape[0]
    each = LANES // capacity
    digit_copy = pltpu.make_async_copy(arrived_hbm.at[:, tall:, :], digit_ref, sem.at[0])
    digit_copy.start()
    data_copy = pltpu.make_async_copy(arrived_hbm.at[:, :tall, :], arrived_ref, sem.at[1])
    data_copy.start()
    digit_copy.wait()
    digits = jnp.sum(digit_ref[...].astype(f32).reshape(sources // each, each, 8, LANES), axis=1)
    code = (digits[:, 0, :] * 16.0 + digits[:, 4, :]).astype(i32) - 1
    counted = jnp.zeros((voxels, LANES), f32)
    for g in range(sources // each):
        member = jnp.where(iota((voxels, LANES), 0) == code[g : g + 1], 1.0, 0.0)
        counted = counted + member
        member_ref[:, g * LANES : (g + 1) * LANES] = member.astype(bf16)
    counts = jnp.sum(counted, axis=1, keepdims=True)
    data_copy.wait()
    data = jnp.concatenate(
        [
            arrived_ref[:, c * capacity : (c + 1) * capacity, :].reshape(sources * capacity, LANES)
            for c in range(CHUNKS)
        ],
        axis=1,
    )
    latent = dot(member_ref[...], data) / jnp.maximum(counts, 1.0)
    latent_ref[...] = latent
    normed = layer_norm(latent).astype(bf16)
    low_ref[...] = normed[: voxels // 2]
    high_ref[...] = normed[voxels // 2 :]


def gather(arrived, voxels):
    sources, tall, _ = arrived.shape
    return pl.pallas_call(
        gather_kernel,
        out_shape=(
            jax.ShapeDtypeStruct((voxels, C), f32),
            jax.ShapeDtypeStruct((voxels // 2, C), bf16),
            jax.ShapeDtypeStruct((voxels // 2, C), bf16),
        ),
        in_specs=[HBM],
        out_specs=(VMEM, VMEM, VMEM),
        scratch_shapes=[
            pltpu.VMEM((sources, tall - 8, LANES), bf16),
            pltpu.VMEM((sources, 8, LANES), bf16),
            pltpu.VMEM((voxels, sources * ((tall - 8) // CHUNKS)), bf16),
            pltpu.SemaphoreType.DMA((2,)),
        ],
        compiler_params=params(24),
        name="gather",
    )(arrived)


def column_of(row):
    return jnp.broadcast_to(row, (LANES, row.shape[1])).T


def by_half(both):
    first, second = jnp.split(both, 2, axis=0)
    return jnp.where(iota(first.shape, 1) < HEAD, first, second)


def scores_of(query_pair, key_pair, bias):
    left = iota(query_pair.shape, 1) < HEAD
    none = jnp.zeros_like(query_pair)
    both = jnp.concatenate([jnp.where(left, query_pair, none), jnp.where(left, none, query_pair)], axis=0)
    return across(both, key_pair) + bias


def weighted(score, highest, value_pair):
    exponent = jnp.exp(score - highest).astype(bf16)
    wide = jnp.concatenate([value_pair, jnp.ones_like(value_pair)], axis=1)
    return dot(exponent, wide)


def bias_of(column, row):
    tiles = [
        jnp.where(column == row[:, k : k + LANES], 0.0, MASKED) for k in range(0, row.shape[1], LANES)
    ]
    bias = jnp.concatenate(tiles, axis=1)
    return jnp.concatenate([bias, bias], axis=0)


def rims(tag_ref, before_tag_ref, after_tag_ref):
    voxels = tag_ref.shape[0]
    blocks = voxels // BLOCK
    start_tag, end_tag = tag_ref[0], tag_ref[voxels - 1]
    head = i32(0)
    tail = i32(0)
    for k in range(blocks):
        head += (tag_ref[k * BLOCK] == start_tag).astype(i32)
        tail += (tag_ref[k * BLOCK + BLOCK - 1] == end_tag).astype(i32)
    ring = [lax.axis_index(axis) for axis in AXES]
    ends = [lax.axis_size(axis) - 1 for axis in AXES]
    first = jnp.logical_and(ring[0] == 0, ring[1] == 0)
    final = jnp.logical_and(ring[0] == ends[0], ring[1] == ends[1])
    head = jnp.where(jnp.logical_or(first, before_tag_ref[voxels - 1] != start_tag), 0, head)
    tail = jnp.where(jnp.logical_or(final, after_tag_ref[0] != end_tag), 0, tail)
    return head, tail


def feed_forward(attended, latent, w_out_ref, w_up_ref, w_down_ref):
    middle = latent + dot(attended, w_out_ref[...])
    normed = layer_norm(middle).astype(bf16)
    total = middle
    part = 512
    parts = range(0, w_up_ref.shape[1], part)
    raised = dot(normed, w_up_ref[:, :part])
    for k in parts:
        coming = dot(normed, w_up_ref[:, k + part : k + 2 * part]) if k + part in parts else None
        bent = jax.nn.gelu(raised, approximate=True).astype(bf16)
        total = total + dot(bent, w_down_ref[k : k + part, :])
        raised = coming
    return total.astype(bf16)


PIECES = 4


def fetched(source, target, sem):
    each = source.shape[0] // PIECES
    pieces = [slice(j * each, (j + 1) * each) for j in range(PIECES)]
    copies = [pltpu.make_async_copy(source.at[p], target.at[p], sem.at[j]) for j, p in enumerate(pieces)]
    for copy in copies:
        copy.start()
    return copies


def near_kernel(
    tag_ref, tag_row_ref, low_ref, high_ref, heads_ref, up_hbm,
    query_ref, value_ref, top_ref, sum_ref, up_ref, kv_ref, column_ref, sem
):
    fetches = fetched(up_hbm, up_ref, sem)
    voxels = query_ref.shape[0]
    blocks = voxels // BLOCK
    normed = jnp.concatenate([low_ref[...], high_ref[...]], axis=0)
    query_ref[...] = dot(normed, heads_ref[:, :C]).astype(bf16) * jnp.asarray(HEAD**-0.5, bf16)
    kv_ref[...] = dot(normed, heads_ref[:, C:]).astype(bf16)
    column_ref[...] = column_of(tag_row_ref[...])

    def one_block(b, carry):
        rows = pl.ds(pl.multiple_of(b * BLOCK, BLOCK), BLOCK)
        first, last = tag_ref[b * BLOCK], tag_ref[b * BLOCK + BLOCK - 1]
        low = i32(0)
        high = i32(0)
        for k in range(blocks):
            low = low + (tag_ref[k * BLOCK + BLOCK - 1] < first).astype(i32)
            high = high + (tag_ref[k * BLOCK] <= last).astype(i32)
        short = high - low <= 2
        low = jnp.where(short, jnp.minimum(low, blocks - 2), 0)

        def attend(n):
            keys = pl.ds(pl.multiple_of(low * BLOCK, BLOCK), n * BLOCK)
            bias = bias_of(column_ref[rows, :], tag_row_ref[:, keys])
            for p in range(PAIRS):
                lanes = slice(p * LANES, (p + 1) * LANES)
                score = scores_of(query_ref[rows, lanes], kv_ref[keys, lanes], bias)
                highest = jnp.max(score, axis=1, keepdims=True)
                result = weighted(score, highest, kv_ref[keys, C + p * LANES : C + (p + 1) * LANES])
                value_ref[rows, lanes] = by_half(result[:, :LANES])
                sum_ref[rows, lanes] = by_half(result[:, LANES:])
                top_ref[rows, lanes] = by_half(jnp.broadcast_to(highest, (2 * BLOCK, LANES)))

        pl.when(short)(lambda: attend(2))
        pl.when(jnp.logical_not(short))(lambda: attend(blocks))
        return carry

    lax.fori_loop(0, blocks, one_block, 0)
    for copy in fetches:
        copy.wait()


def near(tags, low, high, w_heads, w_up):
    voxels = tags.shape[0]
    state = jax.ShapeDtypeStruct((voxels, C), f32)
    return pl.pallas_call(
        near_kernel,
        out_shape=(
            jax.ShapeDtypeStruct((voxels, C), bf16),
            state,
            state,
            state,
            pltpu.VMEM(w_up.shape, bf16),
        ),
        in_specs=[SMEM] + [VMEM] * 4 + [HBM],
        out_specs=(VMEM,) * 5,
        scratch_shapes=[
            pltpu.VMEM((voxels, 2 * C), bf16),
            pltpu.VMEM((voxels, LANES), i32),
            pltpu.SemaphoreType.DMA((PIECES,)),
        ],
        compiler_params=params(20),
        name="near",
    )(tags, tags.reshape(1, voxels), low, high, w_heads, *kept(w_up))


def extend(query_ref, rows, kv_ref, side, bias, old, new):
    for p in range(PAIRS):
        lanes = slice(p * LANES, (p + 1) * LANES)
        values = slice(C + p * LANES, C + (p + 1) * LANES)
        score = scores_of(query_ref[rows, lanes], kv_ref[side, :, lanes], bias)
        highest = jnp.max(score, axis=1, keepdims=True)
        result = weighted(score, highest, kv_ref[side, :, values])
        here = by_half(jnp.broadcast_to(highest, result[:, :LANES].shape))
        known = old[2][rows, lanes]
        top = jnp.maximum(known, here)
        fade, grow = jnp.exp(known - top), jnp.exp(here - top)
        new[0][rows, lanes] = old[0][rows, lanes] * fade + by_half(result[:, :LANES]) * grow
        new[1][rows, lanes] = old[1][rows, lanes] * fade + by_half(result[:, LANES:]) * grow
        new[2][rows, lanes] = top


def late_rows(k, head, late, blocks):
    b = jnp.where(k < head, k, k + blocks - late)
    put = pl.ds(pl.multiple_of(k * BLOCK, BLOCK), BLOCK)
    return b, pl.ds(pl.multiple_of(b * BLOCK, BLOCK), BLOCK), put


def project(need_before, need_after, before_ref, after_ref, heads_ref, kv_ref):
    half = before_ref.shape[0]

    @pl.when(jnp.logical_and(need_before, need_after))
    def _():
        both = jnp.concatenate([before_ref[...], after_ref[...]], axis=0)
        kv_ref[...] = dot(both, heads_ref[:, C:]).astype(bf16).reshape(2, half, 2 * C)

    @pl.when(need_before != need_after)
    def _():
        one = jnp.where(need_before, before_ref[...], after_ref[...])
        kv_ref[jnp.where(need_before, 0, 1)] = dot(one, heads_ref[:, C:]).astype(bf16)


def middle_kernel(
    tag_ref, before_tag_ref, after_tag_ref, tag_row_ref, before_row_ref, after_row_ref,
    before_ref, after_ref, heads_ref, query_ref, value_ref, sum_ref, top_ref, latent_ref, w_out_ref, up_ref, down_hbm,
    late_value_ref, late_sum_ref, late_top_ref, out_ref, down_ref, kv_ref, column_ref, sem
):
    fetches = fetched(down_hbm, down_ref, sem)
    voxels = query_ref.shape[0]
    blocks = voxels // BLOCK
    half = voxels // 2
    head, tail = rims(tag_ref, before_tag_ref, after_tag_ref)
    late = jnp.minimum(head + tail, blocks)

    @pl.when(late > 0)
    def _():
        column_ref[...] = column_of(tag_row_ref[...])

    project(head > 0, tail > 0, before_ref, after_ref, heads_ref, kv_ref)

    old, new = (value_ref, sum_ref, top_ref), (late_value_ref, late_sum_ref, late_top_ref)

    def one_step(step, carry):
        part, side = step // 2, step % 2
        rows = pl.ds(pl.multiple_of(part * half, half), half)
        from_before = head > 2 * part
        needed = jnp.where(side == 0, from_before, tail > 2 * (1 - part))
        again = jnp.logical_and(side == 1, from_before)
        row = jnp.where(side == 0, before_row_ref[:, half:], after_row_ref[:, :half])
        bias = lambda: bias_of(column_ref[rows, :], row)

        @pl.when(jnp.logical_and(needed, jnp.logical_not(again)))
        def _():
            extend(query_ref, rows, kv_ref, side, bias(), old, new)

        @pl.when(jnp.logical_and(needed, again))
        def _():
            extend(query_ref, rows, kv_ref, side, bias(), new, new)

        return carry

    lax.fori_loop(0, 4, one_step, 0)
    for copy in fetches:
        copy.wait()
    early = blocks - late

    def settle(rows):
        attended = (value_ref[rows, :] / sum_ref[rows, :]).astype(bf16)
        out_ref[rows, :] = feed_forward(attended, latent_ref[rows, :], w_out_ref, up_ref, down_ref)

    def one_span(k, carry):
        start = jnp.minimum(head + 2 * k, blocks - 2) * BLOCK
        settle(pl.ds(pl.multiple_of(start, BLOCK), half))
        return carry

    lax.fori_loop(0, (early + 1) // 2, one_span, 0)


def middle(tags, before_tag, after_tag, before, after, w_heads, query, value, total, top, latent, w_out, w_up, w_down):
    voxels = query.shape[0]
    row = lambda t: t.reshape(1, voxels)
    state = jax.ShapeDtypeStruct((voxels, C), f32)
    return pl.pallas_call(
        middle_kernel,
        out_shape=(
            state,
            state,
            state,
            jax.ShapeDtypeStruct((voxels, C), bf16),
            pltpu.VMEM(w_down.shape, bf16),
        ),
        in_specs=[SMEM] * 3 + [VMEM] * 13 + [HBM],
        out_specs=(VMEM,) * 5,
        scratch_shapes=[
            pltpu.VMEM((2, voxels // 2, 2 * C), bf16),
            pltpu.VMEM((voxels, LANES), i32),
            pltpu.SemaphoreType.DMA((PIECES,)),
        ],
        compiler_params=params(20),
        name="middle",
    )(
        tags, before_tag, after_tag, row(tags), row(before_tag), row(after_tag), before, after, w_heads,
        query, value, total, top, latent, w_out, w_up, *kept(w_down)
    )


def finish_kernel(
    tag_ref, before_tag_ref, after_tag_ref, tag_row_ref, before_row_ref, after_row_ref,
    before_ref, after_ref, heads_ref, query_ref, late_value_ref, late_sum_ref, late_top_ref,
    early_ref, latent_ref, w_out_ref, up_ref, down_ref, out_ref,
    kv_ref, column_ref, value_ref, sum_ref, top_ref, attended_ref, late_latent_ref, late_out_ref
):
    voxels = query_ref.shape[0]
    blocks = voxels // BLOCK
    half = voxels // 2
    head, tail = rims(tag_ref, before_tag_ref, after_tag_ref)
    late = jnp.minimum(head + tail, blocks)
    far_before = jnp.logical_and(head > 0, before_tag_ref[half - 1] == tag_ref[0])
    far_after = jnp.logical_and(tail > 0, after_tag_ref[half] == tag_ref[voxels - 1])

    @pl.when(jnp.logical_or(far_before, far_after))
    def _():
        column_ref[...] = column_of(tag_row_ref[...])

    project(far_before, far_after, before_ref, after_ref, heads_ref, kv_ref)

    old, new = (late_value_ref, late_sum_ref, late_top_ref), (value_ref, sum_ref, top_ref)

    def one_part(part, carry):
        @pl.when(jnp.where(part == 0, far_before, far_after))
        def _():
            rows = pl.ds(pl.multiple_of(part * half, half), half)
            row = jnp.where(part == 0, before_row_ref[:, :half], after_row_ref[:, half:])
            extend(query_ref, rows, kv_ref, part, bias_of(column_ref[rows, :], row), old, new)

        return carry

    lax.fori_loop(0, 2, one_part, 0)

    def one_late(k, carry):
        b, rows, put = late_rows(k, head, late, blocks)
        changed = jnp.where(b < blocks // 2, far_before, far_after)

        @pl.when(changed)
        def _():
            attended_ref[put, :] = (value_ref[rows, :] / sum_ref[rows, :]).astype(bf16)

        @pl.when(jnp.logical_not(changed))
        def _():
            attended_ref[put, :] = (late_value_ref[rows, :] / late_sum_ref[rows, :]).astype(bf16)

        late_latent_ref[put, :] = latent_ref[rows, :]
        return carry

    lax.fori_loop(0, late, one_late, 0)
    out_ref[...] = early_ref[...]

    def settle(rows):
        late_out_ref[rows, :] = feed_forward(
            attended_ref[rows, :], late_latent_ref[rows, :], w_out_ref, up_ref, down_ref
        )

    @pl.when(jnp.logical_and(late > 0, late <= 2))
    def _():
        settle(slice(0, half))

    @pl.when(late > 2)
    def _():
        settle(slice(0, voxels))

    def put_back(k, carry):
        _, rows, put = late_rows(k, head, late, blocks)
        out_ref[rows, :] = late_out_ref[put, :]
        return carry

    lax.fori_loop(0, late, put_back, 0)


def finish(
    tags, before_tag, after_tag, before, after, w_heads, query, late_value, late_sum, late_top, early, latent,
    w_out, w_up, w_down
):
    voxels = query.shape[0]
    row = lambda t: t.reshape(1, voxels)
    state = pltpu.VMEM((voxels, C), f32)
    return pl.pallas_call(
        finish_kernel,
        out_shape=jax.ShapeDtypeStruct((voxels, C), bf16),
        in_specs=[SMEM] * 3 + [VMEM] * 15,
        out_specs=VMEM,
        scratch_shapes=[
            pltpu.VMEM((2, voxels // 2, 2 * C), bf16),
            pltpu.VMEM((voxels, LANES), i32),
            state,
            state,
            state,
            pltpu.VMEM((voxels, C), bf16),
            state,
            pltpu.VMEM((voxels, C), bf16),
        ],
        compiler_params=params(28),
        name="finish",
    )(
        tags, before_tag, after_tag, row(tags), row(before_tag), row(after_tag), before, after, w_heads,
        query, late_value, late_sum, late_top, early, latent, w_out, w_up, w_down
    )


def local(features, w_embed, owner_device, voxel_slot, window_ids, w_heads, w_out, w_up, w_down):
    devices = lax.axis_size(AXES)
    patches = features.shape[0]
    voxels = window_ids.shape[0]
    capacity = max(2, 2 * patches // devices)
    buffer = dispatch(
        features, w_embed, owner_device.reshape(1, patches), voxel_slot.reshape(1, patches), devices, capacity
    )
    buffer, tags = lax.optimization_barrier((buffer, window_ids))
    arrived = lax.all_to_all(buffer, AXES, split_axis=0, concat_axis=0, tiled=True)
    before_tag = passed_along(tags, 1)
    after_tag = passed_along(tags, -1)
    arrived, before_tag, after_tag = lax.optimization_barrier((arrived, before_tag, after_tag))
    latent, low, high = gather(arrived, voxels)
    before_near = passed_along(high, 1)
    after_near = passed_along(low, -1)
    before_far = passed_along(low, 1)
    after_far = passed_along(high, -1)
    query, value, top, total, up = near(tags, low, high, w_heads, w_up)
    places = (tags, before_tag, after_tag)
    *late, early, down = middle(
        *places, before_near, after_near, w_heads, query, value, total, top, latent, w_out, up, w_down
    )
    return finish(*places, before_far, after_far, w_heads, query, *late, early, latent, w_out, up, down)


def solution(mesh):
    rows = P(AXES, None)
    return jax.shard_map(
        local,
        mesh=mesh,
        in_specs=(rows, P(), rows, P(AXES), P(AXES), P(), P(), P(), P()),
        out_specs=rows,
        check_vma=False,
    )
```

```python
import jax
import jax.numpy as jnp
from jax import lax
from jax.experimental import pallas as pl
from jax.experimental.pallas import tpu as pltpu
from jax.sharding import PartitionSpec as P

C = 768
HEADS = 12
HEAD = C // HEADS
PAIRS = HEADS // 2
LANES = 128
CHUNKS = C // LANES
BLOCK = 128
epsilon = 1e-06
AXES = ("view", "vox")
f32 = jnp.float32
bf16 = jnp.bfloat16
i32 = jnp.int32
MASKED = -1e30


def passed_along(block, distance):
    devices = range(lax.axis_size(AXES))
    route = [(i - distance, i) for i in devices if i - distance in devices]
    return lax.ppermute(block, AXES, route)


def layer_norm(values):
    average = jnp.mean(values, axis=-1, keepdims=True)
    centered = values - average
    variance = jnp.mean(centered * centered, axis=-1, keepdims=True)
    return centered * lax.rsqrt(variance + epsilon)


def across(a, b):
    return lax.dot_general(a, b, (((1,), (1,)), ((), ())), preferred_element_type=f32)


def dot(a, b):
    return jnp.dot(a, b, preferred_element_type=f32)


def iota(shape, dim):
    return lax.broadcasted_iota(i32, shape, dim)


def params(mib):
    return pltpu.CompilerParams(vmem_limit_bytes=mib << 20)


GROUPS = 4


def dispatch_kernel(
    features_hbm, embed_hbm, owner_hbm, slot_hbm, out_hbm,
    features_ref, embed_ref, owner_ref, slot_ref, out_ref, payload_ref, position_ref, digits_ref, in_sem, out_sem
):
    copies = [
        pltpu.make_async_copy(source, target, in_sem.at[k])
        for k, (source, target) in enumerate(
            (
                (owner_hbm, owner_ref),
                (slot_hbm, slot_ref),
                (features_hbm, features_ref),
                (embed_hbm, embed_ref),
            )
        )
    ]
    for copy in copies:
        copy.start()
    patches = features_ref.shape[0]
    devices = digits_ref.shape[1]
    group = devices // GROUPS
    capacity = (out_ref.shape[1] - 8) // CHUNKS
    part = 256
    mine = lax.rem(lax.axis_index("vox"), LANES // capacity)
    earlier = jnp.where(iota((part, part), 0) < iota((part, part), 1), 1.0, 0.0).astype(bf16)
    copies[0].wait()
    copies[1].wait()
    owner = owner_ref[...]
    hits = jnp.where(iota((devices, patches), 0) == owner, 1.0, 0.0)
    running = jnp.zeros((devices, 1), f32)
    ranks = []
    for start in range(0, patches, part):
        here = hits[:, start : start + part]
        before = dot(here.astype(bf16), earlier) + running
        running = running + jnp.sum(here, axis=1, keepdims=True)
        ranks.append(jnp.sum(here * before, axis=0, keepdims=True))
    rank = jnp.concatenate(ranks, axis=1).astype(i32)
    position_ref[...] = owner * capacity + rank
    place = jnp.where(iota((LANES, patches), 0) == rank + capacity * mine, 1.0, 0.0).astype(bf16)
    code = slot_ref[...] + 1
    digits_ref[0] = across((hits * (code >> 4).astype(f32)).astype(bf16), place)
    digits_ref[1] = across((hits * (code & 15).astype(f32)).astype(bf16), place)
    copies[2].wait()
    copies[3].wait()
    payload_ref[...] = dot(features_ref[...], embed_ref[...]).astype(bf16)
    rows = group * capacity
    sends = []
    for g in range(GROUPS):
        here = slice(g * group, (g + 1) * group)
        chosen = jnp.where(iota((rows, patches), 0) + g * rows == position_ref[...], 1.0, 0.0)
        block = dot(chosen.astype(bf16), payload_ref[...]).astype(bf16)
        for c in range(CHUNKS):
            out_ref[here, c * capacity : (c + 1) * capacity, :] = block[
                :, c * LANES : (c + 1) * LANES
            ].reshape(group, capacity, LANES)
        high = jnp.broadcast_to(digits_ref[0, here, :][:, None, :], (group, 8, LANES))
        low = jnp.broadcast_to(digits_ref[1, here, :][:, None, :], (group, 8, LANES))
        out_ref[here, CHUNKS * capacity :, :] = jnp.where(
            iota((group, 8, LANES), 1) < 4, high, low
        ).astype(bf16)
        send = pltpu.make_async_copy(out_ref.at[here], out_hbm.at[here], out_sem.at[g])
        send.start()
        sends.append(send)
    for send in sends:
        send.wait()


def kept(*arrays):
    return [pltpu.with_memory_space_constraint(array, pltpu.HBM) for array in arrays]


HBM = pl.BlockSpec(memory_space=pltpu.HBM)
VMEM = pl.BlockSpec(memory_space=pltpu.VMEM)
SMEM = pl.BlockSpec(memory_space=pltpu.SMEM)


def dispatch(features, w_embed, owner, slot, devices, capacity):
    patches, width = features.shape
    tall = CHUNKS * capacity + 8
    return pl.pallas_call(
        dispatch_kernel,
        out_shape=pltpu.HBM((devices, tall, LANES), bf16),
        in_specs=[HBM] * 4,
        out_specs=HBM,
        scratch_shapes=[
            pltpu.VMEM((patches, width), bf16),
            pltpu.VMEM((width, C), bf16),
            pltpu.VMEM((1, patches), i32),
            pltpu.VMEM((1, patches), i32),
            pltpu.VMEM((devices, tall, LANES), bf16),
            pltpu.VMEM((patches, C), bf16),
            pltpu.VMEM((1, patches), i32),
            pltpu.VMEM((2, devices, LANES), f32),
            pltpu.SemaphoreType.DMA((4,)),
            pltpu.SemaphoreType.DMA((GROUPS,)),
        ],
        compiler_params=params(32),
        name="dispatch",
    )(*kept(features, w_embed, owner, slot))


def gather_kernel(arrived_hbm, latent_ref, low_ref, high_ref, arrived_ref, digit_ref, member_ref, sem):
    sources = arrived_ref.shape[0]
    capacity = arrived_ref.shape[1] // CHUNKS
    tall = CHUNKS * capacity
    voxels = latent_ref.shape[0]
    each = LANES // capacity
    digit_copy = pltpu.make_async_copy(arrived_hbm.at[:, tall:, :], digit_ref, sem.at[0])
    digit_copy.start()
    data_copy = pltpu.make_async_copy(arrived_hbm.at[:, :tall, :], arrived_ref, sem.at[1])
    data_copy.start()
    digit_copy.wait()
    digits = jnp.sum(digit_ref[...].astype(f32).reshape(sources // each, each, 8, LANES), axis=1)
    code = (digits[:, 0, :] * 16.0 + digits[:, 4, :]).astype(i32) - 1
    counted = jnp.zeros((voxels, LANES), f32)
    for g in range(sources // each):
        member = jnp.where(iota((voxels, LANES), 0) == code[g : g + 1], 1.0, 0.0)
        counted = counted + member
        member_ref[:, g * LANES : (g + 1) * LANES] = member.astype(bf16)
    counts = jnp.sum(counted, axis=1, keepdims=True)
    data_copy.wait()
    data = jnp.concatenate(
        [
            arrived_ref[:, c * capacity : (c + 1) * capacity, :].reshape(sources * capacity, LANES)
            for c in range(CHUNKS)
        ],
        axis=1,
    )
    latent = dot(member_ref[...], data) / jnp.maximum(counts, 1.0)
    latent_ref[...] = latent
    normed = layer_norm(latent).astype(bf16)
    low_ref[...] = normed[: voxels // 2]
    high_ref[...] = normed[voxels // 2 :]


def gather(arrived, voxels):
    sources, tall, _ = arrived.shape
    return pl.pallas_call(
        gather_kernel,
        out_shape=(
            jax.ShapeDtypeStruct((voxels, C), f32),
            jax.ShapeDtypeStruct((voxels // 2, C), bf16),
            jax.ShapeDtypeStruct((voxels // 2, C), bf16),
        ),
        in_specs=[HBM],
        out_specs=(VMEM, VMEM, VMEM),
        scratch_shapes=[
            pltpu.VMEM((sources, tall - 8, LANES), bf16),
            pltpu.VMEM((sources, 8, LANES), bf16),
            pltpu.VMEM((voxels, sources * ((tall - 8) // CHUNKS)), bf16),
            pltpu.SemaphoreType.DMA((2,)),
        ],
        compiler_params=params(24),
        name="gather",
    )(arrived)


def column_of(row):
    return jnp.broadcast_to(row, (LANES, row.shape[1])).T


def by_half(both):
    first, second = jnp.split(both, 2, axis=0)
    return jnp.where(iota(first.shape, 1) < HEAD, first, second)


def scores_of(query_pair, key_pair, bias):
    left = iota(query_pair.shape, 1) < HEAD
    none = jnp.zeros_like(query_pair)
    both = jnp.concatenate([jnp.where(left, query_pair, none), jnp.where(left, none, query_pair)], axis=0)
    return across(both, key_pair) + bias


def weighted(score, highest, value_pair):
    exponent = jnp.exp(score - highest).astype(bf16)
    wide = jnp.concatenate([value_pair, jnp.ones_like(value_pair)], axis=1)
    return dot(exponent, wide)


def bias_of(column, row):
    tiles = [
        jnp.where(column == row[:, k : k + LANES], 0.0, MASKED) for k in range(0, row.shape[1], LANES)
    ]
    bias = jnp.concatenate(tiles, axis=1)
    return jnp.concatenate([bias, bias], axis=0)


def rims(tag_ref, before_tag_ref, after_tag_ref):
    voxels = tag_ref.shape[0]
    blocks = voxels // BLOCK
    start_tag, end_tag = tag_ref[0], tag_ref[voxels - 1]
    head = i32(0)
    tail = i32(0)
    for k in range(blocks):
        head += (tag_ref[k * BLOCK] == start_tag).astype(i32)
        tail += (tag_ref[k * BLOCK + BLOCK - 1] == end_tag).astype(i32)
    ring = [lax.axis_index(axis) for axis in AXES]
    ends = [lax.axis_size(axis) - 1 for axis in AXES]
    first = jnp.logical_and(ring[0] == 0, ring[1] == 0)
    final = jnp.logical_and(ring[0] == ends[0], ring[1] == ends[1])
    head = jnp.where(jnp.logical_or(first, before_tag_ref[voxels - 1] != start_tag), 0, head)
    tail = jnp.where(jnp.logical_or(final, after_tag_ref[0] != end_tag), 0, tail)
    return head, tail


def feed_forward(attended, latent, w_out_ref, w_up_ref, w_down_ref):
    middle = latent + dot(attended, w_out_ref[...])
    normed = layer_norm(middle).astype(bf16)
    total = middle
    part = 512
    parts = range(0, w_up_ref.shape[1], part)
    raised = dot(normed, w_up_ref[:, :part])
    for k in parts:
        coming = dot(normed, w_up_ref[:, k + part : k + 2 * part]) if k + part in parts else None
        bent = jax.nn.gelu(raised, approximate=True).astype(bf16)
        total = total + dot(bent, w_down_ref[k : k + part, :])
        raised = coming
    return total.astype(bf16)


PIECES = 4


def fetched(source, target, sem):
    each = source.shape[0] // PIECES
    pieces = [slice(j * each, (j + 1) * each) for j in range(PIECES)]
    copies = [pltpu.make_async_copy(source.at[p], target.at[p], sem.at[j]) for j, p in enumerate(pieces)]
    for copy in copies:
        copy.start()
    return copies


def near_kernel(
    tag_ref, tag_row_ref, low_ref, high_ref, heads_ref, up_hbm,
    query_ref, value_ref, top_ref, sum_ref, up_ref, kv_ref, column_ref, sem
):
    fetches = fetched(up_hbm, up_ref, sem)
    voxels = query_ref.shape[0]
    blocks = voxels // BLOCK
    normed = jnp.concatenate([low_ref[...], high_ref[...]], axis=0)
    query_ref[...] = dot(normed, heads_ref[:, :C]).astype(bf16) * jnp.asarray(HEAD**-0.5, bf16)
    kv_ref[...] = dot(normed, heads_ref[:, C:]).astype(bf16)
    column_ref[...] = column_of(tag_row_ref[...])

    def one_block(b, carry):
        rows = pl.ds(pl.multiple_of(b * BLOCK, BLOCK), BLOCK)
        first, last = tag_ref[b * BLOCK], tag_ref[b * BLOCK + BLOCK - 1]
        low = i32(0)
        high = i32(0)
        for k in range(blocks):
            low = low + (tag_ref[k * BLOCK + BLOCK - 1] < first).astype(i32)
            high = high + (tag_ref[k * BLOCK] <= last).astype(i32)
        short = high - low <= 2
        low = jnp.where(short, jnp.minimum(low, blocks - 2), 0)

        def attend(n):
            keys = pl.ds(pl.multiple_of(low * BLOCK, BLOCK), n * BLOCK)
            bias = bias_of(column_ref[rows, :], tag_row_ref[:, keys])
            for p in range(PAIRS):
                lanes = slice(p * LANES, (p + 1) * LANES)
                score = scores_of(query_ref[rows, lanes], kv_ref[keys, lanes], bias)
                highest = jnp.max(score, axis=1, keepdims=True)
                result = weighted(score, highest, kv_ref[keys, C + p * LANES : C + (p + 1) * LANES])
                value_ref[rows, lanes] = by_half(result[:, :LANES])
                sum_ref[rows, lanes] = by_half(result[:, LANES:])
                top_ref[rows, lanes] = by_half(jnp.broadcast_to(highest, (2 * BLOCK, LANES)))

        pl.when(short)(lambda: attend(2))
        pl.when(jnp.logical_not(short))(lambda: attend(blocks))
        return carry

    lax.fori_loop(0, blocks, one_block, 0)
    for copy in fetches:
        copy.wait()


def near(tags, low, high, w_heads, w_up):
    voxels = tags.shape[0]
    state = jax.ShapeDtypeStruct((voxels, C), f32)
    return pl.pallas_call(
        near_kernel,
        out_shape=(
            jax.ShapeDtypeStruct((voxels, C), bf16),
            state,
            state,
            state,
            pltpu.VMEM(w_up.shape, bf16),
        ),
        in_specs=[SMEM] + [VMEM] * 4 + [HBM],
        out_specs=(VMEM,) * 5,
        scratch_shapes=[
            pltpu.VMEM((voxels, 2 * C), bf16),
            pltpu.VMEM((voxels, LANES), i32),
            pltpu.SemaphoreType.DMA((PIECES,)),
        ],
        compiler_params=params(20),
        name="near",
    )(tags, tags.reshape(1, voxels), low, high, w_heads, *kept(w_up))


def extend(query_ref, rows, kv_ref, side, bias, old, new):
    for p in range(PAIRS):
        lanes = slice(p * LANES, (p + 1) * LANES)
        values = slice(C + p * LANES, C + (p + 1) * LANES)
        score = scores_of(query_ref[rows, lanes], kv_ref[side, :, lanes], bias)
        highest = jnp.max(score, axis=1, keepdims=True)
        result = weighted(score, highest, kv_ref[side, :, values])
        here = by_half(jnp.broadcast_to(highest, result[:, :LANES].shape))
        known = old[2][rows, lanes]
        top = jnp.maximum(known, here)
        fade, grow = jnp.exp(known - top), jnp.exp(here - top)
        new[0][rows, lanes] = old[0][rows, lanes] * fade + by_half(result[:, :LANES]) * grow
        new[1][rows, lanes] = old[1][rows, lanes] * fade + by_half(result[:, LANES:]) * grow
        new[2][rows, lanes] = top


def late_rows(k, head, late, blocks):
    b = jnp.where(k < head, k, k + blocks - late)
    put = pl.ds(pl.multiple_of(k * BLOCK, BLOCK), BLOCK)
    return b, pl.ds(pl.multiple_of(b * BLOCK, BLOCK), BLOCK), put


def project(need_before, need_after, before_ref, after_ref, heads_ref, kv_ref):
    half = before_ref.shape[0]

    @pl.when(jnp.logical_and(need_before, need_after))
    def _():
        both = jnp.concatenate([before_ref[...], after_ref[...]], axis=0)
        kv_ref[...] = dot(both, heads_ref[:, C:]).astype(bf16).reshape(2, half, 2 * C)

    @pl.when(need_before != need_after)
    def _():
        one = jnp.where(need_before, before_ref[...], after_ref[...])
        kv_ref[jnp.where(need_before, 0, 1)] = dot(one, heads_ref[:, C:]).astype(bf16)


def middle_kernel(
    tag_ref, before_tag_ref, after_tag_ref, tag_row_ref, before_row_ref, after_row_ref,
    before_ref, after_ref, heads_ref, query_ref, value_ref, sum_ref, top_ref, latent_ref, w_out_ref, up_ref, down_hbm,
    late_value_ref, late_sum_ref, late_top_ref, out_ref, down_ref, kv_ref, column_ref, sem
):
    fetches = fetched(down_hbm, down_ref, sem)
    voxels = query_ref.shape[0]
    blocks = voxels // BLOCK
    half = voxels // 2
    head, tail = rims(tag_ref, before_tag_ref, after_tag_ref)
    late = jnp.minimum(head + tail, blocks)

    @pl.when(late > 0)
    def _():
        column_ref[...] = column_of(tag_row_ref[...])

    project(head > 0, tail > 0, before_ref, after_ref, heads_ref, kv_ref)

    old, new = (value_ref, sum_ref, top_ref), (late_value_ref, late_sum_ref, late_top_ref)

    def one_step(step, carry):
        part, side = step // 2, step % 2
        rows = pl.ds(pl.multiple_of(part * half, half), half)
        from_before = head > 2 * part
        needed = jnp.where(side == 0, from_before, tail > 2 * (1 - part))
        again = jnp.logical_and(side == 1, from_before)
        row = jnp.where(side == 0, before_row_ref[:, half:], after_row_ref[:, :half])
        bias = lambda: bias_of(column_ref[rows, :], row)

        @pl.when(jnp.logical_and(needed, jnp.logical_not(again)))
        def _():
            extend(query_ref, rows, kv_ref, side, bias(), old, new)

        @pl.when(jnp.logical_and(needed, again))
        def _():
            extend(query_ref, rows, kv_ref, side, bias(), new, new)

        return carry

    lax.fori_loop(0, 4, one_step, 0)
    for copy in fetches:
        copy.wait()
    early = blocks - late

    def settle(rows):
        attended = (value_ref[rows, :] / sum_ref[rows, :]).astype(bf16)
        out_ref[rows, :] = feed_forward(attended, latent_ref[rows, :], w_out_ref, up_ref, down_ref)

    def one_span(k, carry):
        start = jnp.minimum(head + 2 * k, blocks - 2) * BLOCK
        settle(pl.ds(pl.multiple_of(start, BLOCK), half))
        return carry

    lax.fori_loop(0, (early + 1) // 2, one_span, 0)


def middle(tags, before_tag, after_tag, before, after, w_heads, query, value, total, top, latent, w_out, w_up, w_down):
    voxels = query.shape[0]
    row = lambda t: t.reshape(1, voxels)
    state = jax.ShapeDtypeStruct((voxels, C), f32)
    return pl.pallas_call(
        middle_kernel,
        out_shape=(
            state,
            state,
            state,
            jax.ShapeDtypeStruct((voxels, C), bf16),
            pltpu.VMEM(w_down.shape, bf16),
        ),
        in_specs=[SMEM] * 3 + [VMEM] * 13 + [HBM],
        out_specs=(VMEM,) * 5,
        scratch_shapes=[
            pltpu.VMEM((2, voxels // 2, 2 * C), bf16),
            pltpu.VMEM((voxels, LANES), i32),
            pltpu.SemaphoreType.DMA((PIECES,)),
        ],
        compiler_params=params(20),
        name="middle",
    )(
        tags, before_tag, after_tag, row(tags), row(before_tag), row(after_tag), before, after, w_heads,
        query, value, total, top, latent, w_out, w_up, *kept(w_down)
    )


def finish_kernel(
    tag_ref, before_tag_ref, after_tag_ref, tag_row_ref, before_row_ref, after_row_ref,
    before_ref, after_ref, heads_ref, query_ref, late_value_ref, late_sum_ref, late_top_ref,
    early_ref, latent_ref, w_out_ref, up_ref, down_ref, out_ref,
    kv_ref, column_ref, value_ref, sum_ref, top_ref, attended_ref, late_latent_ref, late_out_ref
):
    voxels = query_ref.shape[0]
    blocks = voxels // BLOCK
    half = voxels // 2
    head, tail = rims(tag_ref, before_tag_ref, after_tag_ref)
    late = jnp.minimum(head + tail, blocks)
    far_before = jnp.logical_and(head > 0, before_tag_ref[half - 1] == tag_ref[0])
    far_after = jnp.logical_and(tail > 0, after_tag_ref[half] == tag_ref[voxels - 1])

    @pl.when(jnp.logical_or(far_before, far_after))
    def _():
        column_ref[...] = column_of(tag_row_ref[...])

    project(far_before, far_after, before_ref, after_ref, heads_ref, kv_ref)

    old, new = (late_value_ref, late_sum_ref, late_top_ref), (value_ref, sum_ref, top_ref)

    def one_part(part, carry):
        @pl.when(jnp.where(part == 0, far_before, far_after))
        def _():
            rows = pl.ds(pl.multiple_of(part * half, half), half)
            row = jnp.where(part == 0, before_row_ref[:, :half], after_row_ref[:, half:])
            extend(query_ref, rows, kv_ref, part, bias_of(column_ref[rows, :], row), old, new)

        return carry

    lax.fori_loop(0, 2, one_part, 0)

    def one_late(k, carry):
        b, rows, put = late_rows(k, head, late, blocks)
        changed = jnp.where(b < blocks // 2, far_before, far_after)

        @pl.when(changed)
        def _():
            attended_ref[put, :] = (value_ref[rows, :] / sum_ref[rows, :]).astype(bf16)

        @pl.when(jnp.logical_not(changed))
        def _():
            attended_ref[put, :] = (late_value_ref[rows, :] / late_sum_ref[rows, :]).astype(bf16)

        late_latent_ref[put, :] = latent_ref[rows, :]
        return carry

    lax.fori_loop(0, late, one_late, 0)
    out_ref[...] = early_ref[...]

    def settle(rows):
        late_out_ref[rows, :] = feed_forward(
            attended_ref[rows, :], late_latent_ref[rows, :], w_out_ref, up_ref, down_ref
        )

    @pl.when(jnp.logical_and(late > 0, late <= 2))
    def _():
        settle(slice(0, half))

    @pl.when(late > 2)
    def _():
        settle(slice(0, voxels))

    def put_back(k, carry):
        _, rows, put = late_rows(k, head, late, blocks)
        out_ref[rows, :] = late_out_ref[put, :]
        return carry

    lax.fori_loop(0, late, put_back, 0)


def finish(
    tags, before_tag, after_tag, before, after, w_heads, query, late_value, late_sum, late_top, early, latent,
    w_out, w_up, w_down
):
    voxels = query.shape[0]
    row = lambda t: t.reshape(1, voxels)
    state = pltpu.VMEM((voxels, C), f32)
    return pl.pallas_call(
        finish_kernel,
        out_shape=jax.ShapeDtypeStruct((voxels, C), bf16),
        in_specs=[SMEM] * 3 + [VMEM] * 15,
        out_specs=VMEM,
        scratch_shapes=[
            pltpu.VMEM((2, voxels // 2, 2 * C), bf16),
            pltpu.VMEM((voxels, LANES), i32),
            state,
            state,
            state,
            pltpu.VMEM((voxels, C), bf16),
            state,
            pltpu.VMEM((voxels, C), bf16),
        ],
        compiler_params=params(28),
        name="finish",
    )(
        tags, before_tag, after_tag, row(tags), row(before_tag), row(after_tag), before, after, w_heads,
        query, late_value, late_sum, late_top, early, latent, w_out, w_up, w_down
    )


def local(features, w_embed, owner_device, voxel_slot, window_ids, w_heads, w_out, w_up, w_down):
    devices = lax.axis_size(AXES)
    patches = features.shape[0]
    voxels = window_ids.shape[0]
    capacity = max(2, 2 * patches // devices)
    buffer = dispatch(
        features, w_embed, owner_device.reshape(1, patches), voxel_slot.reshape(1, patches), devices, capacity
    )
    buffer, tags = lax.optimization_barrier((buffer, window_ids))
    arrived = lax.all_to_all(buffer, AXES, split_axis=0, concat_axis=0, tiled=True)
    before_tag = passed_along(tags, 1)
    after_tag = passed_along(tags, -1)
    arrived, before_tag, after_tag = lax.optimization_barrier((arrived, before_tag, after_tag))
    latent, low, high = gather(arrived, voxels)
    before_near = passed_along(high, 1)
    after_near = passed_along(low, -1)
    query, value, top, total, up = near(tags, low, high, w_heads, w_up)
    low, high, query = lax.optimization_barrier((low, high, query))
    before_far = passed_along(low, 1)
    after_far = passed_along(high, -1)
    places = (tags, before_tag, after_tag)
    *late, early, down = middle(
        *places, before_near, after_near, w_heads, query, value, total, top, latent, w_out, up, w_down
    )
    return finish(*places, before_far, after_far, w_heads, query, *late, early, latent, w_out, up, down)


def solution(mesh):
    rows = P(AXES, None)
    return jax.shard_map(
        local,
        mesh=mesh,
        in_specs=(rows, P(), rows, P(AXES), P(AXES), P(), P(), P(), P()),
        out_specs=rows,
        check_vma=False,
    )
```
